32 devices in a mesh: wide: 8 (over y, x, core), narrow: 4 (over z).
Axes of the slice: x: 2, y: 2, z: 4, core: 2. Of those that a mesh axis runs over, the one named last changes fastest.
Arguments:
- short_input: bfloat16 [32, 16, 32, 768], P(('wide', 'narrow')), may hold values from -6 to 6
- long_input: bfloat16 [32, 4, 128, 768], P(('wide', 'narrow')), may hold values from -6 to 6
- short_cotangent: bfloat16 [32, 16, 32, 768], P(('wide', 'narrow')), may hold values from -6 to 6
- long_cotangent: bfloat16 [32, 4, 128, 768], P(('wide', 'narrow')), may hold values from -6 to 6
- short_live: int32 [8], replicated, may hold values from 1 to 16, as said below
- long_live: int32 [8], replicated, may hold values from 1 to 4, as said below
- position_table: bfloat16 [512, 768], replicated, may hold values from -3 to 3
- embed_gain: bfloat16 [768], replicated, may hold values from 0.5 to 1.5
- embed_shift: bfloat16 [768], replicated, may hold values from -1.5 to 1.5
- project_in: bfloat16 [768, 2304], replicated, may hold values from -0.3125 to 0.3125
- query_bias: bfloat16 [768], replicated, may hold values from -1.5 to 1.5
- value_bias: bfloat16 [768], replicated, may hold values from -1.5 to 1.5
- project_out: bfloat16 [768, 768], replicated, may hold values from -0.875 to 0.875
- output_bias: bfloat16 [768], replicated, may hold values from -1.5 to 1.5
- middle_gain: bfloat16 [768], replicated, may hold values from 0.5 to 1.5
- middle_shift: bfloat16 [768], replicated, may hold values from -1.5 to 1.5
- expand_weight: bfloat16 [768, 3072], replicated, may hold values from -0.21875 to 0.21875
- expand_bias: bfloat16 [3072], replicated, may hold values from -1.5 to 1.5
- shrink_weight: bfloat16 [3072, 768], replicated, may hold values from -0.109375 to 0.109375
- shrink_bias: bfloat16 [768], replicated, may hold values from -1.5 to 1.5
- final_gain: bfloat16 [768], replicated, may hold values from 0.5 to 1.5
- final_shift: bfloat16 [768], replicated, may hold values from -1.5 to 1.5
Outputs:
- short_output: bfloat16 [32, 16, 32, 768], P(('wide', 'narrow'))
- long_output: bfloat16 [32, 4, 128, 768], P(('wide', 'narrow'))
- short_input_grad: bfloat16 [32, 16, 32, 768], P(('wide', 'narrow'))
- long_input_grad: bfloat16 [32, 4, 128, 768], P(('wide', 'narrow'))
- position_grad: float32 [512, 768], P(None, ('wide', 'narrow'))
- embed_gain_grad: float32 [768], P(('wide', 'narrow'))
- embed_shift_grad: float32 [768], P(('wide', 'narrow'))
- project_in_grad: float32 [768, 2304], P(('wide', 'narrow'))
- query_bias_grad: float32 [768], P(('wide', 'narrow'))
- value_bias_grad: float32 [768], P(('wide', 'narrow'))
- project_out_grad: float32 [768, 768], P(('wide', 'narrow'))
- output_bias_grad: float32 [768], P(('wide', 'narrow'))
- middle_gain_grad: float32 [768], P(('wide', 'narrow'))
- middle_shift_grad: float32 [768], P(('wide', 'narrow'))
- expand_weight_grad: float32 [768, 3072], P(('wide', 'narrow'))
- expand_bias_grad: float32 [3072], P(('wide', 'narrow'))
- shrink_weight_grad: float32 [3072, 768], P(('wide', 'narrow'))
- shrink_bias_grad: float32 [768], P(('wide', 'narrow'))
- final_gain_grad: float32 [768], P(('wide', 'narrow'))
- final_shift_grad: float32 [768], P(('wide', 'narrow'))
The draws below stay inside these ranges and needn't reach their ends.
Inputs may be any that keep to these rules, and one draw needn't show every extreme that they name: `short_live`: entry (w // 4) * 4 + n counts the live short rows, rows 0 to that count - 1, of the group of wide index w and narrow index n; some group has all 16 live. `long_live`: likewise for the long rows; some group has all 4 live.
All inputs are finite; a program needn't handle non-finite values.
Results may differ from the reference program's by a relative error of at most 0.015.
Values may be sent and summed in bfloat16 or wider, within the bound.
No kernel may reach another device: no remote copies, remote signals or barrier semaphores. Data moves between devices by JAX's collectives and lax.ppermute only.
A program may use at most 256 MiB of HBM per device.

```python
import jax
import jax.numpy as jnp
from jax import lax

D = 768
HEADS = 12
HEAD_DIM = 64
FF = 3072
LONG_LEN = 512
SHORT_LEN = 128
SHORT_ROWS = 16
LONG_ROWS = 4
GROUPS = 8
SLOTS = 32
N_WIDE = 8
N_NARROW = 4


def live_counts(key, most):
    counts = jax.random.randint(key, (GROUPS,), 1, most + 1)
    chosen = jax.random.randint(jax.random.fold_in(key, 7), (), 0, GROUPS)
    return jnp.where(jnp.arange(GROUPS) == chosen, most, counts).astype(jnp.int32)


def draw_short_live(key, part):
    return live_counts(jax.random.fold_in(key, 11), SHORT_ROWS)


def draw_long_live(key, part):
    return live_counts(jax.random.fold_in(key, 23), LONG_ROWS)


def raised(values, rng, source, target, parts, factor):
    owner, partner = [(jnp.arange(values.shape[axis_at]) // (values.shape[axis_at] // parts)).reshape([-1 if axis == axis_at else 1 for axis in range(values.ndim)]) for axis_at in (source, target)]
    chosen = jax.random.permutation(rng, parts)[partner]
    strong = (owner == chosen) | (owner == (partner + parts // 2) % parts)
    return jnp.where(strong, factor * values, values)


def shard_levels(stream_key, extent, shards, least, largest):
    factor_of = 1.0
    for position, parts in shards:
        draws = jax.random.uniform(jax.random.fold_in(jax.random.fold_in(stream_key, 6), position), (parts,), jnp.float32, least / len(shards), largest / len(shards))
        factor_of = factor_of * jnp.repeat(jnp.exp(draws), extent[position] // parts).reshape((-1,) + (1,) * (len(extent) - 1 - position))
    return factor_of


def noise(stream_key, dims, deviation, bound, shards=(), kind=jnp.bfloat16):
    values = jax.random.normal(stream_key, dims, jnp.float32) * deviation
    if len(shards) > 0:
        values = shard_levels(stream_key, dims, shards, -0.22, 0.18) * values
    return jnp.clip(values, min=-bound, max=bound).astype(kind)


def gaussian_with(stream_key, shape, scale, reach, split, heavy, kind=jnp.bfloat16):
    values = scale * jax.random.normal(stream_key, shape, jnp.float32)
    if split:
        values = values * shard_levels(stream_key, shape, split, -0.22, 0.18)
    return jnp.clip(raised(values, jax.random.fold_in(stream_key, 3), *heavy), -reach, reach).astype(kind)


def setup_inputs(seed: int = 0) -> dict:
    keys = jax.random.split(jax.random.key(seed), 23)
    return {
        "short_input": noise(keys[0], (SLOTS, SHORT_ROWS, SHORT_LEN // 4, D), 1.0, 6.0, ((0, 32),)),
        "long_input": noise(keys[1], (SLOTS, LONG_ROWS, LONG_LEN // 4, D), 1.0, 6.0, ((0, 32),)),
        "short_cotangent": gaussian_with(keys[2], (SLOTS, SHORT_ROWS, SHORT_LEN // 4, D), 1.0, 6.0, ((0, 32),), (0, 3, 32, 2.75)),
        "long_cotangent": gaussian_with(keys[3], (SLOTS, LONG_ROWS, LONG_LEN // 4, D), 1.0, 6.0, ((0, 32),), (0, 3, 32, 2.75)),
        "short_live": draw_short_live(jax.random.fold_in(keys[22], 71), 0),
        "long_live": draw_long_live(jax.random.fold_in(keys[22], 71), 0),
        "position_table": noise(keys[6], (LONG_LEN, D), 0.5, 3.0),
        "embed_gain": jnp.clip(1.0 + 0.1 * jax.random.normal(keys[7], (D,), jnp.float32), 0.5, 1.5).astype(jnp.bfloat16),
        "embed_shift": noise(keys[8], (D,), 0.3, 1.5),
        "project_in": noise(keys[9], (D, 3 * D), (D // 2) ** -0.5, 0.3125),
        "query_bias": noise(keys[10], (D,), 0.3, 1.5),
        "value_bias": noise(keys[11], (D,), 0.3, 1.5),
        "project_out": noise(keys[12], (D, D), (D // 16) ** -0.5, 0.875),
        "output_bias": noise(keys[13], (D,), 0.3, 1.5),
        "middle_gain": jnp.clip(1.0 + 0.1 * jax.random.normal(keys[14], (D,), jnp.float32), 0.5, 1.5).astype(jnp.bfloat16),
        "middle_shift": noise(keys[15], (D,), 0.3, 1.5),
        "expand_weight": noise(keys[16], (D, FF), D ** -0.5, 0.21875),
        "expand_bias": noise(keys[17], (FF,), 0.3, 1.5),
        "shrink_weight": noise(keys[18], (FF, D), FF ** -0.5, 0.109375),
        "shrink_bias": noise(keys[19], (D,), 0.3, 1.5),
        "final_gain": jnp.clip(1.0 + 0.1 * jax.random.normal(keys[20], (D,), jnp.float32), 0.5, 1.5).astype(jnp.bfloat16),
        "final_shift": noise(keys[21], (D,), 0.3, 1.5),
    }


EPS = 1e-05
HIGH = lax.Precision.HIGHEST

@jax.custom_vjp
def low(v):
    return lax.optimization_barrier(v.astype(jnp.bfloat16)).astype(jnp.float32)

@jax.custom_vjp
def low_back(v):
    return v

def low_keep(v):
    return (low(v), None)

def low_pass(kept, grad):
    return (grad,)

def back_keep(v):
    return (v, None)

def back_low(kept, grad):
    return (low(grad),)
low.defvjp(low_keep, low_pass)
low_back.defvjp(back_keep, back_low)

def norm_rows(values, row_gain, row_shift):
    row_mean = lax.optimization_barrier(jnp.mean(values, axis=-1, keepdims=True))
    centered = values - row_mean
    spread = lax.optimization_barrier(jnp.mean(centered * centered, axis=-1, keepdims=True))
    return centered * lax.rsqrt(spread + EPS) * row_gain + row_shift

def attend_row(row_heads):
    factor = HEAD_DIM ** (-0.5)
    scores = low_back(jnp.einsum('qhd,khd->hqk', row_heads[:, 0], row_heads[:, 1], precision=HIGH)) * factor
    weights = low(jax.nn.softmax(scores, axis=-1))
    return jnp.einsum('hqk,khd->qhd', weights, row_heads[:, 2], precision=HIGH)

def layer(params, hidden):
    position_table, embed_gain, embed_shift, project_in, query_bias, value_bias, project_out, output_bias, middle_gain, middle_shift, expand_weight, expand_bias, shrink_weight, shrink_bias, final_gain, final_shift = params
    row_count = hidden.shape[0]
    length = hidden.shape[1]
    embedded = (hidden + position_table[:length]).reshape(-1, D)
    base = norm_rows(embedded, embed_gain, embed_shift)
    bias_all = jnp.concatenate([query_bias, jnp.zeros_like(query_bias), value_bias])
    triple = low_back(low(jnp.dot(low(base), project_in, precision=HIGH) + bias_all))
    heads_all = triple.reshape(row_count, length, 3, HEADS, HEAD_DIM)
    context = lax.map(jax.checkpoint(attend_row), heads_all)
    context = low(low_back(context.reshape(-1, D)))
    branch = low_back(jnp.dot(context, project_out, precision=HIGH) + output_bias)
    middle = norm_rows(base + branch, middle_gain, middle_shift)
    expanded = low_back(jnp.dot(low(middle), expand_weight, precision=HIGH) + expand_bias)
    activated = low(jax.nn.gelu(expanded, approximate=False))
    shrunk = low_back(jnp.dot(activated, shrink_weight, precision=HIGH) + shrink_bias)
    result = norm_rows(middle + shrunk, final_gain, final_shift)
    return result.reshape(hidden.shape)

def regroup(data, row_count, span):
    shaped = data.reshape(N_WIDE // 4, 4, N_NARROW, row_count, span, D)
    return shaped.transpose(0, 2, 3, 1, 4, 5).reshape(GROUPS, row_count, 4 * span, D)

def ungroup(data, row_count, span):
    shaped = data.reshape(N_WIDE // 4, N_NARROW, row_count, 4, span, D)
    return shaped.transpose(0, 3, 1, 2, 4, 5).reshape(N_WIDE * N_NARROW, row_count, span, D)

def reference(short_input, long_input, short_cotangent, long_cotangent, short_live, long_live, position_table, embed_gain, embed_shift, project_in, query_bias, value_bias, project_out, output_bias, middle_gain, middle_shift, expand_weight, expand_bias, shrink_weight, shrink_bias, final_gain, final_shift):
    params = tuple((member.astype(jnp.float32) for member in (position_table, embed_gain, embed_shift, project_in, query_bias, value_bias, project_out, output_bias, middle_gain, middle_shift, expand_weight, expand_bias, shrink_weight, shrink_bias, final_gain, final_shift)))
    short_span = SHORT_LEN // 4
    long_span = LONG_LEN // 4
    items = (regroup(short_input.astype(jnp.float32), SHORT_ROWS, short_span), regroup(long_input.astype(jnp.float32), LONG_ROWS, long_span), regroup(short_cotangent.astype(jnp.float32), SHORT_ROWS, short_span), regroup(long_cotangent.astype(jnp.float32), LONG_ROWS, long_span), short_live, long_live)

    def step(totals, item):
        short_rows, long_rows, short_cot, long_cot, short_count, long_count = item
        short_mask = (jnp.arange(SHORT_ROWS, dtype=jnp.int32) < short_count).astype(jnp.float32)[:, None, None]
        long_mask = (jnp.arange(LONG_ROWS, dtype=jnp.int32) < long_count).astype(jnp.float32)[:, None, None]

        def both(weights_all, short_part, long_part):
            return (layer(weights_all, short_part), layer(weights_all, long_part))
        outputs, pullback = jax.vjp(both, params, short_rows, long_rows)
        param_grads, short_grad, long_grad = pullback((short_cot * short_mask, long_cot * long_mask))
        totals = jax.tree.map(jnp.add, totals, param_grads)
        return (totals, ((outputs[0] * short_mask).astype(jnp.bfloat16), (outputs[1] * long_mask).astype(jnp.bfloat16), short_grad.astype(jnp.bfloat16), long_grad.astype(jnp.bfloat16)))
    start = tuple((jnp.zeros_like(member) for member in params))
    totals, stacked = lax.scan(step, start, items)
    return (ungroup(stacked[0], SHORT_ROWS, short_span), ungroup(stacked[1], LONG_ROWS, long_span), ungroup(stacked[2], SHORT_ROWS, short_span), ungroup(stacked[3], LONG_ROWS, long_span), totals[0], totals[1], totals[2], totals[3], totals[4], totals[5], totals[6], totals[7], totals[8], totals[9], totals[10], totals[11], totals[12], totals[13], totals[14], totals[15])
```

```python
import functools

import jax
import jax.numpy as jnp
from jax import lax
from jax.experimental import pallas as pl
from jax.experimental.pallas import tpu as pltpu
from jax.sharding import PartitionSpec as P

HEAD_DIM = 64
LANES = 128
EPS = 1e-05
QUAD = 4
F32 = jnp.float32
BF16 = jnp.bfloat16
BOTH = ("wide", "narrow")
ROOT_HALF = 0.7071067811865476
PHI_ZERO = 0.3989422804014327
VMEM_LIMIT = 56 << 20


def partner(shard, axis, flip):
    return lax.ppermute(shard, axis, [(i, i ^ flip) for i in range(lax.axis_size(axis))])


def pick(tensor, index, axis):
    return lax.dynamic_index_in_dim(tensor, index, axis, keepdims=False)


def after(value, *first):
    return lax.optimization_barrier((value,) + first)[0]


class Chain:
    def __init__(self, partial, turned=False):
        bits = {axis: lax.axis_size(axis).bit_length() - 1 for axis in BOTH}
        self.dims = [("wide", b) for b in reversed(range(bits["wide"]))]
        self.dims += [("narrow", b) for b in reversed(range(bits["narrow"]))]
        middle = [("wide", b) for b in range(1, bits["wide"])]
        self.steps = [("wide", 0)] + middle[:: -1 if turned else 1]
        self.steps += [("narrow", b) for b in range(bits["narrow"])]
        self.total = partial.reshape((2,) * len(self.dims) + (-1,) + partial.shape[1:])
        self.at = 0

    def launch(self):
        axis, bit = self.steps[self.at]
        self.mine = lax.axis_index(axis) // 2**bit % 2
        self.place = self.dims.index((axis, bit))
        away = pick(self.total, 1 - self.mine, self.place)
        self.arrived = partner(away, axis, 2**bit)
        return away

    def land(self):
        self.dims.pop(self.place)
        self.at += 1
        total = pick(self.total, self.mine, self.place).astype(F32) + self.arrived.astype(F32)
        self.total = total if self.at == len(self.steps) else total.astype(BF16)

    def step(self):
        self.land()
        return self.launch()

    def finish(self):
        self.land()
        while self.at < len(self.steps):
            self.launch()
            self.land()
        return self.total


def left_product(a, b):
    return lax.dot_general(a, b, (((0,), (0,)), ((), ())), preferred_element_type=F32)


def right_product(a, b):
    return lax.dot_general(a, b, (((1,), (1,)), ((), ())), preferred_element_type=F32)


def product(a, b):
    return jnp.dot(a, b, preferred_element_type=F32)


def norm_stats(values):
    row_mean = jnp.mean(values, axis=-1, keepdims=True)
    centered = values - row_mean
    spread = jnp.mean(centered * centered, axis=-1, keepdims=True)
    scale = lax.rsqrt(spread + EPS)
    return centered * scale, scale


def norm_back(grad, unit, scale, gain):
    inner = grad * gain
    first = jnp.mean(inner, axis=-1, keepdims=True)
    second = jnp.mean(inner * unit, axis=-1, keepdims=True)
    return scale * (inner - first - unit * second)


def column_sum(values):
    return jnp.sum(values, axis=0, keepdims=True)


def call(kernel, grid, scalars, ins, outs, arrays, scratch=(), aliases=None, flops=0, moved=0):
    return pl.pallas_call(
        kernel,
        grid_spec=pltpu.PrefetchScalarGridSpec(
            num_scalar_prefetch=len(scalars),
            grid=grid,
            in_specs=ins,
            out_specs=[o[0] for o in outs],
            scratch_shapes=list(scratch),
        ),
        out_shape=[o[1] for o in outs],
        input_output_aliases=aliases or {},
        compiler_params=pltpu.CompilerParams(vmem_limit_bytes=VMEM_LIMIT),
        cost_estimate=pl.CostEstimate(flops=flops, bytes_accessed=moved, transcendentals=0),
    )(*scalars, *arrays)


def whole(shape, once=True):
    mode = {"pipeline_mode": pl.Buffered(1)} if once else {}
    return pl.BlockSpec(shape, lambda *_: (0,) * len(shape), **mode)


def shaped(shape, dtype):
    return jax.ShapeDtypeStruct(shape, dtype)


def front_kernel(layout, spot, *refs):
    rows, spans = layout
    cut = rows[0] * spans[0]
    data, places = refs[:2], refs[2:6]
    gain, shift, weight, bias = refs[6:10]
    embedded_out, low_out, triple_out = refs[-3:]
    for at in range(2):
        tokens = data[at][...].astype(F32)
        width = tokens.shape[-1]
        parts = [tokens[:cut], tokens[cut:]]
        for which in range(2):
            place = places[2 * at + which][...].astype(F32)
            part = parts[which].reshape(rows[which], spans[which], width) + place[None]
            parts[which] = part.reshape(-1, width)
        embedded = jnp.concatenate(parts)
        embedded_out[at] = embedded
        unit, _ = norm_stats(embedded)
        base_low = (unit * gain[...] + shift[...]).astype(BF16)
        low_out[at] = base_low
        triple_out[at] = (product(base_low, weight[...]) + bias[...]).astype(BF16)


def front(layout, half, spot, data, table, gain, shift, weight, bias, earlier):
    rows, spans = layout
    tokens, width = data[0].shape
    triple = weight.shape[1]
    ins = [whole((tokens, width))] * 2
    for at in range(2):
        for span in spans:
            k = 2 * half + at
            ins.append(pl.BlockSpec((span, width), lambda i, s, k=k: (s[0] ^ k, 0)))
    ins += [whole((1, width))] * 2 + [whole((width, triple)), whole((1, triple))]
    ins += [pl.BlockSpec(memory_space=pl.ANY)] * len(earlier)
    outs = [
        (
            pl.BlockSpec((2, tokens, n), lambda i, s: (half, 0, 0)),
            shaped((QUAD, tokens, n), dtype),
        )
        for n, dtype in ((width, F32), (width, BF16), (triple, BF16))
    ]
    arrays = list(data) + [table] * 4 + [gain, shift, weight, bias] + list(earlier)
    return call(
        functools.partial(front_kernel, layout),
        (1,),
        [spot],
        ins,
        outs,
        arrays,
        aliases={1 + 10 + i: i for i in range(len(earlier))},
        flops=4 * tokens * width * triple,
        moved=2 * width * triple + 4 * tokens * (8 * width + triple),
    )


def head_rows(block, rows, span, at):
    part = block[:, at * span : (at + 1) * span, :] if rows > 1 else block
    return part.reshape(-1, part.shape[-1])


def first_head(shape):
    return lax.broadcasted_iota(jnp.int32, shape, len(shape) - 1) < HEAD_DIM


def attend_rows(query, key, value):
    first = first_head(query.shape)
    nothing = jnp.zeros_like(query)
    scaled = query * jnp.asarray(HEAD_DIM**-0.5, BF16)
    found = []
    for head in range(2):
        chosen = jnp.where(first, scaled, nothing) if head == 0 else jnp.where(first, nothing, scaled)
        scores = right_product(chosen, key)
        top = jnp.max(scores, axis=-1, keepdims=True)
        powers = jnp.exp(scores - top)
        share = 1.0 / jnp.sum(powers, axis=-1, keepdims=True)
        found.append(product((powers * share).astype(BF16), value))
    return jnp.where(first, found[0], found[1]).astype(BF16)


def attend_kernel(layout, query, key, value, out):
    rows, spans = layout
    for bucket in range(2):

        @pl.when(pl.program_id(1) == bucket)
        def _(bucket=bucket):
            blocks = [ref[...] for ref in (query, key, value)]
            for at in range(rows[bucket]):
                args = [head_rows(b, rows[bucket], spans[bucket], at) for b in blocks]
                result = attend_rows(*args).reshape(QUAD, spans[bucket], LANES)
                out[:, at * spans[bucket] : (at + 1) * spans[bucket], :] = result


def attend_flops(layout, pairs):
    rows, spans = layout
    return sum(2 * pairs * r * (QUAD * s) ** 2 * 2 * HEAD_DIM * 2 for r, s in zip(rows, spans))


def attend(layout, triple):
    rows, spans = layout
    tokens, width = triple.shape[1], triple.shape[2] // 3
    pairs = width // LANES
    size = rows[0] * spans[0]
    ins = [
        pl.BlockSpec((QUAD, size, LANES), lambda p, b, w=w: (0, b, w * pairs + p)) for w in range(3)
    ]
    outs = [
        (
            pl.BlockSpec((QUAD, size, LANES), lambda p, b: (0, b, p)),
            shaped((QUAD, tokens, width), BF16),
        )
    ]
    return call(
        functools.partial(attend_kernel, layout),
        (pairs, 2),
        [],
        ins,
        outs,
        [triple] * 3,
        flops=attend_flops(layout, pairs),
        moved=QUAD * tokens * width * 8,
    )[0]


def attend_back_rows(query, key, value, grad):
    first = first_head(query.shape)
    nothing = jnp.zeros_like(query)
    scaled = query * jnp.asarray(HEAD_DIM**-0.5, BF16)
    query_grads, key_grads, value_grads = [], [], []
    for head in range(2):
        def only(array):
            return jnp.where(first, array, nothing) if head == 0 else jnp.where(first, nothing, array)

        scores = right_product(key, only(scaled))
        top = jnp.max(scores, axis=0, keepdims=True)
        powers = jnp.exp(scores - top)
        soft = powers * (1.0 / jnp.sum(powers, axis=0, keepdims=True))
        prob_grad = right_product(value, only(grad))
        inner = jnp.sum(soft * prob_grad, axis=0, keepdims=True)
        score_grad = (soft * (prob_grad - inner)).astype(BF16)
        value_grads.append(product(soft.astype(BF16), grad))
        key_grads.append(product(score_grad, scaled))
        query_grads.append(left_product(score_grad, key) * HEAD_DIM**-0.5)
    return [
        jnp.where(first, two[0], two[1]).astype(BF16) for two in (query_grads, key_grads, value_grads)
    ]


def attend_back_kernel(layout, bucket, query, key, value, grad, *rest):
    rows, spans = layout[0][bucket], layout[1][bucket]
    outs = rest[-3:]
    blocks = [ref[...] for ref in (query, key, value, grad)]
    for at in range(rows):
        args = [head_rows(b, rows, spans, at) for b in blocks]
        for ref, result in zip(outs, attend_back_rows(*args)):
            ref[:, at * spans : (at + 1) * spans, :] = result.reshape(QUAD, spans, LANES)


def attend_back(layout, bucket, triple, grad, earlier):
    rows, spans = layout
    tokens, width = triple.shape[1], triple.shape[2] // 3
    pairs = width // LANES
    size = rows[0] * spans[0]
    ins = [
        pl.BlockSpec((QUAD, size, LANES), lambda p, w=w: (0, bucket, w * pairs + p)) for w in range(3)
    ]
    one = pl.BlockSpec((QUAD, size, LANES), lambda p: (0, bucket, p))
    ins += [one] + [pl.BlockSpec(memory_space=pl.ANY)] * len(earlier)
    outs = [(one, shaped((QUAD, tokens, width), BF16))] * 3
    return call(
        functools.partial(attend_back_kernel, layout, bucket),
        (pairs,),
        [],
        ins,
        outs,
        [triple] * 3 + [grad] + list(earlier),
        aliases={4 + i: i for i in range(len(earlier))},
        flops=int(2.5 * attend_flops((rows[bucket : bucket + 1], spans[bucket : bucket + 1]), pairs)),
        moved=QUAD * size * width * 14,
    )


def alive_rows(limits, size, count):
    at = lax.broadcasted_iota(jnp.int32, (count, 1), 0)
    short = (at < limits[0]).astype(F32)
    long = (at >= size).astype(F32) * (at < limits[1]).astype(F32)
    return short + long


def ahead_kernel(size, chunk, limits, *refs):
    (context, embedded, cotangent, embed_gain, embed_shift, project_out, output_bias) = refs[:7]
    (middle_gain, middle_shift, expand, expand_bias, shrink, shrink_bias, gain, shift) = refs[7:15]
    (output, inner_out, middle_out, active_out, slope_out, grad_out, grad_low_out, sums) = refs[15:]
    unit, _ = norm_stats(embedded[0])
    inner = unit * embed_gain[...] + embed_shift[...]
    inner = inner + (product(context[0], project_out[...]) + output_bias[...])
    inner_out[0] = inner
    unit, _ = norm_stats(inner)
    middle = unit * middle_gain[...] + middle_shift[...]
    middle_low = middle.astype(BF16)
    middle_out[0] = middle_low
    hidden = expand.shape[1]
    total = middle + shrink_bias[...]
    for start in range(0, hidden, chunk):
        part = slice(start, start + chunk)
        expanded = product(middle_low, expand[:, part]) + expand_bias[:, part]
        below = 0.5 + 0.5 * lax.erf(expanded * ROOT_HALF)
        active = (expanded * below).astype(BF16)
        active_out[0, :, part] = active
        density = jnp.exp(expanded * expanded * -0.5) * PHI_ZERO
        slope_out[0, :, part] = (below + expanded * density).astype(BF16)
        total = total + product(active, shrink[part, :])
    unit, scale = norm_stats(total)
    alive = alive_rows(limits, size, unit.shape[0])
    result = unit * gain[...] + shift[...]
    output[0] = (result * alive).astype(BF16)
    upstream = cotangent[0].astype(F32) * alive
    grad = norm_back(upstream, unit, scale, gain[...])
    grad_low = grad.astype(BF16)
    grad_out[0] = grad
    grad_low_out[0] = grad_low
    found = [column_sum(upstream * unit), column_sum(upstream), column_sum(grad_low.astype(F32))]

    @pl.when(pl.program_id(0) == 0)
    def _():
        sums[...] = jnp.zeros_like(sums)

    for at, value in enumerate(found):
        sums[at : at + 1, :] += value


def ahead(size, limits, context, embedded, cotangent, weights):
    pieces, tokens, width = context.shape
    hidden = weights[6].shape[1]
    row = pl.BlockSpec((1, tokens, width), lambda i, s: (i, 0, 0))
    wide = pl.BlockSpec((1, tokens, hidden), lambda i, s: (i, 0, 0))
    ins = [row] * 3 + [whole(w.shape) for w in weights]
    outs = [(row, shaped((pieces, tokens, width), dtype)) for dtype in (BF16, F32, BF16)]
    outs += [(wide, shaped((pieces, tokens, hidden), BF16))] * 2
    outs += [(row, shaped((pieces, tokens, width), dtype)) for dtype in (F32, BF16)]
    outs += [(whole((8, width), False), shaped((8, width), F32))]
    return call(
        functools.partial(ahead_kernel, size, width),
        (pieces,),
        [limits],
        ins,
        outs,
        [context, embedded, cotangent] + list(weights),
        flops=2 * pieces * tokens * width * (width + 2 * hidden),
        moved=4 * width * hidden + pieces * tokens * (24 * width + 4 * hidden),
    )


def behind_kernel(chunk, *refs):
    grad_low, slope, grad, inner, shrink, expand, project_out, middle_gain = refs[:8]
    expanded_out, mixed_out, mixed_low_out, context_out, sums, bias_sums = refs[8:]

    @pl.when(pl.program_id(0) == 0)
    def _():
        sums[...] = jnp.zeros_like(sums)
        bias_sums[...] = jnp.zeros_like(bias_sums)

    hidden = expand.shape[1]
    total = grad[0]
    for start in range(0, hidden, chunk):
        part = slice(start, start + chunk)
        raised = right_product(grad_low[0], shrink[part, :]) * slope[0, :, part].astype(F32)
        low = raised.astype(BF16)
        expanded_out[0, :, part] = low
        bias_sums[:, part] += column_sum(low.astype(F32))
        total = total + right_product(low, expand[:, part])
    unit, scale = norm_stats(inner[0])
    mixed = norm_back(total, unit, scale, middle_gain[...])
    mixed_low = mixed.astype(BF16)
    mixed_out[0] = mixed
    mixed_low_out[0] = mixed_low
    context_out[0] = right_product(mixed_low, project_out[...]).astype(BF16)
    found = [column_sum(total * unit), column_sum(total), column_sum(mixed_low.astype(F32))]
    for at, value in enumerate(found):
        sums[at : at + 1, :] += value


def behind(grad_low, slope, grad, inner, shrink, expand, project_out, middle_gain):
    pieces, tokens, width = grad.shape
    hidden = expand.shape[1]
    row = pl.BlockSpec((1, tokens, width), lambda i: (i, 0, 0))
    wide = pl.BlockSpec((1, tokens, hidden), lambda i: (i, 0, 0))
    weights = [shrink, expand, project_out, middle_gain]
    ins = [row, wide, row, row] + [whole(w.shape) for w in weights]
    outs = [(wide, shaped((pieces, tokens, hidden), BF16))]
    outs += [(row, shaped((pieces, tokens, width), dtype)) for dtype in (F32, BF16, BF16)]
    outs += [(whole((8, width), False), shaped((8, width), F32))]
    outs += [(whole((1, hidden), False), shaped((1, hidden), F32))]
    return call(
        functools.partial(behind_kernel, width),
        (pieces,),
        [],
        ins,
        outs,
        [grad_low, slope, grad, inner] + weights,
        flops=2 * pieces * tokens * width * (width + 2 * hidden),
        moved=4 * width * hidden + pieces * tokens * (18 * width + 4 * hidden),
    )


def last_kernel(layout, spot, *refs):
    rows, spans = layout
    cut = rows[0] * spans[0]
    query, key, value, mixed, embedded, weight, gain = refs[:7]
    input_out, short_out, long_out, sums = refs[7:]
    width = mixed.shape[-1]
    total = mixed[0]
    for at, ref in enumerate((query, key, value)):
        total = total + right_product(ref[0], weight[:, at * width : (at + 1) * width])
    unit, scale = norm_stats(embedded[0])
    grad = norm_back(total, unit, scale, gain[...])
    input_out[0] = grad.astype(BF16)
    short_out[...] = jnp.sum(grad[:cut].reshape(rows[0], spans[0], width), axis=0)
    long_out[...] = jnp.sum(grad[cut:].reshape(rows[1], spans[1], width), axis=0)
    found = [
        column_sum(total * unit),
        column_sum(total),
        column_sum(query[0].astype(F32)),
        column_sum(value[0].astype(F32)),
    ]

    @pl.when(pl.program_id(0) == 0)
    def _():
        sums[...] = jnp.zeros_like(sums)

    for at, item in enumerate(found):
        sums[at : at + 1, :] += item


def last(layout, spot, grads, mixed, embedded, weight, gain):
    rows, spans = layout
    pieces, tokens, width = mixed.shape
    row = pl.BlockSpec((1, tokens, width), lambda i, s: (i, 0, 0))
    ins = [row] * 5 + [whole(weight.shape), whole(gain.shape)]
    outs = [(row, shaped((pieces, tokens, width), BF16))]
    outs += [
        (
            pl.BlockSpec((span, width), lambda i, s: (s[0] ^ i, 0)),
            shaped((QUAD * span, width), F32),
        )
        for span in spans
    ]
    outs += [(whole((8, width), False), shaped((8, width), F32))]
    return call(
        functools.partial(last_kernel, layout),
        (pieces,),
        [spot],
        ins,
        outs,
        list(grads) + [mixed, embedded, weight, gain],
        flops=6 * pieces * tokens * width * width,
        moved=6 * width * width + pieces * tokens * 18 * width,
    )


def send_pieces(short, long, spot):
    width = short.shape[-1]
    parts = [a.reshape(QUAD, -1, width) for a in (short, long)]
    pieces = []
    for k in range(QUAD):
        piece = jnp.concatenate([pick(a, spot ^ k, 0) for a in parts])
        pieces.append(piece if k == 0 else partner(piece, "wide", k))
    return pieces


def return_pieces(pieces, size, spot):
    homes = [jnp.zeros((QUAD,) + p.shape[1:], p.dtype) for p in (pieces[:, :size], pieces[:, size:])]
    for k in range(QUAD):
        piece = pieces[k] if k == 0 else partner(pieces[k], "wide", k)
        for at, part in enumerate((piece[:size], piece[size:])):
            homes[at] = lax.dynamic_update_index_in_dim(homes[at], part, spot ^ k, 0)
    return homes


def on_device(
    short_input,
    long_input,
    short_cotangent,
    long_cotangent,
    short_live,
    long_live,
    position_table,
    embed_gain,
    embed_shift,
    project_in,
    query_bias,
    value_bias,
    project_out,
    output_bias,
    middle_gain,
    middle_shift,
    expand_weight,
    expand_bias,
    shrink_weight,
    shrink_bias,
    final_gain,
    final_shift,
):
    width = short_input.shape[-1]
    spot = lax.axis_index("wide") % QUAD
    group = lax.axis_index("wide") // QUAD * lax.axis_size("narrow") + lax.axis_index("narrow")
    rows = (short_input.shape[1] // QUAD, long_input.shape[1] // QUAD)
    spans = (short_input.shape[2], long_input.shape[2])
    layout = (rows, spans)
    size = rows[0] * spans[0]
    assert size == rows[1] * spans[1]
    spots = jnp.asarray(spot, jnp.int32).reshape(1)
    alive = [
        jnp.clip(pick(live, group, 0) - spot * r, 0, r) * s
        for live, r, s in zip((short_live, long_live), rows, spans)
    ]
    limits = jnp.stack([alive[0], size + alive[1]]).astype(jnp.int32)

    def line(*vectors):
        return jnp.concatenate(vectors).astype(F32)[None]

    pieces = send_pieces(short_input, long_input, spot)
    cotangent = jnp.stack(send_pieces(short_cotangent, long_cotangent, spot))
    embed_lines = (line(embed_gain), line(embed_shift))
    bias_line = line(query_bias, jnp.zeros_like(query_bias), value_bias)
    found = ()
    for half in range(2):
        found = front(
            layout,
            half,
            spots,
            pieces[2 * half : 2 * half + 2],
            position_table,
            *embed_lines,
            project_in,
            bias_line,
            found,
        )
    embedded, base_low, triple = found
    context = attend(layout, triple)
    weights = embed_lines + (
        project_out,
        line(output_bias),
        line(middle_gain),
        line(middle_shift),
        expand_weight,
        line(expand_bias),
        shrink_weight,
        line(shrink_bias),
        line(final_gain),
        line(final_shift),
    )
    output, inner, middle_low, active, slope, grad, grad_low, final_sums = ahead(
        size, limits, context, embedded, cotangent, weights
    )
    flat = lambda a: a.reshape(-1, a.shape[-1])
    shrink_chain = Chain(left_product(flat(active), flat(grad_low)).astype(BF16))
    sent = shrink_chain.launch()
    expanded_low, mixed, mixed_low, context_grad, middle_sums, expand_sums = behind(
        after(grad_low, sent), slope, grad, inner, shrink_weight, expand_weight, project_out, line(middle_gain)
    )
    expand_chain = Chain(left_product(flat(middle_low), flat(expanded_low)).astype(BF16), True)
    out_chain = Chain(left_product(flat(context), flat(mixed_low)).astype(BF16), True)
    sent = [expand_chain.launch(), out_chain.launch(), shrink_chain.step()]
    grads = attend_back(layout, 0, triple, after(context_grad, *sent), ())
    sent = [expand_chain.step(), out_chain.step()]
    grads = attend_back(layout, 1, triple, after(context_grad, *sent, grads[0]), grads)
    in_parts = [left_product(flat(base_low), flat(g)).astype(BF16) for g in grads]
    in_chains = [
        Chain(jnp.concatenate([in_parts[0], in_parts[1][:, : width // 2]], axis=1)),
        Chain(jnp.concatenate([in_parts[1][:, width // 2 :], in_parts[2]], axis=1), True),
    ]
    sent = [c.launch() for c in in_chains] + [shrink_chain.step()]
    input_grad, short_sum, long_sum, embed_sums = last(
        layout, spots, grads, after(mixed, *sent), embedded, project_in, embed_lines[0]
    )
    position = jnp.concatenate([long_sum[: short_sum.shape[0]] + short_sum, long_sum[short_sum.shape[0] :]])
    hidden = expand_weight.shape[1]
    vectors = jnp.concatenate(
        [
            embed_sums[:4],
            final_sums[:3],
            middle_sums[:3],
            jnp.zeros((LANES - 10, width), F32),
        ]
    )
    spread = expand_sums.reshape(width, hidden // width)
    tail = jnp.concatenate([position, vectors]).T
    tail = lax.dynamic_update_slice_in_dim(tail, spread, position.shape[0] + 10, 1)
    tail_chain = Chain(tail.astype(BF16), True)
    tail_chain.launch()
    outputs = return_pieces(output, size, spot)
    input_grads = return_pieces(input_grad, size, spot)
    shrink_grad = shrink_chain.finish()
    expand_grad = expand_chain.finish()
    out_grad = out_chain.finish()
    in_grad = jnp.concatenate([c.finish() for c in in_chains], axis=1)
    tail_sum = tail_chain.finish()
    length = position.shape[0]
    position_grad = tail_sum[:, :length].T
    vector = [tail_sum[:, length + i] for i in range(10)]
    expand_bias_grad = tail_sum[:, length + 10 : length + 10 + hidden // width].reshape(-1)
    return (
        outputs[0].reshape(short_input.shape),
        outputs[1].reshape(long_input.shape),
        input_grads[0].reshape(short_input.shape),
        input_grads[1].reshape(long_input.shape),
        position_grad,
        vector[0],
        vector[1],
        in_grad,
        vector[2],
        vector[3],
        out_grad,
        vector[9],
        vector[7],
        vector[8],
        expand_grad,
        expand_bias_grad,
        shrink_grad,
        vector[6],
        vector[4],
        vector[5],
    )


def solution(mesh):
    rows = P(BOTH, None, None, None)
    vector, matrix = P(BOTH), P(BOTH, None)
    in_specs = (rows,) * 4 + (P(),) * 18
    out_specs = (rows,) * 4 + (
        P(None, BOTH),
        vector,
        vector,
        matrix,
        vector,
        vector,
        matrix,
        vector,
        vector,
        vector,
        matrix,
        vector,
        matrix,
        vector,
        vector,
        vector,
    )
    return jax.shard_map(on_device, mesh=mesh, in_specs=in_specs, out_specs=out_specs, check_vma=False)
```

```python
import functools

import jax
import jax.numpy as jnp
from jax import lax
from jax.experimental import pallas as pl
from jax.experimental.pallas import tpu as pltpu
from jax.sharding import PartitionSpec as P

HEAD_DIM = 64
LANES = 128
EPS = 1e-05
QUAD = 4
F32 = jnp.float32
BF16 = jnp.bfloat16
BOTH = ("wide", "narrow")
ROOT_HALF = 0.7071067811865476
PHI_ZERO = 0.3989422804014327


def partner(shard, axis, flip):
    return lax.ppermute(shard, axis, [(i, i ^ flip) for i in range(lax.axis_size(axis))])


def pick(tensor, index, axis):
    return lax.dynamic_index_in_dim(tensor, index, axis, keepdims=False)


def after(value, *first):
    return lax.optimization_barrier((value,) + first)[0]


def halving_steps():
    wide_bits, narrow_bits = [lax.axis_size(axis).bit_length() - 1 for axis in BOTH]
    middle = [("wide", b) for b in range(1, wide_bits)]
    narrow = [("narrow", b) for b in range(narrow_bits)]
    return middle, middle[::-1], narrow


def bit_of(index, bit):
    return index // 2**bit % 2


def sort_rows(width):
    middle, _, narrow = halving_steps()
    each = width // (lax.axis_size("wide") * lax.axis_size("narrow"))
    natural = jnp.arange(width)
    index = {"narrow": natural // each % lax.axis_size("narrow")}
    index["wide"] = natural // each // lax.axis_size("narrow")
    goes = (bit_of(index["wide"], 0) == lax.axis_index("wide") % 2).astype(jnp.int32)
    for axis, bit in middle + narrow:
        goes = 2 * goes + bit_of(index[axis], bit)
    goes = goes * each + natural % each
    return (goes[None, :] == natural[:, None]).astype(BF16)


class Chain:
    def __init__(self, dims, steps):
        self.dims, self.steps = list(dims), list(steps)
        self.away = self.mine = self.arrived = None

    def sides(self, arrays, columns=None):
        axis, bit = self.steps.pop(0)
        place = self.dims.index((axis, bit))
        here = bit_of(lax.axis_index(axis), bit)
        start, size = columns or (0, arrays[0].shape[-1])
        arrays = [a.reshape((2,) * len(self.dims) + (-1, a.shape[-1])) for a in arrays]
        sizes = list(arrays[0].shape[:-1]) + [size]
        sizes[place] = 1
        self.dims.pop(place)
        found = []
        for side in (1 - here, here):
            starts = [jnp.int32(0)] * (len(sizes) - 1) + [jnp.int32(start)]
            starts[place] = jnp.asarray(side, jnp.int32)
            parts = [lax.dynamic_slice(a, starts, sizes).astype(F32) for a in arrays]
            found.append(jnp.squeeze(sum(parts).astype(BF16), place))
        self.away, self.mine = found
        self.arrived = partner(self.away, axis, 2**bit)
        return self.away

    def wait(self, *first):
        self.arrived = after(self.arrived, *first)

    def step(self, *first):
        if first:
            self.wait(*first)
        return self.sides([self.mine, self.arrived])

    def total(self):
        return self.mine.astype(F32) + self.arrived.astype(F32)

    def finish(self):
        while self.steps:
            self.step()
        return self.total()


def fork(arrived, mine, dims, orders):
    mine = lax.optimization_barrier(mine)
    width = mine.shape[-1] // len(orders)
    chains = []
    for at, steps in enumerate(orders):
        chains.append(Chain(dims, steps))
        chains[-1].sides([mine, arrived], (at * width, width))
    return chains


def sends(chains):
    return [chain.away for chain in chains]


def join(chains):
    one = Chain(chains[0].dims, chains[0].steps)
    one.sides([jnp.concatenate([chain.total().astype(BF16) for chain in chains], axis=-1)])
    return one


def left_product(a, b):
    return lax.dot_general(a, b, (((0,), (0,)), ((), ())), preferred_element_type=F32)


def right_product(a, b):
    return lax.dot_general(a, b, (((1,), (1,)), ((), ())), preferred_element_type=F32)


def product(a, b):
    return jnp.dot(a, b, preferred_element_type=F32)


def norm_stats(values):
    row_mean = jnp.mean(values, axis=-1, keepdims=True)
    centered = values - row_mean
    spread = jnp.mean(centered * centered, axis=-1, keepdims=True)
    scale = lax.rsqrt(spread + EPS)
    return centered * scale, scale


def norm_back(grad, unit, scale, gain):
    inner = grad * gain
    first = jnp.mean(inner, axis=-1, keepdims=True)
    second = jnp.mean(inner * unit, axis=-1, keepdims=True)
    return scale * (inner - first - unit * second)


def column_sum(values):
    return jnp.sum(values, axis=0, keepdims=True)


def call(kernel, grid, scalars, ins, outs, arrays, scratch=(), aliases=None, flops=0, moved=0, room=16):
    return pl.pallas_call(
        kernel,
        grid_spec=pltpu.PrefetchScalarGridSpec(
            num_scalar_prefetch=len(scalars),
            grid=grid,
            in_specs=ins,
            out_specs=[o[0] for o in outs],
            scratch_shapes=list(scratch),
        ),
        out_shape=[o[1] for o in outs],
        input_output_aliases=aliases or {},
        compiler_params=pltpu.CompilerParams(vmem_limit_bytes=room << 20),
        cost_estimate=pl.CostEstimate(flops=flops, bytes_accessed=moved, transcendentals=0),
    )(*scalars, *arrays)


def whole(shape, once=True):
    mode = {"pipeline_mode": pl.Buffered(1)} if once else {}
    return pl.BlockSpec(shape, lambda *_: (0,) * len(shape), **mode)


def shaped(shape, dtype):
    return jax.ShapeDtypeStruct(shape, dtype)


def kept(array):
    return pltpu.with_memory_space_constraint(array, pltpu.HBM)


def head_rows(block, rows, span, at):
    part = block[:, at * span : (at + 1) * span, :] if rows > 1 else block
    return part.reshape(-1, part.shape[-1])


def first_head(shape):
    return lax.broadcasted_iota(jnp.int32, shape, len(shape) - 1) < HEAD_DIM


def pair_rows(ref, layout, bucket):
    rows, span = layout[0][bucket], layout[1][bucket]
    found = []
    for start in range(0, ref.shape[-1], LANES):
        block = ref[:, :, start : start + LANES]
        found += [head_rows(block, rows, span, at) for at in range(rows)]
    return found


def attend_rows(queries, keys, values):
    first = first_head(queries[0].shape)
    nothing, ones = jnp.zeros_like(queries[0]), jnp.ones_like(queries[0])
    scores = []
    for query, key in zip(queries, keys):
        query = query * jnp.asarray(HEAD_DIM**-0.5, BF16)
        scores.append(right_product(jnp.where(first, query, nothing), key))
        scores.append(right_product(jnp.where(first, nothing, query), key))
    count = queries[0].shape[0]
    scores = jnp.concatenate(scores)
    powers = jnp.exp(scores - jnp.max(scores, axis=-1, keepdims=True)).astype(BF16)
    results = []
    for at, value in enumerate(values):
        left = product(powers[2 * at * count : (2 * at + 1) * count], jnp.where(first, value, ones))
        right = product(powers[(2 * at + 1) * count : (2 * at + 2) * count], jnp.where(first, ones, value))
        left = left * (1.0 / left[:, HEAD_DIM : HEAD_DIM + 1])
        right = right * (1.0 / right[:, :1])
        results.append(jnp.where(first, left, right).astype(BF16))
    return results


def attend_part(layout, triple, out):
    rows, spans = layout
    size = rows[0] * spans[0]
    width = out.shape[-1]
    columns = width // 2

    @pl.loop(0, 2)
    def _(step):
        for bucket in range(2):
            count, span = rows[bucket], spans[bucket]
            tokens = slice(bucket * size, (bucket + 1) * size)
            lists = []
            for which in range(3):
                place = pl.multiple_of(which * width + step * columns, LANES)
                block = triple[:, tokens, pl.ds(place, columns)]
                lists.append(pair_rows(block, layout, bucket))
            for start in range(0, len(lists[0]), count):
                results = attend_rows(*[part[start : start + count] for part in lists])
                place = pl.multiple_of(step * columns + start // count * LANES, LANES)
                for at, result in enumerate(results):
                    first = bucket * size + at * span
                    result = result.reshape(QUAD, span, LANES)
                    out[:, first : first + span, pl.ds(place, LANES)] = result


def attend_flops(layout, pairs):
    rows, spans = layout
    return sum(2 * pairs * r * (QUAD * s) ** 2 * 2 * HEAD_DIM * 2 for r, s in zip(rows, spans))


def front_kernel(layout, spot, *refs):
    rows, spans = layout
    cut = rows[0] * spans[0]
    data, places = refs[:QUAD], refs[QUAD : 3 * QUAD]
    lines, weight, sort = refs[3 * QUAD : 3 * QUAD + 3]
    embedded_out, away_out, mine_out, triple_out, context_out = refs[3 * QUAD + 3 :]
    gain, shift, query_bias, value_bias = [lines[at : at + 1] for at in range(4)]
    for at in range(QUAD):
        tokens = data[at][...].astype(F32)
        width = tokens.shape[-1]
        parts = [tokens[:cut], tokens[cut:]]
        for which in range(2):
            place = places[2 * at + which][...].astype(F32)
            part = parts[which].reshape(rows[which], spans[which], width) + place[None]
            parts[which] = part.reshape(-1, width)
        embedded = jnp.concatenate(parts)
        embedded_out[at] = embedded
        unit, _ = norm_stats(embedded)
        base_low = (unit * gain + shift).astype(BF16)
        sorted_low = right_product(base_low, sort[...]).astype(BF16)
        away_out[at] = sorted_low[:, : width // 2]
        mine_out[at] = sorted_low[:, width // 2 :]
        for which, bias in enumerate((query_bias, 0.0, value_bias)):
            part = slice(which * width, (which + 1) * width)
            triple_out[at, :, part] = (product(base_low, weight[:, part]) + bias).astype(BF16)
    attend_part(layout, triple_out, context_out)


def front(layout, spot, data, table, lines, weight, sort):
    rows, spans = layout
    tokens, width = data[0].shape
    triple = weight.shape[1]
    ins = [whole((tokens, width))] * QUAD
    for k in range(QUAD):
        ins += [pl.BlockSpec((span, width), lambda i, s, k=k: (s[0] ^ k, 0)) for span in spans]
    ins += [whole(a.shape) for a in (lines, weight, sort)]
    outs = []
    for n, dtype in ((width, F32), (width // 2, BF16), (width // 2, BF16), (triple, BF16), (width, BF16)):
        outs.append((whole((QUAD, tokens, n)), pltpu.HBM((QUAD, tokens, n), dtype)))
    outs[-1] = (outs[-1][0], shaped((QUAD, tokens, width), BF16))
    return call(
        functools.partial(front_kernel, layout),
        (1,),
        [spot],
        ins,
        outs,
        [kept(d) for d in data] + [kept(table)] * (2 * QUAD) + [lines, kept(weight), kept(sort)],
        flops=2 * QUAD * tokens * width * triple + attend_flops(layout, width // LANES),
        moved=2 * width * triple + QUAD * tokens * (8 * width + 2 * triple),
        room=30,
    )


def attend_back_rows(queries, keys, values, grads):
    first = first_head(queries[0].shape)
    nothing = jnp.zeros_like(queries[0])
    scaled = [query * jnp.asarray(HEAD_DIM**-0.5, BF16) for query in queries]
    scores, prob_grads = [], []
    for query, key, value, grad in zip(scaled, keys, values, grads):
        scores.append(right_product(key, jnp.where(first, query, nothing)))
        scores.append(right_product(key, jnp.where(first, nothing, query)))
        prob_grads.append(right_product(value, jnp.where(first, grad, nothing)))
        prob_grads.append(right_product(value, jnp.where(first, nothing, grad)))
    scores = jnp.concatenate(scores, axis=1)
    prob_grad = jnp.concatenate(prob_grads, axis=1)
    powers = jnp.exp(scores - jnp.max(scores, axis=0, keepdims=True))
    soft = powers * (1.0 / jnp.sum(powers, axis=0, keepdims=True))
    inner = jnp.sum(soft * prob_grad, axis=0, keepdims=True)
    score_grad = (soft * (prob_grad - inner)).astype(BF16)
    weights = soft.astype(BF16)
    count = queries[0].shape[0]
    results = []
    for at, (query, key, grad) in enumerate(zip(scaled, keys, grads)):
        two = []
        for head in range(2):
            part = slice((2 * at + head) * count, (2 * at + head + 1) * count)
            two.append(
                (
                    left_product(score_grad[:, part], key) * HEAD_DIM**-0.5,
                    product(score_grad[:, part], query),
                    product(weights[:, part], grad),
                )
            )
        results.append([jnp.where(first, a, b).astype(BF16) for a, b in zip(*two)])
    return results


def attend_back_kernel(layout, bucket, group, query, key, value, grad, *rest):
    count, span = layout[0][bucket], layout[1][bucket]
    out = rest[-1]
    width = out.shape[-1] // 3
    step = pl.program_id(0) * query.shape[-1]
    lists = [pair_rows(ref, layout, bucket) for ref in (query, key, value, grad)]
    for start in range(0, len(lists[0]), group):
        results = attend_back_rows(*[part[start : start + group] for part in lists])
        for at, three in enumerate(results):
            pair, row = divmod(start + at, count)
            for which, result in enumerate(three):
                place = pl.multiple_of(which * width + step + pair * LANES, LANES)
                rows = slice(row * span, (row + 1) * span)
                out[:, rows, pl.ds(place, LANES)] = result.reshape(QUAD, span, LANES)


def attend_back(layout, bucket, triple, grad, earlier):
    rows, spans = layout
    tokens, width = triple.shape[1], triple.shape[2] // 3
    pairs = width // LANES
    size = rows[0] * spans[0]
    steps = 2 if rows[bucket] > 1 else 3
    columns = width // steps
    group = rows[bucket] if rows[bucket] > 1 else 2
    ins = [
        pl.BlockSpec((QUAD, size, columns), lambda p, w=w: (0, bucket, w * steps + p)) for w in range(3)
    ]
    ins += [pl.BlockSpec((QUAD, size, columns), lambda p: (0, bucket, p))]
    ins += [pl.BlockSpec(memory_space=pl.ANY)] * len(earlier)
    outs = [
        (
            pl.BlockSpec((QUAD, size, 3 * width), lambda p: (0, bucket, 0)),
            shaped((QUAD, tokens, 3 * width), BF16),
        )
    ]
    return call(
        functools.partial(attend_back_kernel, layout, bucket, group),
        (steps,),
        [],
        ins,
        outs,
        [kept(triple)] * 3 + [kept(grad)] + list(earlier),
        aliases={4 + i: i for i in range(len(earlier))},
        flops=int(2.5 * attend_flops((rows[bucket : bucket + 1], spans[bucket : bucket + 1]), pairs)),
        room=18,
        moved=QUAD * size * width * 14,
    )


def alive_rows(limits, size, count):
    at = lax.broadcasted_iota(jnp.int32, (count, 1), 0)
    short = (at < limits[0]).astype(F32)
    long = (at >= size).astype(F32) * (at < limits[1]).astype(F32)
    return short + long


def hidden_parts(core, hidden, block, chunk):
    if block % LANES:
        return [([(start, chunk)], start) for start in range(0, hidden, chunk)]
    places = []
    for half in range(2):
        side = core if half else 1 - core
        places += [
            (pl.multiple_of((2 * at + side) * block, LANES), block) for at in range(hidden // block // 2)
        ]
    each = chunk // block
    return [(places[at : at + each], at * block) for at in range(0, len(places), each)]


def columns_of(ref, places, lead=()):
    return jnp.concatenate([ref[lead + (slice(None), pl.ds(*p))] for p in places], axis=-1)


def rows_of(ref, places):
    return jnp.concatenate([ref[pl.ds(*p), :] for p in places], axis=0)


def middle_rows(size, block, chunk, limits, *refs):
    (context, embedded, *cotangents) = refs[: 2 + QUAD]
    refs = refs[2 + QUAD :]
    (sort, lines, project_out, expand, expand_bias, shrink) = refs[:6]
    (output, middle_away, middle_mine, context_away, context_mine, active_away, active_mine) = refs[6:13]
    (grad_low_out, expanded_out, mixed_out, mixed_low_out, context_out, sums, bias_sums, slopes) = refs[13:]
    embed_gain, embed_shift = lines[0:1], lines[1:2]
    output_bias, middle_gain, middle_shift, shrink_bias, gain, shift = [
        lines[at : at + 1] for at in range(4, 10)
    ]
    width = context.shape[-1]
    half = width // 2
    hidden = expand.shape[1]
    parts = hidden_parts(limits[2], hidden, block, chunk)
    unit, _ = norm_stats(embedded[0])
    inner = unit * embed_gain + embed_shift
    inner = inner + (product(context[0], project_out[...]) + output_bias)
    sorted_low = right_product(context[0], sort[...]).astype(BF16)
    context_away[0] = sorted_low[:, :half]
    context_mine[0] = sorted_low[:, half:]
    inner_unit, inner_scale = norm_stats(inner)
    middle = inner_unit * middle_gain + middle_shift
    middle_low = middle.astype(BF16)
    sorted_low = right_product(middle_low, sort[...]).astype(BF16)
    middle_away[0] = sorted_low[:, :half]
    middle_mine[0] = sorted_low[:, half:]
    total = middle + shrink_bias
    for places, start in parts:
        part = slice(start, start + chunk)
        expanded = product(middle_low, columns_of(expand, places)) + columns_of(expand_bias, places)
        below = 0.5 + 0.5 * lax.erf(expanded * ROOT_HALF)
        active = (expanded * below).astype(BF16)
        if start < hidden // 2:
            active_away[0, :, part] = active
        else:
            active_mine[0, :, start - hidden // 2 : start - hidden // 2 + chunk] = active
        density = jnp.exp(expanded * expanded * -0.5) * PHI_ZERO
        slopes[:, part] = (below + expanded * density).astype(BF16)
        total = total + product(active, rows_of(shrink, places))
    unit, scale = norm_stats(total)
    alive = alive_rows(limits, size, unit.shape[0])
    result = unit * gain + shift
    output[0] = (result * alive).astype(BF16)
    cotangent = cotangents[0][...]
    for k in range(1, QUAD):
        cotangent = jnp.where(pl.program_id(0) == k, cotangents[k][...], cotangent)
    upstream = cotangent.astype(F32) * alive
    grad = norm_back(upstream, unit, scale, gain)
    grad_low = grad.astype(BF16)
    grad_low_out[0] = grad_low
    found = [column_sum(upstream * unit), column_sum(upstream), column_sum(grad_low.astype(F32))]
    total = grad
    for places, start in parts:
        part = slice(start, start + chunk)
        raised = right_product(grad_low, rows_of(shrink, places)) * slopes[:, part].astype(F32)
        low = raised.astype(BF16)
        sums_low = column_sum(low.astype(F32))
        done = 0
        for place in places:
            expanded_out[0, :, pl.ds(*place)] = low[:, done : done + place[1]]
            bias_sums[:, pl.ds(*place)] += sums_low[:, done : done + place[1]]
            done += place[1]
        total = total + right_product(low, columns_of(expand, places))
    mixed = norm_back(total, inner_unit, inner_scale, middle_gain)
    mixed_low = mixed.astype(BF16)
    mixed_out[0] = mixed
    mixed_low_out[0] = mixed_low
    context_out[0] = right_product(mixed_low, project_out[...]).astype(BF16)
    found += [column_sum(total * inner_unit), column_sum(total), column_sum(mixed_low.astype(F32))]
    for at, value in enumerate(found):
        sums[at : at + 1, :] += value


def middle_kernel(size, block, chunk, limits, *refs):
    sums, bias_sums = refs[-3:-1]

    @pl.when(pl.program_id(0) == 0)
    def _():
        sums[...] = jnp.zeros_like(sums)
        bias_sums[...] = jnp.zeros_like(bias_sums)

    middle_rows(size, block, chunk, limits, *refs)


def middle_part(size, block, limits, context, embedded, cotangents, weights):
    pieces, tokens, width = context.shape
    hidden = weights[3].shape[1]

    def out(columns, dtype=BF16, keep=pltpu.HBM):
        blocked = pl.BlockSpec((1, tokens, columns), lambda i, s: (i, 0, 0))
        return blocked, keep((pieces, tokens, columns), dtype)

    ins = [out(width)[0]] * 2 + [whole(c.shape) for c in cotangents] + [whole(w.shape) for w in weights]
    outs = [out(width)] + [out(width // 2)] * 4 + [out(hidden // 2, keep=shaped)] * 2
    outs += [out(width, keep=shaped), out(hidden, keep=shaped)]
    outs += [out(width, F32), out(width), out(width)]
    outs += [(whole((8, width), False), shaped((8, width), F32))]
    outs += [(whole((1, hidden), False), shaped((1, hidden), F32))]
    return call(
        functools.partial(middle_kernel, size, block, width),
        (pieces,),
        [limits],
        ins,
        outs,
        [context, kept(embedded)] + [kept(c) for c in cotangents] + [kept(w) for w in weights],
        scratch=[pltpu.VMEM((tokens, hidden), BF16)],
        flops=4 * pieces * tokens * width * (width + 2 * hidden),
        moved=4 * width * hidden + pieces * tokens * (30 * width + 4 * hidden),
        room=38,
    )


def last_kernel(layout, spot, *refs):
    rows, spans = layout
    cut = rows[0] * spans[0]
    length = QUAD * spans[1]
    triple, mixed, embedded, weight, lines, early, sort = refs[:7]
    input_out, tail_away, tail_mine, pile, short_pile = refs[7:]
    width = mixed.shape[-1]
    step = pl.program_id(0)

    @pl.when(step == 0)
    def _():
        pile[length:, :] = jnp.zeros((pile.shape[0] - length, width), F32)
        pile[length + 8 : length + 8 + early.shape[0], :] = early[...]

    total = mixed[0] + right_product(triple[0], weight[...])
    unit, scale = norm_stats(embedded[0])
    grad = norm_back(total, unit, scale, lines[0:1])
    input_out[0] = grad.astype(BF16)
    place = spot[0] ^ step
    short_rows = pl.ds(pl.multiple_of(place * spans[0], spans[0]), spans[0])
    long_rows = pl.ds(pl.multiple_of(place * spans[1], spans[1]), spans[1])
    short_pile[short_rows, :] = jnp.sum(grad[:cut].reshape(rows[0], spans[0], width), axis=0)
    pile[long_rows, :] = jnp.sum(grad[cut:].reshape(rows[1], spans[1], width), axis=0)
    found = [
        column_sum(total * unit),
        column_sum(total),
        column_sum(triple[0, :, :width].astype(F32)),
        column_sum(triple[0, :, 2 * width :].astype(F32)),
    ]
    for at, item in enumerate(found):
        pile[length + at : length + at + 1, :] += item

    @pl.when(step == QUAD - 1)
    def _():
        shorter = short_pile.shape[0]
        pile[:shorter, :] += short_pile[...]
        tail = right_product(sort[...], pile[...].astype(BF16)).astype(BF16)
        tail_away[...] = tail[: width // 2]
        tail_mine[...] = tail[width // 2 :]


def last(layout, spot, grad, mixed, embedded, weight, lines, early, sort):
    rows, spans = layout
    pieces, tokens, width = mixed.shape
    row = pl.BlockSpec((1, tokens, width), lambda i, s: (i, 0, 0))
    triple = pl.BlockSpec((1, tokens, 3 * width), lambda i, s: (i, 0, 0))
    ins = [triple, row, row] + [whole(a.shape) for a in (weight, lines, early, sort)]
    outs = [(row, pltpu.HBM((pieces, tokens, width), BF16))]
    depth = QUAD * spans[1] + LANES
    half = (width // 2, depth)
    outs += [(whole(half, False), shaped(half, BF16))] * 2
    return call(
        functools.partial(last_kernel, layout),
        (pieces,),
        [spot],
        ins,
        outs,
        [grad, kept(mixed), kept(embedded), kept(weight), lines, early, kept(sort)],
        scratch=[pltpu.VMEM((depth, width), F32), pltpu.VMEM((QUAD * spans[0], width), F32)],
        flops=6 * pieces * tokens * width * width,
        moved=6 * width * width + pieces * tokens * 18 * width,
        room=22,
    )


def settle_kernel(size, spot, *refs):
    parts, (short_out, long_out) = refs[:QUAD], refs[QUAD:]
    for k in range(QUAD):

        @pl.when(pl.program_id(0) == k)
        def _(k=k):
            short_out[0] = parts[k][:size]
            long_out[0] = parts[k][size:]


def settle(size, spot, parts):
    tokens, width = parts[0].shape
    sizes = (size, tokens - size)
    outs = [
        (
            pl.BlockSpec((1, n, width), lambda i, s: (s[0] ^ i, 0, 0)),
            shaped((QUAD, n, width), parts[0].dtype),
        )
        for n in sizes
    ]
    return call(
        functools.partial(settle_kernel, size),
        (QUAD,),
        [spot],
        [whole(p.shape) for p in parts],
        outs,
        [kept(p) for p in parts],
        moved=4 * QUAD * tokens * width,
        room=8,
    )


def cut_pieces(short, long, spot):
    parts = [a.reshape(QUAD, -1, a.shape[-1]) for a in (short, long)]
    return {k: jnp.concatenate([pick(a, spot ^ k, 0) for a in parts]) for k in range(QUAD)}


def swap_pieces(pieces):
    return {k: partner(piece, "wide", k) if k else piece for k, piece in pieces.items()}


def on_device(
    short_input,
    long_input,
    short_cotangent,
    long_cotangent,
    short_live,
    long_live,
    position_table,
    embed_gain,
    embed_shift,
    project_in,
    query_bias,
    value_bias,
    project_out,
    output_bias,
    middle_gain,
    middle_shift,
    expand_weight,
    expand_bias,
    shrink_weight,
    shrink_bias,
    final_gain,
    final_shift,
):
    width = short_input.shape[-1]
    spot = lax.axis_index("wide") % QUAD
    group = lax.axis_index("wide") // QUAD * lax.axis_size("narrow") + lax.axis_index("narrow")
    rows = (short_input.shape[1] // QUAD, long_input.shape[1] // QUAD)
    spans = (short_input.shape[2], long_input.shape[2])
    layout = (rows, spans)
    size = rows[0] * spans[0]
    assert size == rows[1] * spans[1]
    spots = jnp.asarray(spot, jnp.int32).reshape(1)
    alive = [
        jnp.clip(pick(live, group, 0) - spot * r, 0, r) * s
        for live, r, s in zip((short_live, long_live), rows, spans)
    ]
    core = lax.axis_index("wide") % 2
    limits = jnp.stack([alive[0], size + alive[1], core]).astype(jnp.int32)
    sort = sort_rows(width)
    middle_steps, middle_back, narrow_steps = halving_steps()
    up, down = middle_steps + narrow_steps, middle_back + narrow_steps
    flat = lambda a: a.reshape(-1, a.shape[-1])

    def weight_grad(a, b):
        return left_product(flat(a), flat(b)).astype(BF16)

    cuts = cut_pieces(short_input, long_input, spot)
    pieces = swap_pieces(cuts)
    vectors = (embed_gain, embed_shift, query_bias, value_bias, output_bias)
    vectors += (middle_gain, middle_shift, shrink_bias, final_gain, final_shift)
    vectors = jnp.concatenate((after(vectors[0], *cuts.values()),) + vectors[1:])
    lines = vectors.astype(F32).reshape(-1, width)
    cot_cuts = cut_pieces(after(short_cotangent, *cuts.values()), after(long_cotangent, *cuts.values()), spot)
    embedded, base_away, base_mine, triple, context = front(
        layout,
        spots,
        [pieces[k] for k in range(QUAD)],
        position_table,
        after(lines, *cot_cuts.values()),
        project_in,
        sort,
    )
    cot_cuts = {k: after(c, pieces[2], pieces[3]) for k, c in cot_cuts.items()}
    cot_pieces = swap_pieces(cot_cuts)
    cotangents = [cot_pieces[k] for k in range(QUAD)]
    weights = (sort, lines, project_out, expand_weight, expand_bias.astype(F32)[None], shrink_weight)
    hidden = expand_weight.shape[1]
    hidden_block = hidden // lax.axis_size("wide")
    found = middle_part(size, hidden_block, limits, context, embedded, cotangents, weights)
    output, middle_away, middle_mine, context_away, context_mine, active_away, active_mine = found[:7]
    grad_low, expanded_low, mixed, mixed_low, context_grad, sums, expand_sums = found[7:]
    back = {k: output[k] for k in range(QUAD)}
    outputs = swap_pieces(back)
    grad_low = after(grad_low, *back.values())
    if hidden_block % LANES:
        partial = jnp.concatenate([weight_grad(active_away, grad_low), weight_grad(active_mine, grad_low)])
        partial = partial.reshape(-1, 2, hidden_block, width)
        away, mine = [pick(partial, side, 1).reshape(-1, width) for side in (1 - core, core)]
    else:
        away = weight_grad(active_away, grad_low)
        mine = weight_grad(active_mine, after(grad_low, away))
    turned = middle_back[:1] + narrow_steps + middle_back[1:]
    shrink_chains = fork(partner(away, "wide", 1), mine, middle_back + narrow_steps[::-1], [up, down])
    expanded_low = after(expanded_low, *sends(shrink_chains), *[outputs[k] for k in range(1, QUAD)])
    away = jnp.concatenate(
        [weight_grad(middle_away, expanded_low), weight_grad(context_away, mixed_low)], axis=1
    )
    arrived = partner(away, "wide", 1)
    ready = [away]
    mine = jnp.concatenate(
        [
            weight_grad(middle_mine, after(expanded_low, *ready)),
            weight_grad(context_mine, after(mixed_low, *ready)),
        ],
        axis=1,
    )
    expand_chains = fork(arrived, mine, up, [up, down])
    sent = [c.step(*sends(expand_chains)) for c in shrink_chains]
    grads = attend_back(layout, 0, triple, after(context_grad, *sent), ())
    outputs = settle(size, spots, [after(outputs[k], grads[0]) for k in range(QUAD)])
    grads = attend_back(layout, 1, triple, after(context_grad, grads[0], *outputs), grads)
    for chain in shrink_chains:
        chain.wait(grads[0])
    shrink_chain = join(shrink_chains)
    sent = [c.step(shrink_chain.away) for c in expand_chains]
    triple_grad = after(grads[0], *sent)
    away = weight_grad(base_away, triple_grad)
    arrived = partner(away, "wide", 1)
    mine = weight_grad(base_mine, after(triple_grad, away))
    in_chains = fork(arrived, mine, up, [up, turned])
    sent = shrink_chain.step(*sends(in_chains))
    for chain in expand_chains:
        chain.wait(sent)
    expand_chain = join(expand_chains)
    spread = expand_sums.reshape(width, hidden // width).T
    early = jnp.concatenate([sums[:6], spread])
    input_grad, away, mine = last(
        layout,
        spots,
        triple_grad,
        after(mixed, expand_chain.away),
        embedded,
        project_in,
        lines,
        early,
        sort,
    )
    back = after(input_grad, shrink_chain.arrived, expand_chain.arrived, *[c.arrived for c in in_chains])
    arrived = partner(after(away, back), "wide", 1)
    far = swap_pieces({k: back[k] for k in range(2, QUAD)})
    sent = [c.step(back) for c in in_chains]
    (tail_chain,) = fork(after(arrived, *sent), mine, up, [turned])
    near = swap_pieces({k: after(back[k], tail_chain.away) for k in range(2)})
    sent = expand_chain.step(tail_chain.away)
    shrink_chain.wait(sent)
    shrink_grad = shrink_chain.finish()
    sent = [c.step(sent) for c in in_chains]
    sent = tail_chain.step(*sent)
    expand_chain.wait(sent)
    expand_grad = expand_chain.finish()
    sent = [c.step(sent) for c in in_chains]
    sent = tail_chain.step(*sent)
    parts = near | far
    input_grads = settle(size, spots, [after(parts[k], sent) for k in range(QUAD)])
    sent = tail_chain.step(*input_grads)
    for chain in in_chains:
        chain.wait(sent)
    in_grad = jnp.concatenate([c.finish() for c in in_chains], axis=1)
    tail_sum = tail_chain.finish()
    length = QUAD * spans[1]
    position_grad = tail_sum[:, :length].T
    order = (0, 1, 2, 3, 8, 9, 10, 11, 12, 13)
    vector = [tail_sum[:, length + i] for i in order]
    expand_bias_grad = tail_sum[:, length + 14 : length + 14 + hidden // width].reshape(-1)
    expand_grad, out_grad = expand_grad[:, :hidden], expand_grad[:, hidden:]
    return (
        outputs[0].reshape(short_input.shape),
        outputs[1].reshape(long_input.shape),
        input_grads[0].reshape(short_input.shape),
        input_grads[1].reshape(long_input.shape),
        position_grad,
        vector[0],
        vector[1],
        in_grad,
        vector[2],
        vector[3],
        out_grad,
        vector[9],
        vector[7],
        vector[8],
        expand_grad,
        expand_bias_grad,
        shrink_grad,
        vector[6],
        vector[4],
        vector[5],
    )


def solution(mesh):
    rows = P(BOTH, None, None, None)
    vector, matrix = P(BOTH), P(BOTH, None)
    in_specs = (rows,) * 4 + (P(),) * 18
    out_specs = (rows,) * 4 + (
        P(None, BOTH),
        vector,
        vector,
        matrix,
        vector,
        vector,
        matrix,
        vector,
        vector,
        vector,
        matrix,
        vector,
        matrix,
        vector,
        vector,
        vector,
    )
    return jax.shard_map(on_device, mesh=mesh, in_specs=in_specs, out_specs=out_specs, check_vma=False)
```

```python
import functools

import jax
import jax.numpy as jnp
from jax import lax
from jax.experimental import pallas as pl
from jax.experimental.pallas import tpu as pltpu
from jax.sharding import PartitionSpec as P

HEAD_DIM = 64
LANES = 128
EPS = 1e-05
QUAD = 4
F32 = jnp.float32
BF16 = jnp.bfloat16
BOTH = ("wide", "narrow")
ROOT_HALF = 0.7071067811865476
PHI_ZERO = 0.3989422804014327


def partner(shard, axis, flip):
    return lax.ppermute(shard, axis, [(i, i ^ flip) for i in range(lax.axis_size(axis))])


def pick(tensor, index, axis):
    return lax.dynamic_index_in_dim(tensor, index, axis, keepdims=False)


def after(value, *first):
    return lax.optimization_barrier((value,) + first)[0]


def halving_steps():
    wide_bits, narrow_bits = [lax.axis_size(axis).bit_length() - 1 for axis in BOTH]
    middle = [("wide", b) for b in range(1, wide_bits)]
    narrow = [("narrow", b) for b in range(narrow_bits)]
    return middle, middle[::-1], narrow


def bit_of(index, bit):
    return index // 2**bit % 2


def sort_rows(width):
    middle, _, narrow = halving_steps()
    each = width // (lax.axis_size("wide") * lax.axis_size("narrow"))
    natural = jnp.arange(width)
    index = {"narrow": natural // each % lax.axis_size("narrow")}
    index["wide"] = natural // each // lax.axis_size("narrow")
    goes = (bit_of(index["wide"], 0) == lax.axis_index("wide") % 2).astype(jnp.int32)
    for axis, bit in middle + narrow:
        goes = 2 * goes + bit_of(index[axis], bit)
    goes = goes * each + natural % each
    return (goes[None, :] == natural[:, None]).astype(BF16)


class Chain:
    def __init__(self, dims, steps):
        self.dims, self.steps = list(dims), list(steps)
        self.away = self.mine = self.arrived = None

    def sides(self, groups):
        axis, bit = self.steps.pop(0)
        place = self.dims.index((axis, bit))
        here = bit_of(lax.axis_index(axis), bit)
        lead = (2,) * len(self.dims)
        self.dims.pop(place)
        found = []
        for side in (1 - here, here):
            parts = []
            for arrays, start, size in groups:
                total = 0.0
                for array in arrays:
                    array = array.reshape(lead + (-1, array.shape[-1]))
                    sizes = list(array.shape[:-1]) + [size]
                    sizes[place] = 1
                    starts = [jnp.int32(0)] * (len(sizes) - 1) + [jnp.int32(start)]
                    starts[place] = jnp.asarray(side, jnp.int32)
                    total = total + lax.dynamic_slice(array, starts, sizes).astype(F32)
                parts.append(jnp.squeeze(total.astype(BF16), place))
            found.append(parts[0] if len(parts) == 1 else jnp.concatenate(parts, axis=-1))
        self.away, self.mine = found
        self.arrived = partner(self.away, axis, 2**bit)
        return self

    def wait(self, *first):
        self.arrived = after(self.arrived, *first)

    def step(self, *first):
        if first:
            self.wait(*first)
        return self.sides([([self.mine, self.arrived], 0, self.mine.shape[-1])]).away

    def total(self):
        return self.mine.astype(F32) + self.arrived.astype(F32)

    def finish(self):
        while self.steps:
            self.step()
        return self.total()


def sends(chains):
    return [chain.away for chain in chains]


def join(chains):
    groups = [([c.mine, c.arrived], 0, c.mine.shape[-1]) for c in chains]
    return Chain(chains[0].dims, chains[0].steps).sides(groups)


def left_product(a, b):
    return lax.dot_general(a, b, (((0,), (0,)), ((), ())), preferred_element_type=F32)


def right_product(a, b):
    return lax.dot_general(a, b, (((1,), (1,)), ((), ())), preferred_element_type=F32)


def product(a, b):
    return jnp.dot(a, b, preferred_element_type=F32)


def norm_stats(values):
    row_mean = jnp.mean(values, axis=-1, keepdims=True)
    centered = values - row_mean
    spread = jnp.mean(centered * centered, axis=-1, keepdims=True)
    scale = lax.rsqrt(spread + EPS)
    return centered * scale, scale


def norm_back(grad, unit, scale, gain):
    inner = grad * gain
    first = jnp.mean(inner, axis=-1, keepdims=True)
    second = jnp.mean(inner * unit, axis=-1, keepdims=True)
    return scale * (inner - first - unit * second)


def piece_outs(tokens, width):
    one = pl.BlockSpec((tokens, width), lambda i, s: (0, 0))
    two = pl.BlockSpec((tokens, width), lambda i, s: (jnp.maximum(i - 2, 0), 0))
    return [
        (one, pltpu.HBM((tokens, width), BF16)),
        (one, pltpu.HBM((tokens, width), BF16)),
        (two, pltpu.HBM((2 * tokens, width), BF16)),
    ]


def put_piece(outs, value):
    step = pl.program_id(0)
    for at, out in enumerate(outs):

        @pl.when((step == at) | (step == at + 1) if at == 2 else step == at)
        def _(out=out):
            out[...] = value


def column_sum(values):
    return jnp.sum(values, axis=0, keepdims=True)


def call(kernel, grid, scalars, ins, outs, arrays, scratch=(), aliases=None, flops=0, moved=0, room=16):
    return pl.pallas_call(
        kernel,
        grid_spec=pltpu.PrefetchScalarGridSpec(
            num_scalar_prefetch=len(scalars),
            grid=grid,
            in_specs=ins,
            out_specs=[o[0] for o in outs],
            scratch_shapes=list(scratch),
        ),
        out_shape=[o[1] for o in outs],
        input_output_aliases=aliases or {},
        compiler_params=pltpu.CompilerParams(vmem_limit_bytes=room << 20),
        cost_estimate=pl.CostEstimate(flops=flops, bytes_accessed=moved, transcendentals=0),
    )(*scalars, *arrays)


def whole(shape, once=True):
    mode = {"pipeline_mode": pl.Buffered(1)} if once else {}
    return pl.BlockSpec(shape, lambda *_: (0,) * len(shape), **mode)


def shaped(shape, dtype):
    return jax.ShapeDtypeStruct(shape, dtype)


def kept(array):
    return pltpu.with_memory_space_constraint(array, pltpu.HBM)


def head_rows(block, rows, span, at):
    part = block[:, at * span : (at + 1) * span, :] if rows > 1 else block
    return part.reshape(-1, part.shape[-1])


def first_head(shape):
    return lax.broadcasted_iota(jnp.int32, shape, len(shape) - 1) < HEAD_DIM


def pair_rows(ref, layout, bucket):
    rows, span = layout[0][bucket], layout[1][bucket]
    found = []
    for start in range(0, ref.shape[-1], LANES):
        block = ref[:, :, start : start + LANES]
        found += [head_rows(block, rows, span, at) for at in range(rows)]
    return found


def attend_rows(queries, keys, values):
    first = first_head(queries[0].shape)
    nothing, ones = jnp.zeros_like(queries[0]), jnp.ones_like(queries[0])
    scores = []
    for query, key in zip(queries, keys):
        query = query * jnp.asarray(HEAD_DIM**-0.5, BF16)
        scores.append(right_product(jnp.where(first, query, nothing), key))
        scores.append(right_product(jnp.where(first, nothing, query), key))
    count = queries[0].shape[0]
    scores = jnp.concatenate(scores)
    powers = jnp.exp(scores - jnp.max(scores, axis=-1, keepdims=True)).astype(BF16)
    results = []
    for at, value in enumerate(values):
        left = product(powers[2 * at * count : (2 * at + 1) * count], jnp.where(first, value, ones))
        right = product(powers[(2 * at + 1) * count : (2 * at + 2) * count], jnp.where(first, ones, value))
        left = left * (1.0 / left[:, HEAD_DIM : HEAD_DIM + 1])
        right = right * (1.0 / right[:, :1])
        results.append(jnp.where(first, left, right).astype(BF16))
    return results


def attend_part(layout, triple, out):
    rows, spans = layout
    size = rows[0] * spans[0]
    width = out.shape[-1]
    columns = 2 * LANES

    @pl.loop(0, width // columns)
    def _(step):
        for bucket in range(2):
            count, span = rows[bucket], spans[bucket]
            tokens = slice(bucket * size, (bucket + 1) * size)
            lists = []
            for which in range(3):
                place = pl.multiple_of(which * width + step * columns, LANES)
                block = triple[:, tokens, pl.ds(place, columns)]
                lists.append(pair_rows(block, layout, bucket))
            for start in range(0, len(lists[0]), count):
                results = attend_rows(*[part[start : start + count] for part in lists])
                place = pl.multiple_of(step * columns + start // count * LANES, LANES)
                for at, result in enumerate(results):
                    first = bucket * size + at * span
                    result = result.reshape(QUAD, span, LANES)
                    out[:, first : first + span, pl.ds(place, LANES)] = result


def attend_flops(layout, pairs):
    rows, spans = layout
    return sum(2 * pairs * r * (QUAD * s) ** 2 * 2 * HEAD_DIM * 2 for r, s in zip(rows, spans))


def front_kernel(layout, spot, *refs):
    rows, spans = layout
    cut = rows[0] * spans[0]
    data, (table, lines, weight, sort) = refs[:QUAD], refs[QUAD : QUAD + 4]
    embedded_out, away_out, mine_out, triple_out, context_out, pieces = refs[QUAD + 4 :]
    gain, shift, query_bias, value_bias = [lines[at : at + 1] for at in range(4)]
    width = table.shape[-1]
    for at in range(QUAD):
        pieces[at] = data[at][...]

    @pl.loop(0, QUAD)
    def _(at):
        tokens = pieces[at].astype(F32)
        parts = [tokens[:cut], tokens[cut:]]
        for which, span in enumerate(spans):
            place = pl.multiple_of((spot[0] ^ at) * span, span)
            place = table[pl.ds(place, span), :].astype(F32)
            part = parts[which].reshape(rows[which], span, width) + place[None]
            parts[which] = part.reshape(-1, width)
        embedded = jnp.concatenate(parts)
        embedded_out[at] = embedded
        unit, _ = norm_stats(embedded)
        base_low = (unit * gain + shift).astype(BF16)
        sorted_low = right_product(base_low, sort[...]).astype(BF16)
        away_out[at] = sorted_low[:, : width // 2]
        mine_out[at] = sorted_low[:, width // 2 :]
        for which, bias in enumerate((query_bias, 0.0, value_bias)):
            part = slice(which * width, (which + 1) * width)
            triple_out[at, :, part] = (product(base_low, weight[:, part]) + bias).astype(BF16)

    attend_part(layout, triple_out, context_out)


def front(layout, spot, data, table, lines, weight, sort):
    rows, spans = layout
    tokens, width = data[0].shape
    triple = weight.shape[1]
    ins = [whole((tokens, width))] * QUAD
    ins += [whole(a.shape) for a in (table, lines, weight, sort)]
    outs = []
    for n, dtype in ((width, F32), (width // 2, BF16), (width // 2, BF16), (triple, BF16), (width, BF16)):
        outs.append((whole((QUAD, tokens, n)), pltpu.HBM((QUAD, tokens, n), dtype)))
    outs[-1] = (outs[-1][0], shaped((QUAD, tokens, width), BF16))
    return call(
        functools.partial(front_kernel, layout),
        (1,),
        [spot],
        ins,
        outs,
        [kept(d) for d in data] + [table, lines, weight, sort],
        scratch=[pltpu.VMEM((QUAD, tokens, width), BF16)],
        flops=2 * QUAD * tokens * width * triple + attend_flops(layout, width // LANES),
        moved=2 * width * triple + QUAD * tokens * (8 * width + 2 * triple),
        room=30,
    )


def attend_back_rows(queries, keys, values, grads):
    first = first_head(queries[0].shape)
    nothing = jnp.zeros_like(queries[0])
    scaled = [query * jnp.asarray(HEAD_DIM**-0.5, BF16) for query in queries]
    scores, prob_grads = [], []
    for query, key, value, grad in zip(scaled, keys, values, grads):
        scores.append(right_product(key, jnp.where(first, query, nothing)))
        scores.append(right_product(key, jnp.where(first, nothing, query)))
        prob_grads.append(right_product(value, jnp.where(first, grad, nothing)))
        prob_grads.append(right_product(value, jnp.where(first, nothing, grad)))
    scores = jnp.concatenate(scores, axis=1)
    prob_grad = jnp.concatenate(prob_grads, axis=1)
    powers = jnp.exp(scores - jnp.max(scores, axis=0, keepdims=True))
    soft = powers * (1.0 / jnp.sum(powers, axis=0, keepdims=True))
    inner = jnp.sum(soft * prob_grad, axis=0, keepdims=True)
    score_grad = (soft * (prob_grad - inner)).astype(BF16)
    weights = soft.astype(BF16)
    count = queries[0].shape[0]
    results = []
    for at, (query, key, grad) in enumerate(zip(scaled, keys, grads)):
        two = []
        for head in range(2):
            part = slice((2 * at + head) * count, (2 * at + head + 1) * count)
            two.append(
                (
                    left_product(score_grad[:, part], key) * HEAD_DIM**-0.5,
                    product(score_grad[:, part], query),
                    product(weights[:, part], grad),
                )
            )
        results.append([jnp.where(first, a, b).astype(BF16) for a, b in zip(*two)])
    return results


def attend_back_kernel(layout, bucket, group, query, key, value, grad, *rest):
    count, span = layout[0][bucket], layout[1][bucket]
    out = rest[-1]
    width = out.shape[-1] // 3
    step = pl.program_id(0) * query.shape[-1]
    lists = [pair_rows(ref, layout, bucket) for ref in (query, key, value, grad)]
    for start in range(0, len(lists[0]), group):
        results = attend_back_rows(*[part[start : start + group] for part in lists])
        for at, three in enumerate(results):
            pair, row = divmod(start + at, count)
            for which, result in enumerate(three):
                place = pl.multiple_of(which * width + step + pair * LANES, LANES)
                rows = slice(row * span, (row + 1) * span)
                out[:, rows, pl.ds(place, LANES)] = result.reshape(QUAD, span, LANES)


def attend_back(layout, bucket, triple, grad, earlier):
    rows, spans = layout
    tokens, width = triple.shape[1], triple.shape[2] // 3
    pairs = width // LANES
    size = rows[0] * spans[0]
    steps = 2 if rows[bucket] > 1 else 6
    columns = width // steps
    group = rows[bucket]
    ins = [
        pl.BlockSpec((QUAD, size, columns), lambda p, w=w: (0, bucket, w * steps + p)) for w in range(3)
    ]
    ins += [pl.BlockSpec((QUAD, size, columns), lambda p: (0, bucket, p))]
    ins += [pl.BlockSpec(memory_space=pl.ANY)] * len(earlier)
    outs = [
        (
            pl.BlockSpec((QUAD, size, 3 * width), lambda p: (0, bucket, 0)),
            shaped((QUAD, tokens, 3 * width), BF16),
        )
    ]
    return call(
        functools.partial(attend_back_kernel, layout, bucket, group),
        (steps,),
        [],
        ins,
        outs,
        [kept(triple)] * 3 + [kept(grad)] + list(earlier),
        aliases={4 + i: i for i in range(len(earlier))},
        flops=int(2.5 * attend_flops((rows[bucket : bucket + 1], spans[bucket : bucket + 1]), pairs)),
        room=18,
        moved=QUAD * size * width * 14,
    )


def alive_rows(limits, size, count):
    at = lax.broadcasted_iota(jnp.int32, (count, 1), 0)
    short = (at < limits[0]).astype(F32)
    long = (at >= size).astype(F32) * (at < limits[1]).astype(F32)
    return short + long


def hidden_parts(core, hidden, block, chunk):
    if block % LANES:
        return [([(start, chunk)], start) for start in range(0, hidden, chunk)]
    places = []
    for half in range(2):
        side = core if half else 1 - core
        places += [
            (pl.multiple_of((2 * at + side) * block, LANES), block) for at in range(hidden // block // 2)
        ]
    each = chunk // block
    return [(places[at : at + each], at * block) for at in range(0, len(places), each)]


def columns_of(ref, places, lead=()):
    return jnp.concatenate([ref[lead + (slice(None), pl.ds(*p))] for p in places], axis=-1)


def rows_of(ref, places):
    return jnp.concatenate([ref[pl.ds(*p), :] for p in places], axis=0)


def middle_rows(size, block, chunk, limits, *refs):
    (context, embedded, *cotangents) = refs[: 2 + QUAD]
    refs = refs[2 + QUAD :]
    (sort, lines, project_out, expand, expand_bias, shrink) = refs[:6]
    outputs, refs = refs[6:9], refs[9:]
    (middle_away, middle_mine, context_away, context_mine, active_away, active_mine) = refs[:6]
    (grad_low_out, expanded_out, mixed_low_out, context_out, sums, bias_sums, slopes) = refs[6:]
    embed_gain, embed_shift = lines[0:1], lines[1:2]
    output_bias, middle_gain, middle_shift, shrink_bias, gain, shift = [
        lines[at : at + 1] for at in range(4, 10)
    ]
    width = context.shape[-1]
    half = width // 2
    hidden = expand.shape[1]
    parts = hidden_parts(limits[2], hidden, block, chunk)
    unit, _ = norm_stats(embedded[0])
    inner = unit * embed_gain + embed_shift
    inner = inner + (product(context[0], project_out[...]) + output_bias)
    sorted_low = right_product(context[0], sort[...]).astype(BF16)
    context_away[0] = sorted_low[:, :half]
    context_mine[0] = sorted_low[:, half:]
    inner_unit, inner_scale = norm_stats(inner)
    middle = inner_unit * middle_gain + middle_shift
    middle_low = middle.astype(BF16)
    sorted_low = right_product(middle_low, sort[...]).astype(BF16)
    middle_away[0] = sorted_low[:, :half]
    middle_mine[0] = sorted_low[:, half:]
    total = middle + shrink_bias
    for places, start in parts:
        part = slice(start, start + chunk)
        expanded = product(middle_low, columns_of(expand, places)) + columns_of(expand_bias, places)
        below = 0.5 + 0.5 * lax.erf(expanded * ROOT_HALF)
        active = (expanded * below).astype(BF16)
        if start < hidden // 2:
            active_away[0, :, part] = active
        else:
            active_mine[0, :, start - hidden // 2 : start - hidden // 2 + chunk] = active
        density = jnp.exp(expanded * expanded * -0.5) * PHI_ZERO
        slopes[:, part] = (below + expanded * density).astype(BF16)
        total = total + product(active, rows_of(shrink, places))
    unit, scale = norm_stats(total)
    alive = alive_rows(limits, size, unit.shape[0])
    result = unit * gain + shift
    put_piece(outputs, (result * alive).astype(BF16))
    cotangent = cotangents[0][...]
    for k in range(1, QUAD):
        cotangent = jnp.where(pl.program_id(0) == k, cotangents[k][...], cotangent)
    upstream = cotangent.astype(F32) * alive
    grad = norm_back(upstream, unit, scale, gain)
    grad_low = grad.astype(BF16)
    grad_low_out[0] = grad_low
    found = [column_sum(upstream * unit), column_sum(upstream), column_sum(grad_low.astype(F32))]
    total = grad
    for places, start in parts:
        part = slice(start, start + chunk)
        raised = right_product(grad_low, rows_of(shrink, places)) * slopes[:, part].astype(F32)
        low = raised.astype(BF16)
        sums_low = column_sum(low.astype(F32))
        done = 0
        for place in places:
            expanded_out[0, :, pl.ds(*place)] = low[:, done : done + place[1]]
            bias_sums[:, pl.ds(*place)] += sums_low[:, done : done + place[1]]
            done += place[1]
        total = total + right_product(low, columns_of(expand, places))
    mixed = norm_back(total, inner_unit, inner_scale, middle_gain)
    mixed_low = mixed.astype(BF16)
    mixed_low_out[0] = mixed_low
    context_out[0] = right_product(mixed_low, project_out[...]).astype(BF16)
    found += [column_sum(total * inner_unit), column_sum(total), column_sum(mixed_low.astype(F32))]
    for at, value in enumerate(found):
        sums[at : at + 1, :] += value


def middle_kernel(size, block, chunk, limits, *refs):
    sums, bias_sums = refs[-3:-1]

    @pl.when(pl.program_id(0) == 0)
    def _():
        sums[...] = jnp.zeros_like(sums)
        bias_sums[...] = jnp.zeros_like(bias_sums)

    middle_rows(size, block, chunk, limits, *refs)


def middle_part(size, block, limits, context, embedded, cotangents, weights):
    pieces, tokens, width = context.shape
    hidden = weights[3].shape[1]

    def out(columns, dtype=BF16, keep=pltpu.HBM):
        blocked = pl.BlockSpec((1, tokens, columns), lambda i, s: (i, 0, 0))
        return blocked, keep((pieces, tokens, columns), dtype)

    ins = [out(width)[0]] * 2 + [whole(c.shape) for c in cotangents] + [whole(w.shape) for w in weights]
    outs = piece_outs(tokens, width)
    outs += [out(width // 2)] * 4 + [out(hidden // 2, keep=shaped)] * 2
    outs += [out(width, keep=shaped), out(hidden, keep=shaped)]
    outs += [out(width), out(width)]
    outs += [(whole((8, width), False), shaped((8, width), F32))]
    outs += [(whole((1, hidden), False), shaped((1, hidden), F32))]
    return call(
        functools.partial(middle_kernel, size, block, width),
        (pieces,),
        [limits],
        ins,
        outs,
        [context, kept(embedded)] + [kept(c) for c in cotangents] + [kept(w) for w in weights],
        scratch=[pltpu.VMEM((tokens, hidden), BF16)],
        flops=4 * pieces * tokens * width * (width + 2 * hidden),
        moved=4 * width * hidden + pieces * tokens * (30 * width + 4 * hidden),
        room=38,
    )


def last_kernel(layout, spot, *refs):
    rows, spans = layout
    cut = rows[0] * spans[0]
    length = QUAD * spans[1]
    triple, mixed, embedded, weight, lines, early, sort = refs[:7]
    pieces_out = refs[7:10]
    tail_away, tail_mine, pile, short_pile = refs[10:]
    width = mixed.shape[-1]
    step = pl.program_id(0)

    @pl.when(step == 0)
    def _():
        pile[length:, :] = jnp.zeros((pile.shape[0] - length, width), F32)
        pile[length + 8 : length + 8 + early.shape[0], :] = early[...]

    total = mixed[0].astype(F32) + right_product(triple[0], weight[...])
    unit, scale = norm_stats(embedded[0])
    grad = norm_back(total, unit, scale, lines[0:1])
    put_piece(pieces_out, grad.astype(BF16))
    place = spot[0] ^ step
    short_rows = pl.ds(pl.multiple_of(place * spans[0], spans[0]), spans[0])
    long_rows = pl.ds(pl.multiple_of(place * spans[1], spans[1]), spans[1])
    short_pile[short_rows, :] = jnp.sum(grad[:cut].reshape(rows[0], spans[0], width), axis=0)
    pile[long_rows, :] = jnp.sum(grad[cut:].reshape(rows[1], spans[1], width), axis=0)
    found = [
        column_sum(total * unit),
        column_sum(total),
        column_sum(triple[0, :, :width].astype(F32)),
        column_sum(triple[0, :, 2 * width :].astype(F32)),
    ]
    for at, item in enumerate(found):
        pile[length + at : length + at + 1, :] += item

    @pl.when(step == QUAD - 1)
    def _():
        shorter = short_pile.shape[0]
        pile[:shorter, :] += short_pile[...]
        tail = right_product(sort[...], pile[...].astype(BF16)).astype(BF16)
        tail_away[...] = tail[: width // 2]
        tail_mine[...] = tail[width // 2 :]


def last(layout, spot, grad, mixed, embedded, weight, lines, early, sort):
    rows, spans = layout
    pieces, tokens, width = mixed.shape
    row = pl.BlockSpec((1, tokens, width), lambda i, s: (i, 0, 0))
    triple = pl.BlockSpec((1, tokens, 3 * width), lambda i, s: (i, 0, 0))
    ins = [triple, row, row] + [whole(a.shape) for a in (weight, lines, early, sort)]
    outs = piece_outs(tokens, width)
    depth = QUAD * spans[1] + LANES
    half = (width // 2, depth)
    outs += [(whole(half, False), shaped(half, BF16))] * 2
    return call(
        functools.partial(last_kernel, layout),
        (pieces,),
        [spot],
        ins,
        outs,
        [grad, kept(mixed), kept(embedded), weight, lines, early, sort],
        scratch=[pltpu.VMEM((depth, width), F32), pltpu.VMEM((QUAD * spans[0], width), F32)],
        flops=6 * pieces * tokens * width * width,
        moved=6 * width * width + pieces * tokens * 18 * width,
        room=22,
    )


def settle_kernel(size, spot, own, near, far, short_out, long_out):
    tokens = own.shape[0]
    for k, (part, start) in enumerate(((own, 0), (near, 0), (far, 0), (near, tokens))):

        @pl.when(pl.program_id(0) == k)
        def _(part=part, start=start):
            short_out[0] = part[start : start + size]
            long_out[0] = part[start + size : start + tokens]


def settle(size, spot, own, near, far):
    tokens, width = own.shape
    sizes = (size, tokens - size)
    outs = [
        (
            pl.BlockSpec((1, n, width), lambda i, s: (s[0] ^ i, 0, 0)),
            shaped((QUAD, n, width), own.dtype),
        )
        for n in sizes
    ]
    return call(
        functools.partial(settle_kernel, size),
        (QUAD,),
        [spot],
        [whole(p.shape) for p in (own, near, far)],
        outs,
        [kept(p) for p in (own, near, far)],
        moved=4 * QUAD * tokens * width,
        room=8,
    )


def hand_on(near, far):
    return partner(jnp.concatenate([near, far[near.shape[0] :]]), "wide", 1)


def cut_pieces(short, long, spot):
    parts = [a.reshape(QUAD, -1, a.shape[-1]) for a in (short, long)]
    return {k: jnp.concatenate([pick(a, spot ^ k, 0) for a in parts]) for k in range(QUAD)}


def swap_pieces(pieces):
    return {k: partner(piece, "wide", k) if k else piece for k, piece in pieces.items()}


def on_device(
    short_input,
    long_input,
    short_cotangent,
    long_cotangent,
    short_live,
    long_live,
    position_table,
    embed_gain,
    embed_shift,
    project_in,
    query_bias,
    value_bias,
    project_out,
    output_bias,
    middle_gain,
    middle_shift,
    expand_weight,
    expand_bias,
    shrink_weight,
    shrink_bias,
    final_gain,
    final_shift,
):
    width = short_input.shape[-1]
    spot = lax.axis_index("wide") % QUAD
    group = lax.axis_index("wide") // QUAD * lax.axis_size("narrow") + lax.axis_index("narrow")
    rows = (short_input.shape[1] // QUAD, long_input.shape[1] // QUAD)
    spans = (short_input.shape[2], long_input.shape[2])
    layout = (rows, spans)
    size = rows[0] * spans[0]
    assert size == rows[1] * spans[1]
    spots = jnp.asarray(spot, jnp.int32).reshape(1)
    alive = [
        jnp.clip(pick(live, group, 0) - spot * r, 0, r) * s
        for live, r, s in zip((short_live, long_live), rows, spans)
    ]
    core = lax.axis_index("wide") % 2
    limits = jnp.stack([alive[0], size + alive[1], core]).astype(jnp.int32)
    sort = sort_rows(width)
    middle_steps, middle_back, narrow_steps = halving_steps()
    up, down = middle_steps + narrow_steps, middle_back + narrow_steps
    flat = lambda a: a.reshape(-1, a.shape[-1])

    def weight_grad(a, b):
        return left_product(flat(a), flat(b)).astype(BF16)

    cuts = cut_pieces(short_input, long_input, spot)
    pieces = swap_pieces(cuts)
    vectors = (embed_gain, embed_shift, query_bias, value_bias, output_bias)
    vectors += (middle_gain, middle_shift, shrink_bias, final_gain, final_shift)
    vectors = jnp.concatenate((after(vectors[0], *cuts.values()),) + vectors[1:])
    lines = vectors.astype(F32).reshape(-1, width)
    cot_cuts = cut_pieces(after(short_cotangent, *cuts.values()), after(long_cotangent, *cuts.values()), spot)
    embedded, base_away, base_mine, triple, context = front(
        layout,
        spots,
        [pieces[k] for k in range(QUAD)],
        position_table,
        after(lines, *cot_cuts.values()),
        project_in,
        sort,
    )
    cot_cuts = {k: after(c, pieces[2], pieces[3]) for k, c in cot_cuts.items()}
    cot_pieces = swap_pieces(cot_cuts)
    cotangents = [cot_pieces[k] for k in range(QUAD)]
    weights = (sort, lines, project_out, expand_weight, expand_bias.astype(F32)[None], shrink_weight)
    hidden = expand_weight.shape[1]
    hidden_block = hidden // lax.axis_size("wide")
    found = middle_part(size, hidden_block, limits, context, embedded, cotangents, weights)
    own_result, near_result, far_result = found[:3]
    far_result = partner(far_result, "wide", 2)
    middle_away, middle_mine, context_away, context_mine, active_away, active_mine = found[3:9]
    grad_low, expanded_low, mixed_low, context_grad, sums, expand_sums = found[9:]
    turned = middle_back[:1] + narrow_steps + middle_back[1:]
    hidden_dims = middle_back + narrow_steps[::-1]

    def weight_sum(a, b, arrived):
        return (left_product(flat(a), flat(b)) + arrived.astype(F32)).astype(BF16)

    if hidden_block % LANES:
        partial = jnp.concatenate([weight_grad(active_away, grad_low), weight_grad(active_mine, grad_low)])
        partial = partial.reshape(-1, 2, hidden_block, width)
        away, mine = [pick(partial, side, 1).reshape(-1, width) for side in (1 - core, core)]
        arrived = partner(away, "wide", 1)
        expand_away = weight_grad(middle_away, after(expanded_low, away))
        shrink_total = (mine.astype(F32) + arrived.astype(F32)).astype(BF16)
    else:
        away = weight_grad(active_away, grad_low)
        arrived = partner(away, "wide", 1)
        expand_away = weight_grad(middle_away, after(expanded_low, away))
        shrink_total = weight_sum(active_mine, after(grad_low, expand_away), arrived)
    shrink_chain = Chain(hidden_dims, turned).sides([([shrink_total], 0, width)])
    expand_arrived = partner(expand_away, "wide", 1)
    out_away = weight_grad(context_away, after(mixed_low, shrink_chain.away))
    out_arrived = partner(out_away, "wide", 1)
    expand_total = weight_sum(middle_mine, after(expanded_low, out_away), expand_arrived)
    out_total = weight_sum(context_mine, after(mixed_low, expand_total), out_arrived)
    cut = (hidden + width) * 3 // 5
    expand_chains = [
        Chain(up, up).sides([([expand_total], 0, cut)]),
        Chain(up, down).sides([([expand_total], cut, hidden - cut), ([out_total], 0, width)]),
    ]
    grads = attend_back(layout, 1, triple, after(context_grad, far_result, *sends(expand_chains)), ())
    near_result = hand_on(near_result, after(far_result, grads[0]))
    sent = shrink_chain.step(grads[0])
    grads = attend_back(layout, 0, triple, after(context_grad, sent, grads[0]), grads)
    sent = [c.step(grads[0]) for c in expand_chains]
    triple_grad = after(grads[0], near_result, *sent)
    in_away = weight_grad(base_away, triple_grad)
    in_arrived = partner(in_away, "wide", 1)
    in_mine = lax.optimization_barrier(weight_grad(base_mine, after(triple_grad, in_away)))
    cut = 3 * width // 2
    in_chains = [
        Chain(up, order).sides([([in_mine, in_arrived], at * cut, cut)]) for at, order in enumerate((up, down))
    ]
    sent = shrink_chain.step(*sends(in_chains))
    spread = expand_sums.reshape(width, hidden // width).T
    early = jnp.concatenate([sums[:6], spread])
    found = last(
        layout, spots, triple_grad, after(mixed_low, sent), embedded, project_in, lines, early, sort
    )
    own_grad, near_grad, far_grad, tail_away, tail_mine = found
    tail_away = after(tail_away, *[c.arrived for c in in_chains])
    tail_arrived = partner(tail_away, "wide", 1)
    for chain in expand_chains + in_chains:
        chain.wait(tail_away)
    sent = [c.step() for c in in_chains]
    far_grad = partner(after(far_grad, *sent), "wide", 2)
    for chain in expand_chains:
        chain.wait(*sent)
    expand_chain = join(expand_chains)
    tail_total = (tail_mine.astype(F32) + after(tail_arrived, expand_chain.away).astype(F32)).astype(BF16)
    tail_chain = Chain(up, turned).sides([([tail_total], 0, tail_total.shape[-1])])
    sent = shrink_chain.step(tail_chain.away)
    outputs = settle(size, spots, after(own_result, sent), near_result, far_result)
    for chain in in_chains:
        chain.wait(*outputs)
    in_chain = join(in_chains)
    sent = tail_chain.step(in_chain.away)
    sent = expand_chain.step(sent)
    sent = in_chain.step(sent)
    sent = tail_chain.step(sent)
    expand_chain.wait(sent)
    expand_grad = expand_chain.finish()
    sent = tail_chain.step(expand_grad)
    in_chain.wait(sent)
    in_grad = in_chain.finish()
    near_grad = hand_on(near_grad, after(far_grad, in_grad))
    tail_chain.wait(near_grad)
    shrink_chain.wait(near_grad)
    tail_sum = tail_chain.finish()
    shrink_grad = shrink_chain.finish()
    input_grads = settle(size, spots, own_grad, near_grad, far_grad)
    length = QUAD * spans[1]
    position_grad = tail_sum[:, :length].T
    order = (0, 1, 2, 3, 8, 9, 10, 11, 12, 13)
    vector = [tail_sum[:, length + i] for i in order]
    expand_bias_grad = tail_sum[:, length + 14 : length + 14 + hidden // width].reshape(-1)
    expand_grad, out_grad = expand_grad[:, :hidden], expand_grad[:, hidden:]
    return (
        outputs[0].reshape(short_input.shape),
        outputs[1].reshape(long_input.shape),
        input_grads[0].reshape(short_input.shape),
        input_grads[1].reshape(long_input.shape),
        position_grad,
        vector[0],
        vector[1],
        in_grad,
        vector[2],
        vector[3],
        out_grad,
        vector[9],
        vector[7],
        vector[8],
        expand_grad,
        expand_bias_grad,
        shrink_grad,
        vector[6],
        vector[4],
        vector[5],
    )


def solution(mesh):
    rows = P(BOTH, None, None, None)
    vector, matrix = P(BOTH), P(BOTH, None)
    in_specs = (rows,) * 4 + (P(),) * 18
    out_specs = (rows,) * 4 + (
        P(None, BOTH),
        vector,
        vector,
        matrix,
        vector,
        vector,
        matrix,
        vector,
        vector,
        vector,
        matrix,
        vector,
        matrix,
        vector,
        vector,
        vector,
    )
    return jax.shard_map(on_device, mesh=mesh, in_specs=in_specs, out_specs=out_specs, check_vma=False)
```

```python
import functools

import jax
import jax.numpy as jnp
from jax import lax
from jax.experimental import pallas as pl
from jax.experimental.pallas import tpu as pltpu
from jax.sharding import PartitionSpec as P

HEAD_DIM = 64
LANES = 128
EPS = 1e-05
QUAD = 4
F32 = jnp.float32
BF16 = jnp.bfloat16
BOTH = ("wide", "narrow")
ROOT_HALF = 0.7071067811865476
PHI_ZERO = 0.3989422804014327


def partner(shard, axis, flip):
    return lax.ppermute(shard, axis, [(i, i ^ flip) for i in range(lax.axis_size(axis))])


def pick(tensor, index, axis):
    return lax.dynamic_index_in_dim(tensor, index, axis, keepdims=False)


def after(value, *first):
    return lax.optimization_barrier((value,) + first)[0]


def halving_steps():
    wide_bits, narrow_bits = [lax.axis_size(axis).bit_length() - 1 for axis in BOTH]
    middle = [("wide", b) for b in range(1, wide_bits)]
    narrow = [("narrow", b) for b in range(narrow_bits)]
    return middle, middle[::-1], narrow


def bit_of(index, bit):
    return index // 2**bit % 2


def sort_rows(width):
    middle, _, narrow = halving_steps()
    each = width // (lax.axis_size("wide") * lax.axis_size("narrow"))
    natural = jnp.arange(width)
    index = {"narrow": natural // each % lax.axis_size("narrow")}
    index["wide"] = natural // each // lax.axis_size("narrow")
    goes = (bit_of(index["wide"], 0) == lax.axis_index("wide") % 2).astype(jnp.int32)
    for axis, bit in middle + narrow:
        goes = 2 * goes + bit_of(index[axis], bit)
    goes = goes * each + natural % each
    return (goes[None, :] == natural[:, None]).astype(BF16)


class Chain:
    def __init__(self, dims, steps):
        self.dims, self.steps = list(dims), list(steps)
        self.away = self.mine = self.arrived = None

    def sides(self, groups):
        axis, bit = self.steps.pop(0)
        place = self.dims.index((axis, bit))
        here = bit_of(lax.axis_index(axis), bit)
        lead = (2,) * len(self.dims)
        self.dims.pop(place)
        found = []
        for side in (1 - here, here):
            parts = []
            for arrays, start, size in groups:
                total = 0.0
                for array in arrays:
                    array = array.reshape(lead + (-1, array.shape[-1]))
                    sizes = list(array.shape[:-1]) + [size]
                    sizes[place] = 1
                    starts = [jnp.int32(0)] * (len(sizes) - 1) + [jnp.int32(start)]
                    starts[place] = jnp.asarray(side, jnp.int32)
                    total = total + lax.dynamic_slice(array, starts, sizes).astype(F32)
                parts.append(jnp.squeeze(total.astype(BF16), place))
            found.append(parts[0] if len(parts) == 1 else jnp.concatenate(parts, axis=-1))
        self.away, self.mine = found
        self.arrived = partner(self.away, axis, 2**bit)
        return self

    def wait(self, *first):
        self.arrived = after(self.arrived, *first)

    def step(self, *first):
        if first:
            self.wait(*first)
        return self.sides([([self.mine, self.arrived], 0, self.mine.shape[-1])]).away

    def finish(self, *cuts):
        while self.steps:
            self.step()
        edges = (0,) + cuts + (self.mine.shape[-1],)
        parts = [
            self.mine[..., a:b].astype(F32) + self.arrived[..., a:b].astype(F32)
            for a, b in zip(edges[:-1], edges[1:])
        ]
        return parts if cuts else parts[0]


def sends(chains):
    return [chain.away for chain in chains]


def join(chains):
    groups = [([c.mine, c.arrived], 0, c.mine.shape[-1]) for c in chains]
    return Chain(chains[0].dims, chains[0].steps).sides(groups)


def left_product(a, b):
    return lax.dot_general(a, b, (((0,), (0,)), ((), ())), preferred_element_type=F32)


def right_product(a, b):
    return lax.dot_general(a, b, (((1,), (1,)), ((), ())), preferred_element_type=F32)


def product(a, b):
    return jnp.dot(a, b, preferred_element_type=F32)


def norm_stats(values):
    row_mean = jnp.mean(values, axis=-1, keepdims=True)
    centered = values - row_mean
    spread = jnp.mean(centered * centered, axis=-1, keepdims=True)
    scale = lax.rsqrt(spread + EPS)
    return centered * scale, scale


def norm_back(grad, unit, scale, gain):
    inner = grad * gain
    first = jnp.mean(inner, axis=-1, keepdims=True)
    second = jnp.mean(inner * unit, axis=-1, keepdims=True)
    return scale * (inner - first - unit * second)


def piece_outs(tokens, width):
    one = pl.BlockSpec((tokens, width), lambda i, s: (0, 0))
    two = pl.BlockSpec((tokens, width), lambda i, s: (jnp.maximum(i - 2, 0), 0))
    return [
        (one, pltpu.HBM((tokens, width), BF16)),
        (one, pltpu.HBM((tokens, width), BF16)),
        (two, pltpu.HBM((2 * tokens, width), BF16)),
    ]


def put_piece(outs, value):
    step = pl.program_id(0)
    for at, out in enumerate(outs):

        @pl.when((step == at) | (step == at + 1) if at == 2 else step == at)
        def _(out=out):
            out[...] = value


def column_sum(values):
    return jnp.sum(values, axis=0, keepdims=True)


def call(kernel, grid, scalars, ins, outs, arrays, scratch=(), aliases=None, flops=0, moved=0, room=16):
    return pl.pallas_call(
        kernel,
        grid_spec=pltpu.PrefetchScalarGridSpec(
            num_scalar_prefetch=len(scalars),
            grid=grid,
            in_specs=ins,
            out_specs=[o[0] for o in outs],
            scratch_shapes=list(scratch),
        ),
        out_shape=[o[1] for o in outs],
        input_output_aliases=aliases or {},
        compiler_params=pltpu.CompilerParams(vmem_limit_bytes=room << 20),
        cost_estimate=pl.CostEstimate(flops=flops, bytes_accessed=moved, transcendentals=0),
    )(*scalars, *arrays)


def whole(shape, once=True):
    mode = {"pipeline_mode": pl.Buffered(1)} if once else {}
    return pl.BlockSpec(shape, lambda *_: (0,) * len(shape), **mode)


def shaped(shape, dtype):
    return jax.ShapeDtypeStruct(shape, dtype)


def kept(array):
    return pltpu.with_memory_space_constraint(array, pltpu.HBM)


def head_rows(block, rows, span, at):
    part = block[:, at * span : (at + 1) * span, :] if rows > 1 else block
    return part.reshape(-1, part.shape[-1])


def first_head(shape):
    return lax.broadcasted_iota(jnp.int32, shape, len(shape) - 1) < HEAD_DIM


def pair_rows(ref, layout, bucket):
    rows, span = layout[0][bucket], layout[1][bucket]
    found = []
    for start in range(0, ref.shape[-1], LANES):
        block = ref[:, :, start : start + LANES]
        found += [head_rows(block, rows, span, at) for at in range(rows)]
    return found


def attend_rows(queries, keys, values):
    first = first_head(queries[0].shape)
    nothing, ones = jnp.zeros_like(queries[0]), jnp.ones_like(queries[0])
    scores = []
    for query, key in zip(queries, keys):
        query = query * jnp.asarray(HEAD_DIM**-0.5, BF16)
        scores.append(right_product(jnp.where(first, query, nothing), key))
        scores.append(right_product(jnp.where(first, nothing, query), key))
    count = queries[0].shape[0]
    scores = jnp.concatenate(scores)
    powers = jnp.exp(scores - jnp.max(scores, axis=-1, keepdims=True)).astype(BF16)
    results = []
    for at, value in enumerate(values):
        left = product(powers[2 * at * count : (2 * at + 1) * count], jnp.where(first, value, ones))
        right = product(powers[(2 * at + 1) * count : (2 * at + 2) * count], jnp.where(first, ones, value))
        left = left * (1.0 / left[:, HEAD_DIM : HEAD_DIM + 1])
        right = right * (1.0 / right[:, :1])
        results.append(jnp.where(first, left, right).astype(BF16))
    return results


def attend_part(layout, triple, out):
    rows, spans = layout
    size = rows[0] * spans[0]
    width = out.shape[-1]
    columns = 2 * LANES

    @pl.loop(0, width // columns)
    def _(step):
        for bucket in range(2):
            count, span = rows[bucket], spans[bucket]
            tokens = slice(bucket * size, (bucket + 1) * size)
            lists = []
            for which in range(3):
                place = pl.multiple_of(which * width + step * columns, LANES)
                block = triple[:, tokens, pl.ds(place, columns)]
                lists.append(pair_rows(block, layout, bucket))
            for start in range(0, len(lists[0]), count):
                results = attend_rows(*[part[start : start + count] for part in lists])
                place = pl.multiple_of(step * columns + start // count * LANES, LANES)
                for at, result in enumerate(results):
                    first = bucket * size + at * span
                    result = result.reshape(QUAD, span, LANES)
                    out[:, first : first + span, pl.ds(place, LANES)] = result


def attend_flops(layout, pairs):
    rows, spans = layout
    return sum(2 * pairs * r * (QUAD * s) ** 2 * 2 * HEAD_DIM * 2 for r, s in zip(rows, spans))


def front_kernel(layout, spot, *refs):
    rows, spans = layout
    cut = rows[0] * spans[0]
    data, (table, lines, weight, sort) = refs[:QUAD], refs[QUAD : QUAD + 4]
    embedded_out, away_out, mine_out, triple_out, context_out, pieces = refs[QUAD + 4 :]
    gain, shift, query_bias, value_bias = [lines[at : at + 1] for at in range(4)]
    width = table.shape[-1]
    for at in range(QUAD):
        pieces[at] = data[at][...]

    @pl.loop(0, QUAD)
    def _(at):
        tokens = pieces[at].astype(F32)
        parts = [tokens[:cut], tokens[cut:]]
        for which, span in enumerate(spans):
            place = pl.multiple_of((spot[0] ^ at) * span, span)
            place = table[pl.ds(place, span), :].astype(F32)
            part = parts[which].reshape(rows[which], span, width) + place[None]
            parts[which] = part.reshape(-1, width)
        embedded = jnp.concatenate(parts)
        embedded_out[at] = embedded
        unit, _ = norm_stats(embedded)
        base_low = (unit * gain + shift).astype(BF16)
        sorted_low = right_product(base_low, sort[...]).astype(BF16)
        away_out[at] = sorted_low[:, : width // 2]
        mine_out[at] = sorted_low[:, width // 2 :]
        for which, bias in enumerate((query_bias, 0.0, value_bias)):
            part = slice(which * width, (which + 1) * width)
            triple_out[at, :, part] = (product(base_low, weight[:, part]) + bias).astype(BF16)

    attend_part(layout, triple_out, context_out)


def front(layout, spot, data, table, lines, weight, sort):
    rows, spans = layout
    tokens, width = data[0].shape
    triple = weight.shape[1]
    ins = [whole((tokens, width))] * QUAD
    ins += [whole(a.shape) for a in (table, lines, weight, sort)]
    outs = []
    for n, dtype in ((width, F32), (width // 2, BF16), (width // 2, BF16), (triple, BF16), (width, BF16)):
        outs.append((whole((QUAD, tokens, n)), pltpu.HBM((QUAD, tokens, n), dtype)))
    outs[-1] = (outs[-1][0], shaped((QUAD, tokens, width), BF16))
    return call(
        functools.partial(front_kernel, layout),
        (1,),
        [spot],
        ins,
        outs,
        [kept(d) for d in data] + [kept(table), lines, kept(weight), kept(sort)],
        scratch=[pltpu.VMEM((QUAD, tokens, width), BF16)],
        flops=2 * QUAD * tokens * width * triple + attend_flops(layout, width // LANES),
        moved=2 * width * triple + QUAD * tokens * (8 * width + 2 * triple),
        room=30,
    )


def attend_back_rows(queries, keys, values, grads):
    first = first_head(queries[0].shape)
    nothing = jnp.zeros_like(queries[0])
    scaled = [query * jnp.asarray(HEAD_DIM**-0.5, BF16) for query in queries]
    scores, prob_grads = [], []
    for query, key, value, grad in zip(scaled, keys, values, grads):
        scores.append(right_product(key, jnp.where(first, query, nothing)))
        scores.append(right_product(key, jnp.where(first, nothing, query)))
        prob_grads.append(right_product(value, jnp.where(first, grad, nothing)))
        prob_grads.append(right_product(value, jnp.where(first, nothing, grad)))
    scores = jnp.concatenate(scores, axis=1)
    prob_grad = jnp.concatenate(prob_grads, axis=1)
    powers = jnp.exp(scores - jnp.max(scores, axis=0, keepdims=True))
    soft = powers * (1.0 / jnp.sum(powers, axis=0, keepdims=True))
    inner = jnp.sum(soft * prob_grad, axis=0, keepdims=True)
    score_grad = (soft * (prob_grad - inner)).astype(BF16)
    weights = soft.astype(BF16)
    count = queries[0].shape[0]
    results = []
    for at, (query, key, grad) in enumerate(zip(scaled, keys, grads)):
        two = []
        for head in range(2):
            part = slice((2 * at + head) * count, (2 * at + head + 1) * count)
            two.append(
                (
                    left_product(score_grad[:, part], key) * HEAD_DIM**-0.5,
                    product(score_grad[:, part], query),
                    product(weights[:, part], grad),
                )
            )
        results.append([jnp.where(first, a, b).astype(BF16) for a, b in zip(*two)])
    return results


def attend_back_kernel(layout, bucket, group, query, key, value, grad, *rest):
    count, span = layout[0][bucket], layout[1][bucket]
    out = rest[-1]
    width = out.shape[-1] // 3
    step = pl.program_id(0) * query.shape[-1]
    lists = [pair_rows(ref, layout, bucket) for ref in (query, key, value, grad)]
    for start in range(0, len(lists[0]), group):
        results = attend_back_rows(*[part[start : start + group] for part in lists])
        for at, three in enumerate(results):
            pair, row = divmod(start + at, count)
            for which, result in enumerate(three):
                place = pl.multiple_of(which * width + step + pair * LANES, LANES)
                rows = slice(row * span, (row + 1) * span)
                out[:, rows, pl.ds(place, LANES)] = result.reshape(QUAD, span, LANES)


def attend_back(layout, bucket, triple, grad, earlier):
    rows, spans = layout
    tokens, width = triple.shape[1], triple.shape[2] // 3
    pairs = width // LANES
    size = rows[0] * spans[0]
    steps = 2 if rows[bucket] > 1 else 6
    columns = width // steps
    group = rows[bucket]
    ins = [
        pl.BlockSpec((QUAD, size, columns), lambda p, w=w: (0, bucket, w * steps + p)) for w in range(3)
    ]
    ins += [pl.BlockSpec((QUAD, size, columns), lambda p: (0, bucket, p))]
    ins += [pl.BlockSpec(memory_space=pl.ANY)] * len(earlier)
    outs = [
        (
            pl.BlockSpec((QUAD, size, 3 * width), lambda p: (0, bucket, 0)),
            shaped((QUAD, tokens, 3 * width), BF16),
        )
    ]
    return call(
        functools.partial(attend_back_kernel, layout, bucket, group),
        (steps,),
        [],
        ins,
        outs,
        [kept(triple)] * 3 + [kept(grad)] + list(earlier),
        aliases={4 + i: i for i in range(len(earlier))},
        flops=int(2.5 * attend_flops((rows[bucket : bucket + 1], spans[bucket : bucket + 1]), pairs)),
        room=18,
        moved=QUAD * size * width * 14,
    )


def alive_rows(limits, size, count):
    at = lax.broadcasted_iota(jnp.int32, (count, 1), 0)
    short = (at < limits[0]).astype(F32)
    long = (at >= size).astype(F32) * (at < limits[1]).astype(F32)
    return short + long


def hidden_parts(core, hidden, block, chunk):
    if block % LANES:
        return [([(start, chunk)], start) for start in range(0, hidden, chunk)]
    places = []
    for half in range(2):
        side = core if half else 1 - core
        places += [
            (pl.multiple_of((2 * at + side) * block, LANES), block) for at in range(hidden // block // 2)
        ]
    each = chunk // block
    return [(places[at : at + each], at * block) for at in range(0, len(places), each)]


def columns_of(ref, places, lead=()):
    return jnp.concatenate([ref[lead + (slice(None), pl.ds(*p))] for p in places], axis=-1)


def rows_of(ref, places):
    return jnp.concatenate([ref[pl.ds(*p), :] for p in places], axis=0)


def middle_rows(size, block, chunk, limits, *refs):
    (context, embedded, *cotangents) = refs[: 2 + QUAD]
    refs = refs[2 + QUAD :]
    (sort, lines, project_out, expand, expand_bias, shrink) = refs[:6]
    outputs, refs = refs[6:9], refs[9:]
    (middle_away, middle_mine, context_away, context_mine, active_away, active_mine) = refs[:6]
    (grad_low_out, expanded_out, mixed_low_out, context_out, sums, bias_sums, slopes) = refs[6:]
    embed_gain, embed_shift = lines[0:1], lines[1:2]
    output_bias, middle_gain, middle_shift, shrink_bias, gain, shift = [
        lines[at : at + 1] for at in range(4, 10)
    ]
    width = context.shape[-1]
    half = width // 2
    hidden = expand.shape[1]
    parts = hidden_parts(limits[2], hidden, block, chunk)
    unit, _ = norm_stats(embedded[0])
    inner = unit * embed_gain + embed_shift
    inner = inner + (product(context[0], project_out[...]) + output_bias)
    sorted_low = right_product(context[0], sort[...]).astype(BF16)
    context_away[0] = sorted_low[:, :half]
    context_mine[0] = sorted_low[:, half:]
    inner_unit, inner_scale = norm_stats(inner)
    middle = inner_unit * middle_gain + middle_shift
    middle_low = middle.astype(BF16)
    sorted_low = right_product(middle_low, sort[...]).astype(BF16)
    middle_away[0] = sorted_low[:, :half]
    middle_mine[0] = sorted_low[:, half:]
    total = middle + shrink_bias
    for places, start in parts:
        part = slice(start, start + chunk)
        expanded = product(middle_low, columns_of(expand, places)) + columns_of(expand_bias, places)
        below = 0.5 + 0.5 * lax.erf(expanded * ROOT_HALF)
        active = (expanded * below).astype(BF16)
        if start < hidden // 2:
            active_away[0, :, part] = active
        else:
            active_mine[0, :, start - hidden // 2 : start - hidden // 2 + chunk] = active
        density = jnp.exp(expanded * expanded * -0.5) * PHI_ZERO
        slopes[:, part] = (below + expanded * density).astype(BF16)
        total = total + product(active, rows_of(shrink, places))
    unit, scale = norm_stats(total)
    alive = alive_rows(limits, size, unit.shape[0])
    result = unit * gain + shift
    put_piece(outputs, (result * alive).astype(BF16))
    cotangent = cotangents[0][...]
    for k in range(1, QUAD):
        cotangent = jnp.where(pl.program_id(0) == k, cotangents[k][...], cotangent)
    upstream = cotangent.astype(F32) * alive
    grad = norm_back(upstream, unit, scale, gain)
    grad_low = grad.astype(BF16)
    grad_low_out[0] = grad_low
    found = [column_sum(upstream * unit), column_sum(upstream), column_sum(grad_low.astype(F32))]
    total = grad
    for places, start in parts:
        part = slice(start, start + chunk)
        raised = right_product(grad_low, rows_of(shrink, places)) * slopes[:, part].astype(F32)
        low = raised.astype(BF16)
        sums_low = column_sum(low.astype(F32))
        done = 0
        for place in places:
            expanded_out[0, :, pl.ds(*place)] = low[:, done : done + place[1]]
            bias_sums[:, pl.ds(*place)] += sums_low[:, done : done + place[1]]
            done += place[1]
        total = total + right_product(low, columns_of(expand, places))
    mixed = norm_back(total, inner_unit, inner_scale, middle_gain)
    mixed_low = mixed.astype(BF16)
    mixed_low_out[0] = mixed_low
    context_out[0] = right_product(mixed_low, project_out[...]).astype(BF16)
    found += [column_sum(total * inner_unit), column_sum(total), column_sum(mixed_low.astype(F32))]
    for at, value in enumerate(found):
        sums[at : at + 1, :] += value


def middle_kernel(size, block, chunk, limits, *refs):
    sums, bias_sums = refs[-3:-1]

    @pl.when(pl.program_id(0) == 0)
    def _():
        sums[...] = jnp.zeros_like(sums)
        bias_sums[...] = jnp.zeros_like(bias_sums)

    middle_rows(size, block, chunk, limits, *refs)


def middle_part(size, block, limits, context, embedded, cotangents, weights):
    pieces, tokens, width = context.shape
    hidden = weights[3].shape[1]

    def out(columns, dtype=BF16, keep=pltpu.HBM):
        blocked = pl.BlockSpec((1, tokens, columns), lambda i, s: (i, 0, 0))
        return blocked, keep((pieces, tokens, columns), dtype)

    ins = [out(width)[0]] * 2 + [whole(c.shape) for c in cotangents] + [whole(w.shape) for w in weights]
    outs = piece_outs(tokens, width)
    outs += [out(width // 2)] * 4 + [out(hidden // 2, keep=shaped)] * 2
    outs += [out(width, keep=shaped), out(hidden, keep=shaped)]
    outs += [out(width), out(width)]
    outs += [(whole((8, width), False), shaped((8, width), F32))]
    outs += [(whole((1, hidden), False), shaped((1, hidden), F32))]
    return call(
        functools.partial(middle_kernel, size, block, width),
        (pieces,),
        [limits],
        ins,
        outs,
        [context, kept(embedded)] + [kept(c) for c in cotangents] + [kept(w) for w in weights],
        scratch=[pltpu.VMEM((tokens, hidden), BF16)],
        flops=4 * pieces * tokens * width * (width + 2 * hidden),
        moved=4 * width * hidden + pieces * tokens * (30 * width + 4 * hidden),
        room=38,
    )


def last_kernel(layout, spot, *refs):
    rows, spans = layout
    cut = rows[0] * spans[0]
    length = QUAD * spans[1]
    triple, mixed, embedded, weight, lines, early, sort = refs[:7]
    pieces_out = refs[7:10]
    tail_away, tail_mine, pile, short_pile = refs[10:]
    width = mixed.shape[-1]
    step = pl.program_id(0)

    @pl.when(step == 0)
    def _():
        pile[length:, :] = jnp.zeros((pile.shape[0] - length, width), F32)
        pile[length + 8 : length + 8 + early.shape[0], :] = early[...]

    total = mixed[0].astype(F32) + right_product(triple[0], weight[...])
    unit, scale = norm_stats(embedded[0])
    grad = norm_back(total, unit, scale, lines[0:1])
    put_piece(pieces_out, grad.astype(BF16))
    place = spot[0] ^ step
    short_rows = pl.ds(pl.multiple_of(place * spans[0], spans[0]), spans[0])
    long_rows = pl.ds(pl.multiple_of(place * spans[1], spans[1]), spans[1])
    short_pile[short_rows, :] = jnp.sum(grad[:cut].reshape(rows[0], spans[0], width), axis=0)
    pile[long_rows, :] = jnp.sum(grad[cut:].reshape(rows[1], spans[1], width), axis=0)
    found = [
        column_sum(total * unit),
        column_sum(total),
        column_sum(triple[0, :, :width].astype(F32)),
        column_sum(triple[0, :, 2 * width :].astype(F32)),
    ]
    for at, item in enumerate(found):
        pile[length + at : length + at + 1, :] += item

    @pl.when(step == QUAD - 1)
    def _():
        shorter = short_pile.shape[0]
        pile[:shorter, :] += short_pile[...]
        tail = right_product(sort[...], pile[...].astype(BF16)).astype(BF16)
        tail_away[...] = tail[: width // 2]
        tail_mine[...] = tail[width // 2 :]


def last(layout, spot, grad, mixed, embedded, weight, lines, early, sort):
    rows, spans = layout
    pieces, tokens, width = mixed.shape
    row = pl.BlockSpec((1, tokens, width), lambda i, s: (i, 0, 0))
    triple = pl.BlockSpec((1, tokens, 3 * width), lambda i, s: (i, 0, 0))
    ins = [triple, row, row] + [whole(a.shape) for a in (weight, lines, early, sort)]
    outs = piece_outs(tokens, width)
    depth = QUAD * spans[1] + LANES
    half = (width // 2, depth)
    outs += [(whole(half, False), shaped(half, BF16))] * 2
    return call(
        functools.partial(last_kernel, layout),
        (pieces,),
        [spot],
        ins,
        outs,
        [grad, kept(mixed), kept(embedded), weight, lines, early, sort],
        scratch=[pltpu.VMEM((depth, width), F32), pltpu.VMEM((QUAD * spans[0], width), F32)],
        flops=6 * pieces * tokens * width * width,
        moved=6 * width * width + pieces * tokens * 18 * width,
        room=22,
    )


def settle_kernel(size, spot, own, near, far, short_out, long_out):
    tokens = own.shape[0]
    for k, (part, start) in enumerate(((own, 0), (near, 0), (far, 0), (near, tokens))):
        short_out[spot[0] ^ k] = part[start : start + size]
        long_out[spot[0] ^ k] = part[start + size : start + tokens]


def settle(size, spot, own, near, far):
    tokens, width = own.shape
    sizes = (size, tokens - size)
    outs = [(whole((QUAD, n, width)), shaped((QUAD, n, width), own.dtype)) for n in sizes]
    return call(
        functools.partial(settle_kernel, size),
        (1,),
        [spot],
        [whole(p.shape) for p in (own, near, far)],
        outs,
        [kept(p) for p in (own, near, far)],
        moved=4 * QUAD * tokens * width,
        room=8,
    )


def hand_on(near, far):
    return partner(jnp.concatenate([near, far[near.shape[0] :]]), "wide", 1)


def cut_pieces(short, long, spot):
    parts = [a.reshape(QUAD, -1, a.shape[-1]) for a in (short, long)]
    return {k: jnp.concatenate([pick(a, spot ^ k, 0) for a in parts]) for k in range(QUAD)}


def swap_pieces(pieces):
    return {k: partner(piece, "wide", k) if k else piece for k, piece in pieces.items()}


def on_device(
    short_input,
    long_input,
    short_cotangent,
    long_cotangent,
    short_live,
    long_live,
    position_table,
    embed_gain,
    embed_shift,
    project_in,
    query_bias,
    value_bias,
    project_out,
    output_bias,
    middle_gain,
    middle_shift,
    expand_weight,
    expand_bias,
    shrink_weight,
    shrink_bias,
    final_gain,
    final_shift,
):
    width = short_input.shape[-1]
    spot = lax.axis_index("wide") % QUAD
    group = lax.axis_index("wide") // QUAD * lax.axis_size("narrow") + lax.axis_index("narrow")
    rows = (short_input.shape[1] // QUAD, long_input.shape[1] // QUAD)
    spans = (short_input.shape[2], long_input.shape[2])
    layout = (rows, spans)
    size = rows[0] * spans[0]
    assert size == rows[1] * spans[1]
    spots = jnp.asarray(spot, jnp.int32).reshape(1)
    alive = [
        jnp.clip(pick(live, group, 0) - spot * r, 0, r) * s
        for live, r, s in zip((short_live, long_live), rows, spans)
    ]
    core = lax.axis_index("wide") % 2
    limits = jnp.stack([alive[0], size + alive[1], core]).astype(jnp.int32)
    sort = sort_rows(width)
    middle_steps, middle_back, narrow_steps = halving_steps()
    up, down = middle_steps + narrow_steps, middle_back + narrow_steps
    flat = lambda a: a.reshape(-1, a.shape[-1])

    def weight_grad(a, b):
        return left_product(flat(a), flat(b)).astype(BF16)

    cuts = cut_pieces(short_input, long_input, spot)
    pieces = swap_pieces(cuts)
    vectors = (embed_gain, embed_shift, query_bias, value_bias, output_bias)
    vectors += (middle_gain, middle_shift, shrink_bias, final_gain, final_shift)
    vectors = jnp.concatenate((after(vectors[0], *cuts.values()),) + vectors[1:])
    lines = vectors.astype(F32).reshape(-1, width)
    cot_cuts = cut_pieces(after(short_cotangent, *cuts.values()), after(long_cotangent, *cuts.values()), spot)
    embedded, base_away, base_mine, triple, context = front(
        layout,
        spots,
        [pieces[k] for k in range(QUAD)],
        position_table,
        after(lines, *cot_cuts.values()),
        project_in,
        sort,
    )
    cot_cuts = {k: after(c, pieces[2], pieces[3]) for k, c in cot_cuts.items()}
    cot_pieces = swap_pieces(cot_cuts)
    cotangents = [cot_pieces[k] for k in range(QUAD)]
    weights = (sort, lines, project_out, expand_weight, expand_bias.astype(F32)[None], shrink_weight)
    hidden = expand_weight.shape[1]
    hidden_block = hidden // lax.axis_size("wide")
    found = middle_part(size, hidden_block, limits, context, embedded, cotangents, weights)
    own_result, near_result, far_result = found[:3]
    far_result = partner(far_result, "wide", 2)
    middle_away, middle_mine, context_away, context_mine, active_away, active_mine = found[3:9]
    grad_low, expanded_low, mixed_low, context_grad, sums, expand_sums = found[9:]
    turned = middle_back[:1] + narrow_steps + middle_back[1:]
    hidden_dims = middle_back + narrow_steps[::-1]

    def weight_sum(a, b, arrived):
        return (left_product(flat(a), flat(b)) + arrived.astype(F32)).astype(BF16)

    if hidden_block % LANES:
        partial = jnp.concatenate([weight_grad(active_away, grad_low), weight_grad(active_mine, grad_low)])
        partial = partial.reshape(-1, 2, hidden_block, width)
        away, mine = [pick(partial, side, 1).reshape(-1, width) for side in (1 - core, core)]
        arrived = partner(away, "wide", 1)
        expand_away = weight_grad(middle_away, after(expanded_low, away))
        shrink_total = (mine.astype(F32) + arrived.astype(F32)).astype(BF16)
    else:
        away = weight_grad(active_away, grad_low)
        arrived = partner(away, "wide", 1)
        expand_away = weight_grad(middle_away, after(expanded_low, away))
        shrink_total = weight_sum(active_mine, after(grad_low, expand_away), arrived)
    shrink_chain = Chain(hidden_dims, turned).sides([([shrink_total], 0, width)])
    expand_arrived = partner(expand_away, "wide", 1)
    out_away = weight_grad(context_away, after(mixed_low, shrink_chain.away))
    out_arrived = partner(out_away, "wide", 1)
    expand_total = weight_sum(middle_mine, after(expanded_low, out_away), expand_arrived)
    out_total = weight_sum(context_mine, after(mixed_low, expand_total), out_arrived)
    cut = (hidden + width) * 3 // 5
    expand_chains = [
        Chain(up, up).sides([([expand_total], 0, cut)]),
        Chain(up, down).sides([([expand_total], cut, hidden - cut), ([out_total], 0, width)]),
    ]
    grads = attend_back(layout, 1, triple, after(context_grad, far_result, *sends(expand_chains)), ())
    near_result = hand_on(near_result, after(far_result, grads[0]))
    sent = shrink_chain.step(grads[0])
    grads = attend_back(layout, 0, triple, after(context_grad, sent, grads[0]), grads)
    sent = [c.step(grads[0]) for c in expand_chains]
    sent.append(shrink_chain.step(*sent))
    triple_grad = after(grads[0], near_result, *sent)
    in_away = weight_grad(base_away, triple_grad)
    in_arrived = partner(in_away, "wide", 1)
    in_mine = lax.optimization_barrier(weight_grad(base_mine, after(triple_grad, in_away)))
    cut = 3 * width // 2
    in_chains = [
        Chain(up, order).sides([([in_mine, in_arrived], at * cut, cut)]) for at, order in enumerate((up, down))
    ]
    spread = expand_sums.reshape(width, hidden // width).T
    early = jnp.concatenate([sums[:6], spread])
    found = last(
        layout, spots, triple_grad, after(mixed_low, *sends(in_chains)), embedded, project_in, lines, early, sort
    )
    own_grad, near_grad, far_grad, tail_away, tail_mine = found
    tail_away = after(tail_away, *[c.arrived for c in in_chains])
    tail_arrived = partner(tail_away, "wide", 1)
    for chain in expand_chains + in_chains:
        chain.wait(tail_away)
    sent = [c.step() for c in in_chains]
    far_grad = partner(after(far_grad, *sent), "wide", 2)
    for chain in expand_chains:
        chain.wait(*sent)
    expand_chain = join(expand_chains)
    tail_total = (tail_mine.astype(F32) + after(tail_arrived, expand_chain.away).astype(F32)).astype(BF16)
    tail_chain = Chain(up, turned).sides([([tail_total], 0, tail_total.shape[-1])])
    sent = shrink_chain.step(tail_chain.away)
    outputs = settle(size, spots, after(own_result, sent), near_result, far_result)
    for chain in in_chains:
        chain.wait(*outputs)
    in_chain = join(in_chains)
    sent = tail_chain.step(in_chain.away)
    sent = expand_chain.step(sent)
    sent = tail_chain.step(sent)
    sent = in_chain.step(sent)
    expand_chain.wait(sent)
    expand_grad, out_grad = expand_chain.finish(hidden)
    near_grad = hand_on(near_grad, after(far_grad, expand_grad))
    sent = tail_chain.step(near_grad)
    input_grads = settle(size, spots, after(own_grad, sent), near_grad, far_grad)
    in_chain.wait(*input_grads)
    in_grad = in_chain.finish()
    shrink_chain.wait(in_grad)
    shrink_grad = shrink_chain.finish()
    tail_sum = tail_chain.finish()
    length = QUAD * spans[1]
    position_grad = tail_sum[:, :length].T
    order = (0, 1, 2, 3, 8, 9, 10, 11, 12, 13)
    vector = [tail_sum[:, length + i] for i in order]
    expand_bias_grad = tail_sum[:, length + 14 : length + 14 + hidden // width].reshape(-1)
    return (
        outputs[0].reshape(short_input.shape),
        outputs[1].reshape(long_input.shape),
        input_grads[0].reshape(short_input.shape),
        input_grads[1].reshape(long_input.shape),
        position_grad,
        vector[0],
        vector[1],
        in_grad,
        vector[2],
        vector[3],
        out_grad,
        vector[9],
        vector[7],
        vector[8],
        expand_grad,
        expand_bias_grad,
        shrink_grad,
        vector[6],
        vector[4],
        vector[5],
    )


def solution(mesh):
    rows = P(BOTH, None, None, None)
    vector, matrix = P(BOTH), P(BOTH, None)
    in_specs = (rows,) * 4 + (P(),) * 18
    out_specs = (rows,) * 4 + (
        P(None, BOTH),
        vector,
        vector,
        matrix,
        vector,
        vector,
        matrix,
        vector,
        vector,
        vector,
        matrix,
        vector,
        matrix,
        vector,
        vector,
        vector,
    )
    return jax.shard_map(on_device, mesh=mesh, in_specs=in_specs, out_specs=out_specs, check_vma=False)
```

```python
import functools

import jax
import jax.numpy as jnp
from jax import lax
from jax.experimental import pallas as pl
from jax.experimental.pallas import tpu as pltpu
from jax.sharding import PartitionSpec as P

HEAD_DIM = 64
LANES = 128
EPS = 1e-05
QUAD = 4
F32 = jnp.float32
BF16 = jnp.bfloat16
BOTH = ("wide", "narrow")
ROOT_HALF = 0.7071067811865476
PHI_ZERO = 0.3989422804014327


def partner(shard, axis, flip):
    return lax.ppermute(shard, axis, [(i, i ^ flip) for i in range(lax.axis_size(axis))])


def pick(tensor, index, axis):
    return lax.dynamic_index_in_dim(tensor, index, axis, keepdims=False)


def after(value, *first):
    return lax.optimization_barrier((value,) + first)[0]


def halving_steps():
    wide_bits, narrow_bits = [lax.axis_size(axis).bit_length() - 1 for axis in BOTH]
    middle = [("wide", b) for b in range(1, wide_bits)]
    narrow = [("narrow", b) for b in range(narrow_bits)]
    return middle, middle[::-1], narrow


def bit_of(index, bit):
    return index // 2**bit % 2


def sort_rows(width):
    middle, _, narrow = halving_steps()
    each = width // (lax.axis_size("wide") * lax.axis_size("narrow"))
    natural = jnp.arange(width)
    index = {"narrow": natural // each % lax.axis_size("narrow")}
    index["wide"] = natural // each // lax.axis_size("narrow")
    goes = (bit_of(index["wide"], 0) == lax.axis_index("wide") % 2).astype(jnp.int32)
    for axis, bit in middle + narrow:
        goes = 2 * goes + bit_of(index[axis], bit)
    goes = goes * each + natural % each
    return (goes[None, :] == natural[:, None]).astype(BF16)


class Chain:
    def __init__(self, dims, steps):
        self.dims, self.steps = list(dims), list(steps)
        self.away = self.mine = self.arrived = None

    def sides(self, groups):
        axis, bit = self.steps.pop(0)
        place = self.dims.index((axis, bit))
        here = bit_of(lax.axis_index(axis), bit)
        lead = (2,) * len(self.dims)
        self.dims.pop(place)
        found = []
        for side in (1 - here, here):
            parts = []
            for arrays, start, size in groups:
                total = 0.0
                for array in arrays:
                    array = array.reshape(lead + (-1, array.shape[-1]))
                    sizes = list(array.shape[:-1]) + [size]
                    sizes[place] = 1
                    starts = [jnp.int32(0)] * (len(sizes) - 1) + [jnp.int32(start)]
                    starts[place] = jnp.asarray(side, jnp.int32)
                    total = total + lax.dynamic_slice(array, starts, sizes).astype(F32)
                parts.append(jnp.squeeze(total.astype(BF16), place))
            found.append(parts[0] if len(parts) == 1 else jnp.concatenate(parts, axis=-1))
        self.away, self.mine = found
        self.arrived = partner(self.away, axis, 2**bit)
        return self

    def wait(self, *first):
        self.arrived = after(self.arrived, *first)

    def step(self, *first):
        if first:
            self.wait(*first)
        return self.sides([([self.mine, self.arrived], 0, self.mine.shape[-1])]).away

    def finish(self, *cuts):
        while self.steps:
            self.step()
        edges = (0,) + cuts + (self.mine.shape[-1],)
        parts = [
            self.mine[..., a:b].astype(F32) + self.arrived[..., a:b].astype(F32)
            for a, b in zip(edges[:-1], edges[1:])
        ]
        return parts if cuts else parts[0]


def sends(chains):
    return [chain.away for chain in chains]


def join(chains):
    groups = [([c.mine, c.arrived], 0, c.mine.shape[-1]) for c in chains]
    return Chain(chains[0].dims, chains[0].steps).sides(groups)


def left_product(a, b):
    return lax.dot_general(a, b, (((0,), (0,)), ((), ())), preferred_element_type=F32)


def right_product(a, b):
    return lax.dot_general(a, b, (((1,), (1,)), ((), ())), preferred_element_type=F32)


def product(a, b):
    return jnp.dot(a, b, preferred_element_type=F32)


def norm_stats(values):
    row_mean = jnp.mean(values, axis=-1, keepdims=True)
    centered = values - row_mean
    spread = jnp.mean(centered * centered, axis=-1, keepdims=True)
    scale = lax.rsqrt(spread + EPS)
    return centered * scale, scale


def norm_back(grad, unit, scale, gain):
    inner = grad * gain
    first = jnp.mean(inner, axis=-1, keepdims=True)
    second = jnp.mean(inner * unit, axis=-1, keepdims=True)
    return scale * (inner - first - unit * second)


def piece_outs(tokens, width):
    one = pl.BlockSpec((tokens, width), lambda i, s: (0, 0))
    two = pl.BlockSpec((tokens, width), lambda i, s: (jnp.maximum(i - 2, 0), 0))
    return [
        (one, pltpu.HBM((tokens, width), BF16)),
        (one, pltpu.HBM((tokens, width), BF16)),
        (two, pltpu.HBM((2 * tokens, width), BF16)),
    ]


def put_piece(outs, value):
    step = pl.program_id(0)
    for at, out in enumerate(outs):

        @pl.when((step == at) | (step == at + 1) if at == 2 else step == at)
        def _(out=out):
            out[...] = value


def column_sum(values):
    return jnp.sum(values, axis=0, keepdims=True)


def call(kernel, grid, scalars, ins, outs, arrays, scratch=(), aliases=None, flops=0, moved=0, room=16):
    return pl.pallas_call(
        kernel,
        grid_spec=pltpu.PrefetchScalarGridSpec(
            num_scalar_prefetch=len(scalars),
            grid=grid,
            in_specs=ins,
            out_specs=[o[0] for o in outs],
            scratch_shapes=list(scratch),
        ),
        out_shape=[o[1] for o in outs],
        input_output_aliases=aliases or {},
        compiler_params=pltpu.CompilerParams(vmem_limit_bytes=room << 20),
        cost_estimate=pl.CostEstimate(flops=flops, bytes_accessed=moved, transcendentals=0),
    )(*scalars, *arrays)


def whole(shape, once=True):
    mode = {"pipeline_mode": pl.Buffered(1)} if once else {}
    return pl.BlockSpec(shape, lambda *_: (0,) * len(shape), **mode)


def shaped(shape, dtype):
    return jax.ShapeDtypeStruct(shape, dtype)


def kept(array):
    return pltpu.with_memory_space_constraint(array, pltpu.HBM)


def head_rows(block, rows, span, at):
    part = block[:, at * span : (at + 1) * span, :] if rows > 1 else block
    return part.reshape(-1, part.shape[-1])


def first_head(shape):
    return lax.broadcasted_iota(jnp.int32, shape, len(shape) - 1) < HEAD_DIM


def pair_rows(ref, layout, bucket):
    rows, span = layout[0][bucket], layout[1][bucket]
    found = []
    for start in range(0, ref.shape[-1], LANES):
        block = ref[:, :, start : start + LANES]
        found += [head_rows(block, rows, span, at) for at in range(rows)]
    return found


def attend_rows(queries, keys, values):
    first = first_head(queries[0].shape)
    nothing, ones = jnp.zeros_like(queries[0]), jnp.ones_like(queries[0])
    scores = []
    for query, key in zip(queries, keys):
        query = query * jnp.asarray(HEAD_DIM**-0.5, BF16)
        scores.append(right_product(jnp.where(first, query, nothing), key))
        scores.append(right_product(jnp.where(first, nothing, query), key))
    count = queries[0].shape[0]
    scores = jnp.concatenate(scores)
    powers = jnp.exp(scores - jnp.max(scores, axis=-1, keepdims=True)).astype(BF16)
    results = []
    for at, value in enumerate(values):
        left = product(powers[2 * at * count : (2 * at + 1) * count], jnp.where(first, value, ones))
        right = product(powers[(2 * at + 1) * count : (2 * at + 2) * count], jnp.where(first, ones, value))
        left = left * (1.0 / left[:, HEAD_DIM : HEAD_DIM + 1])
        right = right * (1.0 / right[:, :1])
        results.append(jnp.where(first, left, right).astype(BF16))
    return results


def attend_part(layout, triple, out):
    rows, spans = layout
    size = rows[0] * spans[0]
    width = out.shape[-1]
    columns = 2 * LANES

    @pl.loop(0, width // columns)
    def _(step):
        for bucket in range(2):
            count, span = rows[bucket], spans[bucket]
            tokens = slice(bucket * size, (bucket + 1) * size)
            lists = []
            for which in range(3):
                place = pl.multiple_of(which * width + step * columns, LANES)
                block = triple[:, tokens, pl.ds(place, columns)]
                lists.append(pair_rows(block, layout, bucket))
            for start in range(0, len(lists[0]), count):
                results = attend_rows(*[part[start : start + count] for part in lists])
                place = pl.multiple_of(step * columns + start // count * LANES, LANES)
                for at, result in enumerate(results):
                    first = bucket * size + at * span
                    result = result.reshape(QUAD, span, LANES)
                    out[:, first : first + span, pl.ds(place, LANES)] = result


def attend_flops(layout, pairs):
    rows, spans = layout
    return sum(2 * pairs * r * (QUAD * s) ** 2 * 2 * HEAD_DIM * 2 for r, s in zip(rows, spans))


def front_kernel(layout, spot, *refs):
    rows, spans = layout
    cut = rows[0] * spans[0]
    data, (table, lines, weight, sort) = refs[:QUAD], refs[QUAD : QUAD + 4]
    embedded_out, away_out, mine_out, triple_out, context_out, pieces = refs[QUAD + 4 :]
    gain, shift, query_bias, value_bias = [lines[at : at + 1] for at in range(4)]
    width = table.shape[-1]
    for at in range(QUAD):
        pieces[at] = data[at][...]

    def project(at):
        tokens = pieces[at].astype(F32)
        parts = [tokens[:cut], tokens[cut:]]
        for which, span in enumerate(spans):
            place = pl.multiple_of((spot[0] ^ at) * span, span)
            place = table[pl.ds(place, span), :].astype(F32)
            part = parts[which].reshape(rows[which], span, width) + place[None]
            parts[which] = part.reshape(-1, width)
        embedded = jnp.concatenate(parts)
        embedded_out[at] = embedded
        unit, _ = norm_stats(embedded)
        base_low = (unit * gain + shift).astype(BF16)
        sorted_low = right_product(base_low, sort[...]).astype(BF16)
        away_out[at] = sorted_low[:, : width // 2]
        mine_out[at] = sorted_low[:, width // 2 :]
        for which, bias in enumerate((query_bias, 0.0, value_bias)):
            part = slice(which * width, (which + 1) * width)
            triple_out[at, :, part] = (product(base_low, weight[:, part]) + bias).astype(BF16)

    @pl.loop(0, QUAD, step=2)
    def _(at):
        project(at)
        project(at + 1)

    attend_part(layout, triple_out, context_out)


def front(layout, spot, data, table, lines, weight, sort):
    rows, spans = layout
    tokens, width = data[0].shape
    triple = weight.shape[1]
    ins = [whole((tokens, width))] * QUAD
    ins += [whole(a.shape) for a in (table, lines, weight, sort)]
    outs = []
    for n, dtype in ((width, F32), (width // 2, BF16), (width // 2, BF16), (triple, BF16), (width, BF16)):
        outs.append((whole((QUAD, tokens, n)), pltpu.HBM((QUAD, tokens, n), dtype)))
    outs[-1] = (outs[-1][0], shaped((QUAD, tokens, width), BF16))
    return call(
        functools.partial(front_kernel, layout),
        (1,),
        [spot],
        ins,
        outs,
        [kept(d) for d in data] + [table, lines, weight, sort],
        scratch=[pltpu.VMEM((QUAD, tokens, width), BF16)],
        flops=2 * QUAD * tokens * width * triple + attend_flops(layout, width // LANES),
        moved=2 * width * triple + QUAD * tokens * (8 * width + 2 * triple),
        room=30,
    )


def attend_back_rows(queries, keys, values, grads):
    first = first_head(queries[0].shape)
    nothing = jnp.zeros_like(queries[0])
    scaled = [query * jnp.asarray(HEAD_DIM**-0.5, BF16) for query in queries]
    scores, prob_grads = [], []
    for query, key, value, grad in zip(scaled, keys, values, grads):
        scores.append(right_product(key, jnp.where(first, query, nothing)))
        scores.append(right_product(key, jnp.where(first, nothing, query)))
        prob_grads.append(right_product(value, jnp.where(first, grad, nothing)))
        prob_grads.append(right_product(value, jnp.where(first, nothing, grad)))
    scores = jnp.concatenate(scores, axis=1)
    prob_grad = jnp.concatenate(prob_grads, axis=1)
    powers = jnp.exp(scores - jnp.max(scores, axis=0, keepdims=True))
    soft = powers * (1.0 / jnp.sum(powers, axis=0, keepdims=True))
    inner = jnp.sum(soft * prob_grad, axis=0, keepdims=True)
    score_grad = (soft * (prob_grad - inner)).astype(BF16)
    weights = soft.astype(BF16)
    count = queries[0].shape[0]
    results = []
    for at, (query, key, grad) in enumerate(zip(scaled, keys, grads)):
        two = []
        for head in range(2):
            part = slice((2 * at + head) * count, (2 * at + head + 1) * count)
            two.append(
                (
                    left_product(score_grad[:, part], key) * HEAD_DIM**-0.5,
                    product(score_grad[:, part], query),
                    product(weights[:, part], grad),
                )
            )
        results.append([jnp.where(first, a, b).astype(BF16) for a, b in zip(*two)])
    return results


def attend_back_kernel(layout, bucket, group, query, key, value, grad, *rest):
    count, span = layout[0][bucket], layout[1][bucket]
    out = rest[-1]
    width = out.shape[-1] // 3
    step = pl.program_id(0) * query.shape[-1]
    lists = [pair_rows(ref, layout, bucket) for ref in (query, key, value, grad)]
    for start in range(0, len(lists[0]), group):
        results = attend_back_rows(*[part[start : start + group] for part in lists])
        for at, three in enumerate(results):
            pair, row = divmod(start + at, count)
            for which, result in enumerate(three):
                place = pl.multiple_of(which * width + step + pair * LANES, LANES)
                rows = slice(row * span, (row + 1) * span)
                out[:, rows, pl.ds(place, LANES)] = result.reshape(QUAD, span, LANES)


def attend_back(layout, bucket, triple, grad, earlier):
    rows, spans = layout
    tokens, width = triple.shape[1], triple.shape[2] // 3
    pairs = width // LANES
    size = rows[0] * spans[0]
    steps = 2 if rows[bucket] > 1 else 6
    columns = width // steps
    group = rows[bucket]
    ins = [
        pl.BlockSpec((QUAD, size, columns), lambda p, w=w: (0, bucket, w * steps + p)) for w in range(3)
    ]
    ins += [pl.BlockSpec((QUAD, size, columns), lambda p: (0, bucket, p))]
    ins += [pl.BlockSpec(memory_space=pl.ANY)] * len(earlier)
    outs = [
        (
            pl.BlockSpec((QUAD, size, 3 * width), lambda p: (0, bucket, 0)),
            shaped((QUAD, tokens, 3 * width), BF16),
        )
    ]
    return call(
        functools.partial(attend_back_kernel, layout, bucket, group),
        (steps,),
        [],
        ins,
        outs,
        [kept(triple)] * 3 + [kept(grad)] + list(earlier),
        aliases={4 + i: i for i in range(len(earlier))},
        flops=int(2.5 * attend_flops((rows[bucket : bucket + 1], spans[bucket : bucket + 1]), pairs)),
        room=18,
        moved=QUAD * size * width * 14,
    )


def alive_rows(limits, size, count):
    at = lax.broadcasted_iota(jnp.int32, (count, 1), 0)
    short = (at < limits[0]).astype(F32)
    long = (at >= size).astype(F32) * (at < limits[1]).astype(F32)
    return short + long


def hidden_parts(core, hidden, block, chunk):
    if block % LANES:
        return [([(start, chunk)], start) for start in range(0, hidden, chunk)]
    places = []
    for half in range(2):
        side = core if half else 1 - core
        places += [
            (pl.multiple_of((2 * at + side) * block, LANES), block) for at in range(hidden // block // 2)
        ]
    each = chunk // block
    return [(places[at : at + each], at * block) for at in range(0, len(places), each)]


def columns_of(ref, places, lead=()):
    return jnp.concatenate([ref[lead + (slice(None), pl.ds(*p))] for p in places], axis=-1)


def rows_of(ref, places):
    return jnp.concatenate([ref[pl.ds(*p), :] for p in places], axis=0)


def middle_rows(size, block, chunk, limits, *refs):
    (context, embedded, *cotangents) = refs[: 2 + QUAD]
    refs = refs[2 + QUAD :]
    (sort, lines, project_out, expand, expand_bias, shrink) = refs[:6]
    outputs, refs = refs[6:9], refs[9:]
    (middle_away, middle_mine, context_away, context_mine, active_away, active_mine) = refs[:6]
    (grad_low_out, expanded_out, mixed_low_out, context_out, sums, bias_sums, slopes) = refs[6:]
    embed_gain, embed_shift = lines[0:1], lines[1:2]
    output_bias, middle_gain, middle_shift, shrink_bias, gain, shift = [
        lines[at : at + 1] for at in range(4, 10)
    ]
    width = context.shape[-1]
    half = width // 2
    hidden = expand.shape[1]
    parts = hidden_parts(limits[2], hidden, block, chunk)
    unit, _ = norm_stats(embedded[0])
    inner = unit * embed_gain + embed_shift
    inner = inner + (product(context[0], project_out[...]) + output_bias)
    sorted_low = right_product(context[0], sort[...]).astype(BF16)
    context_away[0] = sorted_low[:, :half]
    context_mine[0] = sorted_low[:, half:]
    inner_unit, inner_scale = norm_stats(inner)
    middle = inner_unit * middle_gain + middle_shift
    middle_low = middle.astype(BF16)
    sorted_low = right_product(middle_low, sort[...]).astype(BF16)
    middle_away[0] = sorted_low[:, :half]
    middle_mine[0] = sorted_low[:, half:]
    total = middle + shrink_bias
    for places, start in parts:
        part = slice(start, start + chunk)
        expanded = product(middle_low, columns_of(expand, places)) + columns_of(expand_bias, places)
        below = 0.5 + 0.5 * lax.erf(expanded * ROOT_HALF)
        active = (expanded * below).astype(BF16)
        if start < hidden // 2:
            active_away[0, :, part] = active
        else:
            active_mine[0, :, start - hidden // 2 : start - hidden // 2 + chunk] = active
        density = jnp.exp(expanded * expanded * -0.5) * PHI_ZERO
        slopes[:, part] = (below + expanded * density).astype(BF16)
        total = total + product(active, rows_of(shrink, places))
    unit, scale = norm_stats(total)
    alive = alive_rows(limits, size, unit.shape[0])
    result = unit * gain + shift
    put_piece(outputs, (result * alive).astype(BF16))
    cotangent = cotangents[0][...]
    for k in range(1, QUAD):
        cotangent = jnp.where(pl.program_id(0) == k, cotangents[k][...], cotangent)
    upstream = cotangent.astype(F32) * alive
    grad = norm_back(upstream, unit, scale, gain)
    grad_low = grad.astype(BF16)
    grad_low_out[0] = grad_low
    found = [column_sum(upstream * unit), column_sum(upstream), column_sum(grad_low.astype(F32))]
    total = grad
    for places, start in parts:
        part = slice(start, start + chunk)
        raised = right_product(grad_low, rows_of(shrink, places)) * slopes[:, part].astype(F32)
        low = raised.astype(BF16)
        sums_low = column_sum(low.astype(F32))
        done = 0
        for place in places:
            expanded_out[0, :, pl.ds(*place)] = low[:, done : done + place[1]]
            bias_sums[:, pl.ds(*place)] += sums_low[:, done : done + place[1]]
            done += place[1]
        total = total + right_product(low, columns_of(expand, places))
    mixed = norm_back(total, inner_unit, inner_scale, middle_gain)
    mixed_low = mixed.astype(BF16)
    mixed_low_out[0] = mixed_low
    context_out[0] = right_product(mixed_low, project_out[...]).astype(BF16)
    found += [column_sum(total * inner_unit), column_sum(total), column_sum(mixed_low.astype(F32))]
    for at, value in enumerate(found):
        sums[at : at + 1, :] += value


def middle_kernel(size, block, chunk, limits, *refs):
    sums, bias_sums = refs[-3:-1]

    @pl.when(pl.program_id(0) == 0)
    def _():
        sums[...] = jnp.zeros_like(sums)
        bias_sums[...] = jnp.zeros_like(bias_sums)

    middle_rows(size, block, chunk, limits, *refs)


def middle_part(size, block, limits, context, embedded, cotangents, weights):
    pieces, tokens, width = context.shape
    hidden = weights[3].shape[1]

    def out(columns, dtype=BF16, keep=pltpu.HBM):
        blocked = pl.BlockSpec((1, tokens, columns), lambda i, s: (i, 0, 0))
        return blocked, keep((pieces, tokens, columns), dtype)

    ins = [out(width)[0]] * 2 + [whole(c.shape) for c in cotangents] + [whole(w.shape) for w in weights]
    outs = piece_outs(tokens, width)
    outs += [out(width // 2)] * 4 + [out(hidden // 2, keep=shaped)] * 2
    outs += [out(width, keep=shaped), out(hidden, keep=shaped)]
    outs += [out(width), out(width)]
    outs += [(whole((8, width), False), shaped((8, width), F32))]
    outs += [(whole((1, hidden), False), shaped((1, hidden), F32))]
    return call(
        functools.partial(middle_kernel, size, block, width),
        (pieces,),
        [limits],
        ins,
        outs,
        [context, kept(embedded)] + [kept(c) for c in cotangents] + [kept(w) for w in weights],
        scratch=[pltpu.VMEM((tokens, hidden), BF16)],
        flops=4 * pieces * tokens * width * (width + 2 * hidden),
        moved=4 * width * hidden + pieces * tokens * (30 * width + 4 * hidden),
        room=38,
    )


def last_kernel(layout, spot, *refs):
    rows, spans = layout
    cut = rows[0] * spans[0]
    length = QUAD * spans[1]
    triple, mixed, embedded, weight, lines, early, sort = refs[:7]
    pieces_out = refs[7:10]
    tail_away, tail_mine, pile, short_pile = refs[10:]
    width = mixed.shape[-1]
    step = pl.program_id(0)

    @pl.when(step == 0)
    def _():
        pile[length:, :] = jnp.zeros((pile.shape[0] - length, width), F32)
        pile[length + 8 : length + 8 + early.shape[0], :] = early[...]

    total = mixed[0].astype(F32) + right_product(triple[0], weight[...])
    unit, scale = norm_stats(embedded[0])
    grad = norm_back(total, unit, scale, lines[0:1])
    put_piece(pieces_out, grad.astype(BF16))
    place = spot[0] ^ step
    short_rows = pl.ds(pl.multiple_of(place * spans[0], spans[0]), spans[0])
    long_rows = pl.ds(pl.multiple_of(place * spans[1], spans[1]), spans[1])
    short_pile[short_rows, :] = jnp.sum(grad[:cut].reshape(rows[0], spans[0], width), axis=0)
    pile[long_rows, :] = jnp.sum(grad[cut:].reshape(rows[1], spans[1], width), axis=0)
    found = [
        column_sum(total * unit),
        column_sum(total),
        column_sum(triple[0, :, :width].astype(F32)),
        column_sum(triple[0, :, 2 * width :].astype(F32)),
    ]
    for at, item in enumerate(found):
        pile[length + at : length + at + 1, :] += item

    @pl.when(step == QUAD - 1)
    def _():
        shorter = short_pile.shape[0]
        pile[:shorter, :] += short_pile[...]
        tail = right_product(sort[...], pile[...].astype(BF16)).astype(BF16)
        tail_away[...] = tail[: width // 2]
        tail_mine[...] = tail[width // 2 :]


def last(layout, spot, grad, mixed, embedded, weight, lines, early, sort):
    rows, spans = layout
    pieces, tokens, width = mixed.shape
    row = pl.BlockSpec((1, tokens, width), lambda i, s: (i, 0, 0))
    triple = pl.BlockSpec((1, tokens, 3 * width), lambda i, s: (i, 0, 0))
    ins = [triple, row, row] + [whole(a.shape) for a in (weight, lines, early, sort)]
    outs = piece_outs(tokens, width)
    depth = QUAD * spans[1] + LANES
    half = (width // 2, depth)
    outs += [(whole(half, False), shaped(half, BF16))] * 2
    return call(
        functools.partial(last_kernel, layout),
        (pieces,),
        [spot],
        ins,
        outs,
        [grad, kept(mixed), kept(embedded), weight, lines, early, sort],
        scratch=[pltpu.VMEM((depth, width), F32), pltpu.VMEM((QUAD * spans[0], width), F32)],
        flops=6 * pieces * tokens * width * width,
        moved=6 * width * width + pieces * tokens * 18 * width,
        room=22,
    )


def settle_kernel(size, spot, own, near, far, short_out, long_out):
    tokens = own.shape[0]
    for k, (part, start) in enumerate(((own, 0), (near, 0), (far, 0), (near, tokens))):
        short_out[spot[0] ^ k] = part[start : start + size]
        long_out[spot[0] ^ k] = part[start + size : start + tokens]


def settle(size, spot, own, near, far):
    tokens, width = own.shape
    sizes = (size, tokens - size)
    outs = [(whole((QUAD, n, width)), shaped((QUAD, n, width), own.dtype)) for n in sizes]
    return call(
        functools.partial(settle_kernel, size),
        (1,),
        [spot],
        [whole(p.shape) for p in (own, near, far)],
        outs,
        [kept(p) for p in (own, near, far)],
        moved=4 * QUAD * tokens * width,
        room=8,
    )


def hand_on(near, far):
    return partner(jnp.concatenate([near, far[near.shape[0] :]]), "wide", 1)


def cut_pieces(short, long, spot):
    parts = [a.reshape(QUAD, -1, a.shape[-1]) for a in (short, long)]
    return {k: jnp.concatenate([pick(a, spot ^ k, 0) for a in parts]) for k in range(QUAD)}


def swap_pieces(pieces):
    return {k: partner(piece, "wide", k) if k else piece for k, piece in pieces.items()}


def on_device(
    short_input,
    long_input,
    short_cotangent,
    long_cotangent,
    short_live,
    long_live,
    position_table,
    embed_gain,
    embed_shift,
    project_in,
    query_bias,
    value_bias,
    project_out,
    output_bias,
    middle_gain,
    middle_shift,
    expand_weight,
    expand_bias,
    shrink_weight,
    shrink_bias,
    final_gain,
    final_shift,
):
    width = short_input.shape[-1]
    spot = lax.axis_index("wide") % QUAD
    group = lax.axis_index("wide") // QUAD * lax.axis_size("narrow") + lax.axis_index("narrow")
    rows = (short_input.shape[1] // QUAD, long_input.shape[1] // QUAD)
    spans = (short_input.shape[2], long_input.shape[2])
    layout = (rows, spans)
    size = rows[0] * spans[0]
    assert size == rows[1] * spans[1]
    spots = jnp.asarray(spot, jnp.int32).reshape(1)
    alive = [
        jnp.clip(pick(live, group, 0) - spot * r, 0, r) * s
        for live, r, s in zip((short_live, long_live), rows, spans)
    ]
    core = lax.axis_index("wide") % 2
    limits = jnp.stack([alive[0], size + alive[1], core]).astype(jnp.int32)
    sort = sort_rows(width)
    middle_steps, middle_back, narrow_steps = halving_steps()
    up, down = middle_steps + narrow_steps, middle_back + narrow_steps
    flat = lambda a: a.reshape(-1, a.shape[-1])

    def weight_grad(a, b):
        return left_product(flat(a), flat(b)).astype(BF16)

    cuts = cut_pieces(short_input, long_input, spot)
    pieces = swap_pieces(cuts)
    vectors = (embed_gain, embed_shift, query_bias, value_bias, output_bias)
    vectors += (middle_gain, middle_shift, shrink_bias, final_gain, final_shift)
    vectors = jnp.concatenate((after(vectors[0], *cuts.values()),) + vectors[1:])
    lines = vectors.astype(F32).reshape(-1, width)
    cot_cuts = cut_pieces(after(short_cotangent, *cuts.values()), after(long_cotangent, *cuts.values()), spot)
    embedded, base_away, base_mine, triple, context = front(
        layout,
        spots,
        [pieces[k] for k in range(QUAD)],
        position_table,
        after(lines, *cot_cuts.values()),
        project_in,
        sort,
    )
    cot_cuts = {k: after(c, pieces[2], pieces[3]) for k, c in cot_cuts.items()}
    cot_pieces = swap_pieces(cot_cuts)
    cotangents = [cot_pieces[k] for k in range(QUAD)]
    weights = (sort, lines, project_out, expand_weight, expand_bias.astype(F32)[None], shrink_weight)
    hidden = expand_weight.shape[1]
    hidden_block = hidden // lax.axis_size("wide")
    found = middle_part(size, hidden_block, limits, context, embedded, cotangents, weights)
    own_result, near_result, far_result = found[:3]
    far_result = partner(far_result, "wide", 2)
    middle_away, middle_mine, context_away, context_mine, active_away, active_mine = found[3:9]
    grad_low, expanded_low, mixed_low, context_grad, sums, expand_sums = found[9:]
    turned = middle_back[:1] + narrow_steps + middle_back[1:]
    hidden_dims = middle_back + narrow_steps[::-1]

    def weight_sum(a, b, arrived):
        return (left_product(flat(a), flat(b)) + arrived.astype(F32)).astype(BF16)

    if hidden_block % LANES:
        partial = jnp.concatenate([weight_grad(active_away, grad_low), weight_grad(active_mine, grad_low)])
        partial = partial.reshape(-1, 2, hidden_block, width)
        away, mine = [pick(partial, side, 1).reshape(-1, width) for side in (1 - core, core)]
        arrived = partner(away, "wide", 1)
        expand_away = weight_grad(middle_away, after(expanded_low, away))
        shrink_total = (mine.astype(F32) + arrived.astype(F32)).astype(BF16)
    else:
        away = weight_grad(active_away, grad_low)
        arrived = partner(away, "wide", 1)
        expand_away = weight_grad(middle_away, after(expanded_low, away))
        shrink_total = weight_sum(active_mine, after(grad_low, expand_away), arrived)
    shrink_chain = Chain(hidden_dims, turned).sides([([shrink_total], 0, width)])
    expand_arrived = partner(expand_away, "wide", 1)
    out_away = weight_grad(context_away, after(mixed_low, shrink_chain.away))
    out_arrived = partner(out_away, "wide", 1)
    expand_total = weight_sum(middle_mine, after(expanded_low, out_away), expand_arrived)
    out_total = weight_sum(context_mine, after(mixed_low, expand_total), out_arrived)
    cut = (hidden + width) * 3 // 5
    expand_chains = [
        Chain(up, up).sides([([expand_total], 0, cut)]),
        Chain(up, down).sides([([expand_total], cut, hidden - cut), ([out_total], 0, width)]),
    ]
    grads = attend_back(layout, 1, triple, after(context_grad, far_result, *sends(expand_chains)), ())
    near_result = hand_on(near_result, after(far_result, grads[0]))
    sent = shrink_chain.step(grads[0])
    grads = attend_back(layout, 0, triple, after(context_grad, sent, grads[0]), grads)
    sent = [c.step(grads[0]) for c in expand_chains]
    sent.append(shrink_chain.step(*sent))
    triple_grad = after(grads[0], near_result, *sent)
    in_away = weight_grad(base_away, triple_grad)
    in_arrived = partner(in_away, "wide", 1)
    in_mine = lax.optimization_barrier(weight_grad(base_mine, after(triple_grad, in_away)))
    cut = 3 * width // 2
    in_chains = [
        Chain(up, order).sides([([in_mine, in_arrived], at * cut, cut)]) for at, order in enumerate((up, down))
    ]
    spread = expand_sums.reshape(width, hidden // width).T
    early = jnp.concatenate([sums[:6], spread])
    found = last(
        layout, spots, triple_grad, after(mixed_low, *sends(in_chains)), embedded, project_in, lines, early, sort
    )
    own_grad, near_grad, far_grad, tail_away, tail_mine = found
    tail_away = after(tail_away, *[c.arrived for c in in_chains])
    tail_arrived = partner(tail_away, "wide", 1)
    for chain in expand_chains + in_chains:
        chain.wait(tail_away)
    sent = [c.step() for c in in_chains]
    far_grad = partner(after(far_grad, *sent), "wide", 2)
    for chain in expand_chains:
        chain.wait(*sent)
    expand_chain = join(expand_chains)
    tail_total = (tail_mine.astype(F32) + after(tail_arrived, expand_chain.away).astype(F32)).astype(BF16)
    tail_steps = middle_back[:1] + narrow_steps[::-1] + middle_back[1:]
    tail_chain = Chain(up, tail_steps).sides([([tail_total], 0, tail_total.shape[-1])])
    sent = shrink_chain.step(tail_chain.away)
    outputs = settle(size, spots, after(own_result, sent), near_result, far_result)
    for chain in in_chains:
        chain.wait(*outputs)
    in_chain = join(in_chains)
    sent = tail_chain.step(in_chain.away)
    sent = expand_chain.step(sent)
    sent = tail_chain.step(sent)
    sent = in_chain.step(sent)
    expand_chain.wait(sent)
    expand_grad, out_grad = expand_chain.finish(hidden)
    near_grad = hand_on(near_grad, after(far_grad, expand_grad))
    sent = tail_chain.step(near_grad)
    input_grads = settle(size, spots, after(own_grad, sent), near_grad, far_grad)
    in_chain.wait(*input_grads)
    in_grad = in_chain.finish()
    shrink_chain.wait(in_grad)
    shrink_grad = shrink_chain.finish()
    tail_sum = tail_chain.finish()
    length = QUAD * spans[1]
    position_grad = tail_sum[:, :length].T
    order = (0, 1, 2, 3, 8, 9, 10, 11, 12, 13)
    vector = [tail_sum[:, length + i] for i in order]
    expand_bias_grad = tail_sum[:, length + 14 : length + 14 + hidden // width].reshape(-1)
    return (
        outputs[0].reshape(short_input.shape),
        outputs[1].reshape(long_input.shape),
        input_grads[0].reshape(short_input.shape),
        input_grads[1].reshape(long_input.shape),
        position_grad,
        vector[0],
        vector[1],
        in_grad,
        vector[2],
        vector[3],
        out_grad,
        vector[9],
        vector[7],
        vector[8],
        expand_grad,
        expand_bias_grad,
        shrink_grad,
        vector[6],
        vector[4],
        vector[5],
    )


def solution(mesh):
    rows = P(BOTH, None, None, None)
    vector, matrix = P(BOTH), P(BOTH, None)
    in_specs = (rows,) * 4 + (P(),) * 18
    out_specs = (rows,) * 4 + (
        P(None, BOTH),
        vector,
        vector,
        matrix,
        vector,
        vector,
        matrix,
        vector,
        vector,
        vector,
        matrix,
        vector,
        matrix,
        vector,
        vector,
        vector,
    )
    return jax.shard_map(on_device, mesh=mesh, in_specs=in_specs, out_specs=out_specs, check_vma=False)
```

```python
import functools

import jax
import jax.numpy as jnp
from jax import lax
from jax.experimental import pallas as pl
from jax.experimental.pallas import tpu as pltpu
from jax.sharding import PartitionSpec as P

HEAD_DIM = 64
LANES = 128
EPS = 1e-05
QUAD = 4
F32 = jnp.float32
BF16 = jnp.bfloat16
BOTH = ("wide", "narrow")
ROOT_HALF = 0.7071067811865476
PHI_ZERO = 0.3989422804014327


def partner(shard, axis, flip):
    return lax.ppermute(shard, axis, [(i, i ^ flip) for i in range(lax.axis_size(axis))])


def pick(tensor, index, axis):
    return lax.dynamic_index_in_dim(tensor, index, axis, keepdims=False)


def after(value, *first):
    return lax.optimization_barrier((value,) + first)[0]


def halving_steps():
    wide_bits, narrow_bits = [lax.axis_size(axis).bit_length() - 1 for axis in BOTH]
    middle = [("wide", b) for b in range(1, wide_bits)]
    narrow = [("narrow", b) for b in range(narrow_bits)]
    return middle, middle[::-1], narrow


def bit_of(index, bit):
    return index // 2**bit % 2


def sort_rows(width):
    middle, _, narrow = halving_steps()
    each = width // (lax.axis_size("wide") * lax.axis_size("narrow"))
    natural = jnp.arange(width)
    index = {"narrow": natural // each % lax.axis_size("narrow")}
    index["wide"] = natural // each // lax.axis_size("narrow")
    goes = (bit_of(index["wide"], 0) == lax.axis_index("wide") % 2).astype(jnp.int32)
    for axis, bit in middle + narrow:
        goes = 2 * goes + bit_of(index[axis], bit)
    goes = goes * each + natural % each
    return (goes[None, :] == natural[:, None]).astype(BF16)


class Chain:
    def __init__(self, dims, steps):
        self.dims, self.steps = list(dims), list(steps)
        self.away = self.mine = self.arrived = None

    def sides(self, groups):
        axis, bit = self.steps.pop(0)
        place = self.dims.index((axis, bit))
        here = bit_of(lax.axis_index(axis), bit)
        lead = (2,) * len(self.dims)
        self.dims.pop(place)
        found = []
        for side in (1 - here, here):
            parts = []
            for arrays, start, size in groups:
                total = 0.0
                for array in arrays:
                    array = array.reshape(lead + (-1, array.shape[-1]))
                    sizes = list(array.shape[:-1]) + [size]
                    sizes[place] = 1
                    starts = [jnp.int32(0)] * (len(sizes) - 1) + [jnp.int32(start)]
                    starts[place] = jnp.asarray(side, jnp.int32)
                    total = total + lax.dynamic_slice(array, starts, sizes).astype(F32)
                parts.append(jnp.squeeze(total.astype(BF16), place))
            found.append(parts[0] if len(parts) == 1 else jnp.concatenate(parts, axis=-1))
        self.away, self.mine = found
        self.arrived = partner(self.away, axis, 2**bit)
        return self

    def wait(self, *first):
        self.arrived = after(self.arrived, *first)

    def step(self, *first):
        if first:
            self.wait(*first)
        return self.sides([([self.mine, self.arrived], 0, self.mine.shape[-1])]).away

    def finish(self, *cuts):
        while self.steps:
            self.step()
        edges = (0,) + cuts + (self.mine.shape[-1],)
        parts = [
            self.mine[..., a:b].astype(F32) + self.arrived[..., a:b].astype(F32)
            for a, b in zip(edges[:-1], edges[1:])
        ]
        return parts if cuts else parts[0]


def sends(chains):
    return [chain.away for chain in chains]


def join(chains):
    groups = [([c.mine, c.arrived], 0, c.mine.shape[-1]) for c in chains]
    return Chain(chains[0].dims, chains[0].steps).sides(groups)


def left_product(a, b):
    return lax.dot_general(a, b, (((0,), (0,)), ((), ())), preferred_element_type=F32)


def right_product(a, b):
    return lax.dot_general(a, b, (((1,), (1,)), ((), ())), preferred_element_type=F32)


def product(a, b):
    return jnp.dot(a, b, preferred_element_type=F32)


def norm_stats(values):
    row_mean = jnp.mean(values, axis=-1, keepdims=True)
    centered = values - row_mean
    spread = jnp.mean(centered * centered, axis=-1, keepdims=True)
    scale = lax.rsqrt(spread + EPS)
    return centered * scale, scale


def norm_back(grad, unit, scale, gain):
    inner = grad * gain
    first = jnp.mean(inner, axis=-1, keepdims=True)
    second = jnp.mean(inner * unit, axis=-1, keepdims=True)
    return scale * (inner - first - unit * second)


def piece_outs(tokens, width):
    one = pl.BlockSpec((tokens, width), lambda i, s: (0, 0))
    two = pl.BlockSpec((tokens, width), lambda i, s: (jnp.maximum(i - 2, 0), 0))
    return [
        (one, pltpu.HBM((tokens, width), BF16)),
        (one, pltpu.HBM((tokens, width), BF16)),
        (two, pltpu.HBM((2 * tokens, width), BF16)),
    ]


def put_piece(outs, value):
    step = pl.program_id(0)
    for at, out in enumerate(outs):

        @pl.when((step == at) | (step == at + 1) if at == 2 else step == at)
        def _(out=out):
            out[...] = value


def column_sum(values):
    return jnp.sum(values, axis=0, keepdims=True)


def call(kernel, grid, scalars, ins, outs, arrays, scratch=(), aliases=None, flops=0, moved=0, room=16):
    return pl.pallas_call(
        kernel,
        grid_spec=pltpu.PrefetchScalarGridSpec(
            num_scalar_prefetch=len(scalars),
            grid=grid,
            in_specs=ins,
            out_specs=[o[0] for o in outs],
            scratch_shapes=list(scratch),
        ),
        out_shape=[o[1] for o in outs],
        input_output_aliases=aliases or {},
        compiler_params=pltpu.CompilerParams(vmem_limit_bytes=room << 20),
        cost_estimate=pl.CostEstimate(flops=flops, bytes_accessed=moved, transcendentals=0),
    )(*scalars, *arrays)


def whole(shape, once=True):
    mode = {"pipeline_mode": pl.Buffered(1)} if once else {}
    return pl.BlockSpec(shape, lambda *_: (0,) * len(shape), **mode)


def shaped(shape, dtype):
    return jax.ShapeDtypeStruct(shape, dtype)


def kept(array):
    return pltpu.with_memory_space_constraint(array, pltpu.HBM)


def head_rows(block, rows, span, at):
    part = block[:, at * span : (at + 1) * span, :] if rows > 1 else block
    return part.reshape(-1, part.shape[-1])


def first_head(shape):
    return lax.broadcasted_iota(jnp.int32, shape, len(shape) - 1) < HEAD_DIM


def pair_rows(ref, layout, bucket):
    rows, span = layout[0][bucket], layout[1][bucket]
    found = []
    for start in range(0, ref.shape[-1], LANES):
        block = ref[:, :, start : start + LANES]
        found += [head_rows(block, rows, span, at) for at in range(rows)]
    return found


def attend_rows(queries, keys, values):
    first = first_head(queries[0].shape)
    nothing, ones = jnp.zeros_like(queries[0]), jnp.ones_like(queries[0])
    scores = []
    for query, key in zip(queries, keys):
        query = query * jnp.asarray(HEAD_DIM**-0.5, BF16)
        scores.append(right_product(jnp.where(first, query, nothing), key))
        scores.append(right_product(jnp.where(first, nothing, query), key))
    count = queries[0].shape[0]
    scores = jnp.concatenate(scores)
    powers = jnp.exp(scores - jnp.max(scores, axis=-1, keepdims=True)).astype(BF16)
    results = []
    for at, value in enumerate(values):
        left = product(powers[2 * at * count : (2 * at + 1) * count], jnp.where(first, value, ones))
        right = product(powers[(2 * at + 1) * count : (2 * at + 2) * count], jnp.where(first, ones, value))
        left = left * (1.0 / left[:, HEAD_DIM : HEAD_DIM + 1])
        right = right * (1.0 / right[:, :1])
        results.append(jnp.where(first, left, right).astype(BF16))
    return results


def attend_part(layout, triple, out):
    rows, spans = layout
    size = rows[0] * spans[0]
    width = out.shape[-1]
    columns = 3 * LANES

    @pl.loop(0, width // columns)
    def _(step):
        for bucket in range(2):
            count, span = rows[bucket], spans[bucket]
            tokens = slice(bucket * size, (bucket + 1) * size)
            lists = []
            for which in range(3):
                place = pl.multiple_of(which * width + step * columns, LANES)
                block = triple[:, tokens, pl.ds(place, columns)]
                lists.append(pair_rows(block, layout, bucket))
            for start in range(0, len(lists[0]), count):
                results = attend_rows(*[part[start : start + count] for part in lists])
                place = pl.multiple_of(step * columns + start // count * LANES, LANES)
                for at, result in enumerate(results):
                    first = bucket * size + at * span
                    result = result.reshape(QUAD, span, LANES)
                    out[:, first : first + span, pl.ds(place, LANES)] = result


def attend_flops(layout, pairs):
    rows, spans = layout
    return sum(2 * pairs * r * (QUAD * s) ** 2 * 2 * HEAD_DIM * 2 for r, s in zip(rows, spans))


def front_kernel(layout, spot, *refs):
    rows, spans = layout
    cut = rows[0] * spans[0]
    data, (table, lines, weight, sort) = refs[:QUAD], refs[QUAD : QUAD + 4]
    embedded_out, away_out, mine_out, triple_out, context_out, pieces = refs[QUAD + 4 :]
    gain, shift, query_bias, value_bias = [lines[at : at + 1] for at in range(4)]
    width = table.shape[-1]
    for at in range(QUAD):
        pieces[at] = data[at][...]

    def project(at):
        tokens = pieces[at].astype(F32)
        parts = [tokens[:cut], tokens[cut:]]
        for which, span in enumerate(spans):
            place = pl.multiple_of((spot[0] ^ at) * span, span)
            place = table[pl.ds(place, span), :].astype(F32)
            part = parts[which].reshape(rows[which], span, width) + place[None]
            parts[which] = part.reshape(-1, width)
        embedded = jnp.concatenate(parts)
        embedded_out[at] = embedded
        unit, _ = norm_stats(embedded)
        base_low = (unit * gain + shift).astype(BF16)
        sorted_low = right_product(base_low, sort[...]).astype(BF16)
        away_out[at] = sorted_low[:, : width // 2]
        mine_out[at] = sorted_low[:, width // 2 :]
        for which, bias in enumerate((query_bias, 0.0, value_bias)):
            part = slice(which * width, (which + 1) * width)
            triple_out[at, :, part] = (product(base_low, weight[:, part]) + bias).astype(BF16)

    @pl.loop(0, QUAD, step=2)
    def _(at):
        project(at)
        project(at + 1)

    attend_part(layout, triple_out, context_out)


def front(layout, spot, data, table, lines, weight, sort):
    rows, spans = layout
    tokens, width = data[0].shape
    triple = weight.shape[1]
    ins = [whole((tokens, width))] * QUAD
    ins += [whole(a.shape) for a in (table, lines, weight, sort)]
    outs = []
    for n, dtype in ((width, F32), (width // 2, BF16), (width // 2, BF16), (triple, BF16), (width, BF16)):
        outs.append((whole((QUAD, tokens, n)), pltpu.HBM((QUAD, tokens, n), dtype)))
    outs[-1] = (outs[-1][0], shaped((QUAD, tokens, width), BF16))
    return call(
        functools.partial(front_kernel, layout),
        (1,),
        [spot],
        ins,
        outs,
        [kept(d) for d in data] + [table, lines, weight, sort],
        scratch=[pltpu.VMEM((QUAD, tokens, width), BF16)],
        flops=2 * QUAD * tokens * width * triple + attend_flops(layout, width // LANES),
        moved=2 * width * triple + QUAD * tokens * (8 * width + 2 * triple),
        room=30,
    )


def attend_back_rows(queries, keys, values, grads):
    first = first_head(queries[0].shape)
    nothing = jnp.zeros_like(queries[0])
    scaled = [query * jnp.asarray(HEAD_DIM**-0.5, BF16) for query in queries]
    scores, prob_grads = [], []
    for query, key, value, grad in zip(scaled, keys, values, grads):
        scores.append(right_product(key, jnp.where(first, query, nothing)))
        scores.append(right_product(key, jnp.where(first, nothing, query)))
        prob_grads.append(right_product(value, jnp.where(first, grad, nothing)))
        prob_grads.append(right_product(value, jnp.where(first, nothing, grad)))
    scores = jnp.concatenate(scores, axis=1)
    prob_grad = jnp.concatenate(prob_grads, axis=1)
    powers = jnp.exp(scores - jnp.max(scores, axis=0, keepdims=True))
    soft = powers * (1.0 / jnp.sum(powers, axis=0, keepdims=True))
    inner = jnp.sum(soft * prob_grad, axis=0, keepdims=True)
    score_grad = (soft * (prob_grad - inner)).astype(BF16)
    weights = soft.astype(BF16)
    count = queries[0].shape[0]
    results = []
    for at, (query, key, grad) in enumerate(zip(scaled, keys, grads)):
        two = []
        for head in range(2):
            part = slice((2 * at + head) * count, (2 * at + head + 1) * count)
            two.append(
                (
                    left_product(score_grad[:, part], key) * HEAD_DIM**-0.5,
                    product(score_grad[:, part], query),
                    product(weights[:, part], grad),
                )
            )
        results.append([jnp.where(first, a, b).astype(BF16) for a, b in zip(*two)])
    return results


def attend_back_kernel(layout, bucket, group, query, key, value, grad, *rest):
    count, span = layout[0][bucket], layout[1][bucket]
    out = rest[-1]
    width = out.shape[-1] // 3
    step = pl.program_id(0) * query.shape[-1]
    lists = [pair_rows(ref, layout, bucket) for ref in (query, key, value, grad)]
    for start in range(0, len(lists[0]), group):
        results = attend_back_rows(*[part[start : start + group] for part in lists])
        for at, three in enumerate(results):
            pair, row = divmod(start + at, count)
            for which, result in enumerate(three):
                place = pl.multiple_of(which * width + step + pair * LANES, LANES)
                rows = slice(row * span, (row + 1) * span)
                out[:, rows, pl.ds(place, LANES)] = result.reshape(QUAD, span, LANES)


def attend_back(layout, bucket, triple, grad, earlier):
    rows, spans = layout
    tokens, width = triple.shape[1], triple.shape[2] // 3
    pairs = width // LANES
    size = rows[0] * spans[0]
    steps = 2 if rows[bucket] > 1 else 3
    columns = width // steps
    group = rows[bucket] if rows[bucket] > 1 else 2
    ins = [
        pl.BlockSpec((QUAD, size, columns), lambda p, w=w: (0, bucket, w * steps + p)) for w in range(3)
    ]
    ins += [pl.BlockSpec((QUAD, size, columns), lambda p: (0, bucket, p))]
    ins += [pl.BlockSpec(memory_space=pl.ANY)] * len(earlier)
    outs = [
        (
            pl.BlockSpec((QUAD, size, 3 * width), lambda p: (0, bucket, 0)),
            shaped((QUAD, tokens, 3 * width), BF16),
        )
    ]
    return call(
        functools.partial(attend_back_kernel, layout, bucket, group),
        (steps,),
        [],
        ins,
        outs,
        [kept(triple)] * 3 + [kept(grad)] + list(earlier),
        aliases={4 + i: i for i in range(len(earlier))},
        flops=int(2.5 * attend_flops((rows[bucket : bucket + 1], spans[bucket : bucket + 1]), pairs)),
        room=18,
        moved=QUAD * size * width * 14,
    )


def alive_rows(limits, size, count):
    at = lax.broadcasted_iota(jnp.int32, (count, 1), 0)
    short = (at < limits[0]).astype(F32)
    long = (at >= size).astype(F32) * (at < limits[1]).astype(F32)
    return short + long


def hidden_parts(core, hidden, block, chunk):
    if block % LANES:
        return [([(start, chunk)], start) for start in range(0, hidden, chunk)]
    places = []
    for half in range(2):
        side = core if half else 1 - core
        places += [
            (pl.multiple_of((2 * at + side) * block, LANES), block) for at in range(hidden // block // 2)
        ]
    each = chunk // block
    return [(places[at : at + each], at * block) for at in range(0, len(places), each)]


def columns_of(ref, places, lead=()):
    return jnp.concatenate([ref[lead + (slice(None), pl.ds(*p))] for p in places], axis=-1)


def rows_of(ref, places):
    return jnp.concatenate([ref[pl.ds(*p), :] for p in places], axis=0)


def middle_rows(size, block, chunk, limits, *refs):
    (context, embedded, *cotangents) = refs[: 2 + QUAD]
    refs = refs[2 + QUAD :]
    (sort, lines, project_out, expand, expand_bias, shrink) = refs[:6]
    outputs, refs = refs[6:9], refs[9:]
    (middle_away, middle_mine, context_away, context_mine, active_away, active_mine) = refs[:6]
    (grad_low_out, expanded_out, mixed_low_out, context_out, sums, bias_sums, slopes) = refs[6:]
    embed_gain, embed_shift = lines[0:1], lines[1:2]
    output_bias, middle_gain, middle_shift, shrink_bias, gain, shift = [
        lines[at : at + 1] for at in range(4, 10)
    ]
    width = context.shape[-1]
    half = width // 2
    hidden = expand.shape[1]
    parts = hidden_parts(limits[2], hidden, block, chunk)
    unit, _ = norm_stats(embedded[0])
    inner = unit * embed_gain + embed_shift
    inner = inner + (product(context[0], project_out[...]) + output_bias)
    sorted_low = right_product(context[0], sort[...]).astype(BF16)
    context_away[0] = sorted_low[:, :half]
    context_mine[0] = sorted_low[:, half:]
    inner_unit, inner_scale = norm_stats(inner)
    middle = inner_unit * middle_gain + middle_shift
    middle_low = middle.astype(BF16)
    sorted_low = right_product(middle_low, sort[...]).astype(BF16)
    middle_away[0] = sorted_low[:, :half]
    middle_mine[0] = sorted_low[:, half:]
    total = middle + shrink_bias
    for places, start in parts:
        part = slice(start, start + chunk)
        expanded = product(middle_low, columns_of(expand, places)) + columns_of(expand_bias, places)
        below = 0.5 + 0.5 * lax.erf(expanded * ROOT_HALF)
        active = (expanded * below).astype(BF16)
        if start < hidden // 2:
            active_away[0, :, part] = active
        else:
            active_mine[0, :, start - hidden // 2 : start - hidden // 2 + chunk] = active
        density = jnp.exp(expanded * expanded * -0.5) * PHI_ZERO
        slopes[:, part] = (below + expanded * density).astype(BF16)
        total = total + product(active, rows_of(shrink, places))
    unit, scale = norm_stats(total)
    alive = alive_rows(limits, size, unit.shape[0])
    result = unit * gain + shift
    put_piece(outputs, (result * alive).astype(BF16))
    cotangent = cotangents[0][...]
    for k in range(1, QUAD):
        cotangent = jnp.where(pl.program_id(0) == k, cotangents[k][...], cotangent)
    upstream = cotangent.astype(F32) * alive
    grad = norm_back(upstream, unit, scale, gain)
    grad_low = grad.astype(BF16)
    grad_low_out[0] = grad_low
    found = [column_sum(upstream * unit), column_sum(upstream), column_sum(grad_low.astype(F32))]
    total = grad
    for places, start in parts:
        part = slice(start, start + chunk)
        raised = right_product(grad_low, rows_of(shrink, places)) * slopes[:, part].astype(F32)
        low = raised.astype(BF16)
        sums_low = column_sum(low.astype(F32))
        done = 0
        for place in places:
            expanded_out[0, :, pl.ds(*place)] = low[:, done : done + place[1]]
            bias_sums[:, pl.ds(*place)] += sums_low[:, done : done + place[1]]
            done += place[1]
        total = total + right_product(low, columns_of(expand, places))
    mixed = norm_back(total, inner_unit, inner_scale, middle_gain)
    mixed_low = mixed.astype(BF16)
    mixed_low_out[0] = mixed_low
    context_out[0] = right_product(mixed_low, project_out[...]).astype(BF16)
    found += [column_sum(total * inner_unit), column_sum(total), column_sum(mixed_low.astype(F32))]
    for at, value in enumerate(found):
        sums[at : at + 1, :] += value


def middle_kernel(size, block, chunk, limits, *refs):
    sums, bias_sums = refs[-3:-1]

    @pl.when(pl.program_id(0) == 0)
    def _():
        sums[...] = jnp.zeros_like(sums)
        bias_sums[...] = jnp.zeros_like(bias_sums)

    middle_rows(size, block, chunk, limits, *refs)


def middle_part(size, block, limits, context, embedded, cotangents, weights):
    pieces, tokens, width = context.shape
    hidden = weights[3].shape[1]

    def out(columns, dtype=BF16, keep=pltpu.HBM):
        blocked = pl.BlockSpec((1, tokens, columns), lambda i, s: (i, 0, 0))
        return blocked, keep((pieces, tokens, columns), dtype)

    ins = [out(width)[0]] * 2 + [whole(c.shape) for c in cotangents] + [whole(w.shape) for w in weights]
    outs = piece_outs(tokens, width)
    outs += [out(width // 2)] * 4 + [out(hidden // 2, keep=shaped)] * 2
    outs += [out(width, keep=shaped), out(hidden, keep=shaped)]
    outs += [out(width), out(width)]
    outs += [(whole((8, width), False), shaped((8, width), F32))]
    outs += [(whole((1, hidden), False), shaped((1, hidden), F32))]
    return call(
        functools.partial(middle_kernel, size, block, width),
        (pieces,),
        [limits],
        ins,
        outs,
        [context, kept(embedded)] + [kept(c) for c in cotangents] + [kept(w) for w in weights],
        scratch=[pltpu.VMEM((tokens, hidden), BF16)],
        flops=4 * pieces * tokens * width * (width + 2 * hidden),
        moved=4 * width * hidden + pieces * tokens * (30 * width + 4 * hidden),
        room=38,
    )


def last_kernel(layout, spot, *refs):
    rows, spans = layout
    cut = rows[0] * spans[0]
    length = QUAD * spans[1]
    triple, mixed, embedded, weight, lines, early, sort = refs[:7]
    pieces_out = refs[7:10]
    tail_away, tail_mine, pile, short_pile = refs[10:]
    width = mixed.shape[-1]
    step = pl.program_id(0)

    @pl.when(step == 0)
    def _():
        pile[length:, :] = jnp.zeros((pile.shape[0] - length, width), F32)
        pile[length + 8 : length + 8 + early.shape[0], :] = early[...]

    total = mixed[0].astype(F32) + right_product(triple[0], weight[...])
    unit, scale = norm_stats(embedded[0])
    grad = norm_back(total, unit, scale, lines[0:1])
    put_piece(pieces_out, grad.astype(BF16))
    place = spot[0] ^ step
    short_rows = pl.ds(pl.multiple_of(place * spans[0], spans[0]), spans[0])
    long_rows = pl.ds(pl.multiple_of(place * spans[1], spans[1]), spans[1])
    short_pile[short_rows, :] = jnp.sum(grad[:cut].reshape(rows[0], spans[0], width), axis=0)
    pile[long_rows, :] = jnp.sum(grad[cut:].reshape(rows[1], spans[1], width), axis=0)
    found = [
        column_sum(total * unit),
        column_sum(total),
        column_sum(triple[0, :, :width].astype(F32)),
        column_sum(triple[0, :, 2 * width :].astype(F32)),
    ]
    for at, item in enumerate(found):
        pile[length + at : length + at + 1, :] += item

    @pl.when(step == QUAD - 1)
    def _():
        shorter = short_pile.shape[0]
        pile[:shorter, :] += short_pile[...]
        tail = right_product(sort[...], pile[...].astype(BF16)).astype(BF16)
        tail_away[...] = tail[: width // 2]
        tail_mine[...] = tail[width // 2 :]


def last(layout, spot, grad, mixed, embedded, weight, lines, early, sort):
    rows, spans = layout
    pieces, tokens, width = mixed.shape
    row = pl.BlockSpec((1, tokens, width), lambda i, s: (i, 0, 0))
    triple = pl.BlockSpec((1, tokens, 3 * width), lambda i, s: (i, 0, 0))
    ins = [triple, row, row] + [whole(a.shape) for a in (weight, lines, early, sort)]
    outs = piece_outs(tokens, width)
    depth = QUAD * spans[1] + LANES
    half = (width // 2, depth)
    outs += [(whole(half, False), shaped(half, BF16))] * 2
    return call(
        functools.partial(last_kernel, layout),
        (pieces,),
        [spot],
        ins,
        outs,
        [grad, kept(mixed), kept(embedded), weight, lines, early, sort],
        scratch=[pltpu.VMEM((depth, width), F32), pltpu.VMEM((QUAD * spans[0], width), F32)],
        flops=6 * pieces * tokens * width * width,
        moved=6 * width * width + pieces * tokens * 18 * width,
        room=22,
    )


def settle_kernel(size, spot, own, near, far, short_out, long_out):
    tokens = own.shape[0]
    for k, (part, start) in enumerate(((own, 0), (near, 0), (far, 0), (near, tokens))):
        short_out[spot[0] ^ k] = part[start : start + size]
        long_out[spot[0] ^ k] = part[start + size : start + tokens]


def settle(size, spot, own, near, far):
    tokens, width = own.shape
    sizes = (size, tokens - size)
    outs = [(whole((QUAD, n, width)), shaped((QUAD, n, width), own.dtype)) for n in sizes]
    return call(
        functools.partial(settle_kernel, size),
        (1,),
        [spot],
        [whole(p.shape) for p in (own, near, far)],
        outs,
        [kept(p) for p in (own, near, far)],
        moved=4 * QUAD * tokens * width,
        room=8,
    )


def hand_on(near, far):
    return partner(jnp.concatenate([near, far[near.shape[0] :]]), "wide", 1)


def cut_pieces(short, long, spot):
    parts = [a.reshape(QUAD, -1, a.shape[-1]) for a in (short, long)]
    return {k: jnp.concatenate([pick(a, spot ^ k, 0) for a in parts]) for k in range(QUAD)}


def swap_pieces(pieces):
    return {k: partner(piece, "wide", k) if k else piece for k, piece in pieces.items()}


def on_device(
    short_input,
    long_input,
    short_cotangent,
    long_cotangent,
    short_live,
    long_live,
    position_table,
    embed_gain,
    embed_shift,
    project_in,
    query_bias,
    value_bias,
    project_out,
    output_bias,
    middle_gain,
    middle_shift,
    expand_weight,
    expand_bias,
    shrink_weight,
    shrink_bias,
    final_gain,
    final_shift,
):
    width = short_input.shape[-1]
    spot = lax.axis_index("wide") % QUAD
    group = lax.axis_index("wide") // QUAD * lax.axis_size("narrow") + lax.axis_index("narrow")
    rows = (short_input.shape[1] // QUAD, long_input.shape[1] // QUAD)
    spans = (short_input.shape[2], long_input.shape[2])
    layout = (rows, spans)
    size = rows[0] * spans[0]
    assert size == rows[1] * spans[1]
    spots = jnp.asarray(spot, jnp.int32).reshape(1)
    alive = [
        jnp.clip(pick(live, group, 0) - spot * r, 0, r) * s
        for live, r, s in zip((short_live, long_live), rows, spans)
    ]
    core = lax.axis_index("wide") % 2
    limits = jnp.stack([alive[0], size + alive[1], core]).astype(jnp.int32)
    sort = sort_rows(width)
    middle_steps, middle_back, narrow_steps = halving_steps()
    up, down = middle_steps + narrow_steps, middle_back + narrow_steps
    flat = lambda a: a.reshape(-1, a.shape[-1])

    def weight_grad(a, b):
        return left_product(flat(a), flat(b)).astype(BF16)

    cuts = cut_pieces(short_input, long_input, spot)
    pieces = swap_pieces(cuts)
    vectors = (embed_gain, embed_shift, query_bias, value_bias, output_bias)
    vectors += (middle_gain, middle_shift, shrink_bias, final_gain, final_shift)
    vectors = jnp.concatenate((after(vectors[0], *cuts.values()),) + vectors[1:])
    lines = vectors.astype(F32).reshape(-1, width)
    cot_cuts = cut_pieces(after(short_cotangent, *cuts.values()), after(long_cotangent, *cuts.values()), spot)
    embedded, base_away, base_mine, triple, context = front(
        layout,
        spots,
        [pieces[k] for k in range(QUAD)],
        position_table,
        after(lines, *cot_cuts.values()),
        project_in,
        sort,
    )
    cot_cuts = {k: after(c, pieces[2], pieces[3]) for k, c in cot_cuts.items()}
    cot_pieces = swap_pieces(cot_cuts)
    cotangents = [cot_pieces[k] for k in range(QUAD)]
    weights = (sort, lines, project_out, expand_weight, expand_bias.astype(F32)[None], shrink_weight)
    hidden = expand_weight.shape[1]
    hidden_block = hidden // lax.axis_size("wide")
    found = middle_part(size, hidden_block, limits, context, embedded, cotangents, weights)
    own_result, near_result, far_result = found[:3]
    far_result = partner(far_result, "wide", 2)
    middle_away, middle_mine, context_away, context_mine, active_away, active_mine = found[3:9]
    grad_low, expanded_low, mixed_low, context_grad, sums, expand_sums = found[9:]
    turned = middle_back[:1] + narrow_steps + middle_back[1:]
    hidden_dims = middle_back + narrow_steps[::-1]

    def weight_sum(a, b, arrived):
        return (left_product(flat(a), flat(b)) + arrived.astype(F32)).astype(BF16)

    if hidden_block % LANES:
        partial = jnp.concatenate([weight_grad(active_away, grad_low), weight_grad(active_mine, grad_low)])
        partial = partial.reshape(-1, 2, hidden_block, width)
        away, mine = [pick(partial, side, 1).reshape(-1, width) for side in (1 - core, core)]
        arrived = partner(away, "wide", 1)
        expand_away = weight_grad(middle_away, after(expanded_low, away))
        shrink_total = (mine.astype(F32) + arrived.astype(F32)).astype(BF16)
    else:
        away = weight_grad(active_away, grad_low)
        arrived = partner(away, "wide", 1)
        expand_away = weight_grad(middle_away, after(expanded_low, away))
        shrink_total = weight_sum(active_mine, after(grad_low, expand_away), arrived)
    shrink_chain = Chain(hidden_dims, turned).sides([([shrink_total], 0, width)])
    expand_arrived = partner(expand_away, "wide", 1)
    out_away = weight_grad(context_away, after(mixed_low, shrink_chain.away))
    out_arrived = partner(out_away, "wide", 1)
    expand_total = weight_sum(middle_mine, after(expanded_low, out_away), expand_arrived)
    out_total = weight_sum(context_mine, after(mixed_low, expand_total), out_arrived)
    cut = (hidden + width) * 3 // 5
    expand_chains = [
        Chain(up, up).sides([([expand_total], 0, cut)]),
        Chain(up, down).sides([([expand_total], cut, hidden - cut), ([out_total], 0, width)]),
    ]
    grads = attend_back(layout, 1, triple, after(context_grad, far_result, *sends(expand_chains)), ())
    near_result = hand_on(near_result, after(far_result, grads[0]))
    sent = shrink_chain.step(grads[0])
    grads = attend_back(layout, 0, triple, after(context_grad, sent, grads[0]), grads)
    sent = [c.step(grads[0]) for c in expand_chains]
    sent.append(shrink_chain.step(*sent))
    triple_grad = after(grads[0], near_result, *sent)
    in_away = weight_grad(base_away, triple_grad)
    in_arrived = partner(in_away, "wide", 1)
    in_mine = lax.optimization_barrier(weight_grad(base_mine, after(triple_grad, in_away)))
    cut = 3 * width // 2
    in_chains = [
        Chain(up, order).sides([([in_mine, in_arrived], at * cut, cut)]) for at, order in enumerate((up, down))
    ]
    spread = expand_sums.reshape(width, hidden // width).T
    early = jnp.concatenate([sums[:6], spread])
    found = last(
        layout, spots, triple_grad, after(mixed_low, *sends(in_chains)), embedded, project_in, lines, early, sort
    )
    own_grad, near_grad, far_grad, tail_away, tail_mine = found
    tail_away = after(tail_away, *[c.arrived for c in in_chains])
    tail_arrived = partner(tail_away, "wide", 1)
    for chain in expand_chains + in_chains:
        chain.wait(tail_away)
    sent = [c.step() for c in in_chains]
    far_grad = partner(after(far_grad, *sent), "wide", 2)
    for chain in expand_chains:
        chain.wait(*sent)
    expand_chain = join(expand_chains)
    tail_total = (tail_mine.astype(F32) + after(tail_arrived, expand_chain.away).astype(F32)).astype(BF16)
    tail_steps = middle_back[:1] + narrow_steps[::-1] + middle_back[1:]
    tail_chain = Chain(up, tail_steps).sides([([tail_total], 0, tail_total.shape[-1])])
    sent = shrink_chain.step(tail_chain.away)
    outputs = settle(size, spots, after(own_result, sent), near_result, far_result)
    for chain in in_chains:
        chain.wait(*outputs)
    in_chain = join(in_chains)
    sent = tail_chain.step(in_chain.away)
    sent = expand_chain.step(sent)
    sent = tail_chain.step(sent)
    sent = in_chain.step(sent)
    expand_chain.wait(sent)
    expand_grad, out_grad = expand_chain.finish(hidden)
    near_grad = hand_on(near_grad, after(far_grad, expand_grad))
    sent = tail_chain.step(near_grad)
    input_grads = settle(size, spots, after(own_grad, sent), near_grad, far_grad)
    in_chain.wait(*input_grads)
    in_grad = in_chain.finish()
    shrink_chain.wait(in_grad)
    shrink_grad = shrink_chain.finish()
    tail_sum = tail_chain.finish()
    length = QUAD * spans[1]
    position_grad = tail_sum[:, :length].T
    order = (0, 1, 2, 3, 8, 9, 10, 11, 12, 13)
    vector = [tail_sum[:, length + i] for i in order]
    expand_bias_grad = tail_sum[:, length + 14 : length + 14 + hidden // width].reshape(-1)
    return (
        outputs[0].reshape(short_input.shape),
        outputs[1].reshape(long_input.shape),
        input_grads[0].reshape(short_input.shape),
        input_grads[1].reshape(long_input.shape),
        position_grad,
        vector[0],
        vector[1],
        in_grad,
        vector[2],
        vector[3],
        out_grad,
        vector[9],
        vector[7],
        vector[8],
        expand_grad,
        expand_bias_grad,
        shrink_grad,
        vector[6],
        vector[4],
        vector[5],
    )


def solution(mesh):
    rows = P(BOTH, None, None, None)
    vector, matrix = P(BOTH), P(BOTH, None)
    in_specs = (rows,) * 4 + (P(),) * 18
    out_specs = (rows,) * 4 + (
        P(None, BOTH),
        vector,
        vector,
        matrix,
        vector,
        vector,
        matrix,
        vector,
        vector,
        vector,
        matrix,
        vector,
        matrix,
        vector,
        vector,
        vector,
    )
    return jax.shard_map(on_device, mesh=mesh, in_specs=in_specs, out_specs=out_specs, check_vma=False)
```
